32 devices in a mesh: seq: 4 (over y, x), ctx: 8 (over z, core).
Axes of the slice: x: 2, y: 2, z: 4, core: 2. Of those that a mesh axis runs over, the one named last changes fastest.
Arguments:
- hidden_in: bfloat16 [16, 1024, 768], P('seq', 'ctx'), may hold values from -6 to 6
- cotangent: bfloat16 [16, 1024, 768], P('seq', 'ctx'), may hold values from -6 to 6
- segments: int32 [16, 1024], P('seq', 'ctx'), may hold values from 0 to 3, never falling along the last dimension, each value on 1 to 512 neighbouring positions
- qkv_weight: bfloat16 [768, 2304], P('seq'), may hold values from -0.21875 to 0.21875
- query_bias: bfloat16 [768], P('seq'), may hold values from -3 to 3
- value_bias: bfloat16 [768], P('seq'), may hold values from -0.29882812 to 0.29882812
- out_weight: bfloat16 [768, 768], P('seq'), may hold values from -1.75 to 1.75
- out_bias: bfloat16 [768], P('seq'), may hold values from -2 to 2
- first_gain: bfloat16 [768], P('seq'), may hold values from 0.5 to 1.5
- first_shift: bfloat16 [768], P('seq'), may hold values from -2 to 2
- inner_weight: bfloat16 [768, 3072], P('seq'), may hold values from -0.21875 to 0.21875
- inner_bias: bfloat16 [3072], P('seq'), may hold values from -3 to 3
- outer_weight: bfloat16 [3072, 768], P('seq'), may hold values from -0.21875 to 0.21875
- outer_bias: bfloat16 [768], P('seq'), may hold values from -2 to 2
- second_gain: bfloat16 [768], P('seq'), may hold values from 0.5 to 1.5
- second_shift: bfloat16 [768], P('seq'), may hold values from -2 to 2
Outputs:
- output: bfloat16 [16, 1024, 768], P('seq', 'ctx')
- grad_input: float32 [16, 1024, 768], P('seq', 'ctx')
- grad_qkv_weight: float32 [768, 2304], P('seq')
- grad_query_bias: float32 [768], P('seq')
- grad_value_bias: float32 [768], P('seq')
- grad_out_weight: float32 [768, 768], P('seq')
- grad_out_bias: float32 [768], P('seq')
- grad_first_gain: float32 [768], P('seq')
- grad_first_shift: float32 [768], P('seq')
- grad_inner_weight: float32 [768, 3072], P('seq')
- grad_inner_bias: float32 [3072], P('seq')
- grad_outer_weight: float32 [3072, 768], P('seq')
- grad_outer_bias: float32 [768], P('seq')
- grad_second_gain: float32 [768], P('seq')
- grad_second_shift: float32 [768], P('seq')
The draws below stay inside these ranges and needn't reach their ends.
Inputs may be any that keep to these rules, and one draw needn't show every extreme that they name: `segments`: in each sequence the document numbers never fall along the positions; a document holds 1 to 512 positions, and some document holds exactly 512; attention joins only positions of one document of one sequence.
All inputs are finite; a program needn't handle non-finite values.
Results may differ from the reference program's by a relative error of at most 0.035.
Values may be sent and summed in bfloat16 or wider, within the bound.
A program may use at most 320 MiB of HBM per device.

```python
import math
import jax
import jax.numpy as jnp
import numpy as np
from jax import lax

D = 768
HEADS = 12
HEAD_DIM = 64
FF = 3072
LEN = 1024
SEQS = 16
DOCS = 4


def block_levels(rng, shape, pieces, least, top_value):
    def one(axis_at, parts):
        steps = jax.random.uniform(jax.random.fold_in(jax.random.fold_in(rng, 6), axis_at), (parts,), jnp.float32, least / len(pieces), top_value / len(pieces))
        return jnp.repeat(jnp.exp(steps), shape[axis_at] // parts).reshape((-1,) + (1,) * (len(shape) - axis_at - 1))

    factor_of = one(*pieces[0])
    for cut in pieces[1:]:
        factor_of = factor_of * one(*cut)
    return factor_of


def length_profile(count, total, limit, lean):
    weights = [(1 << 20) // math.isqrt(rank ** lean) + 1 for rank in range(2, count + 1)]
    spare, counts = total - limit - (count - 1), [1] * (count - 1)
    while spare > 0:
        movable = [i for i in range(count - 1) if counts[i] < limit]
        mass, left = sum([weights[i] for i in movable]), spare
        for i in movable:
            addition = min(limit - counts[i], max(1, left * weights[i] // mass), spare)
            counts[i] = counts[i] + addition
            spare = spare - addition
    return np.array([limit] + counts)


def ragged_sizes(stream_key, count, total, limit, slope):
    if count == 2:
        one = jax.random.randint(stream_key, (), max(1, total - limit), min(limit, total - 1) + 1)
        return jnp.stack([one, total - one])
    tallies = jnp.asarray(length_profile(count, total, limit, slope), jnp.int32)
    pairs = (count - 1) // 2
    giver, sink = tallies[1:1 + 2 * pairs:2], tallies[2:2 + 2 * pairs:2]
    slack = jnp.minimum(giver - 1, limit - sink)
    moved = jax.random.randint(jax.random.fold_in(stream_key, 1), (pairs,), 0, 1 << 20) % (slack + 1)
    tallies = tallies.at[1:1 + 2 * pairs:2].set(giver - moved).at[2:2 + 2 * pairs:2].set(sink + moved)
    return tallies[jax.random.permutation(jax.random.fold_in(stream_key, 2), count)]


def noise(rng, extent, spread, most, cuts=(), dtype=jnp.bfloat16):
    factor_of = block_levels(rng, extent, cuts, -0.22, 0.18) if cuts else 1.0
    values = jax.random.normal(rng, extent, jnp.float32) * spread * factor_of
    return jnp.minimum(jnp.maximum(values, -most), most).astype(dtype)


def setup_inputs(seed: int = 0) -> dict:
    seeds = jax.random.split(jax.random.key(seed), 17)
    return {
        "hidden_in": noise(seeds[0], (SEQS, LEN, D), 1.0, 6.0, ((0, 4), (1, 8))),
        "cotangent": noise(seeds[1], (SEQS, LEN, D), 1.0, 6.0, ((0, 4), (1, 8))),
        "segments": jax.vmap(lambda own: jnp.searchsorted(jnp.cumsum(ragged_sizes(own, DOCS, LEN, LEN // 2, 2)), jnp.arange(LEN), side="right"))(jax.random.split(seeds[2], SEQS)).reshape((SEQS, LEN)).astype(jnp.int32),
        "qkv_weight": noise(seeds[3], (D, 3 * D), D ** -0.5, 0.21875, ((0, 4),)),
        "query_bias": noise(seeds[4], (D,), 0.5, 3.0, ((0, 4),)),
        "value_bias": noise(seeds[5], (D,), 0.05, 0.29882812, ((0, 4),)),
        "out_weight": noise(seeds[6], (D, D), (max(1, D // 64)) ** -0.5, 1.75, ((0, 4),)),
        "out_bias": noise(seeds[7], (D,), 0.3, 2.0, ((0, 4),)),
        "first_gain": jnp.clip(1.0 + 0.1 * jax.random.normal(seeds[8], (D,), jnp.float32), 0.5, 1.5).astype(jnp.bfloat16),
        "first_shift": noise(seeds[9], (D,), 0.3, 2.0, ((0, 4),)),
        "inner_weight": noise(seeds[10], (D, FF), D ** -0.5, 0.21875, ((0, 4),)),
        "inner_bias": noise(seeds[11], (FF,), 0.5, 3.0, ((0, 4),)),
        "outer_weight": noise(seeds[12], (FF, D), (FF // 4) ** -0.5, 0.21875, ((0, 4),)),
        "outer_bias": noise(seeds[13], (D,), 0.3, 2.0, ((0, 4),)),
        "second_gain": jnp.clip(1.0 + 0.1 * jax.random.normal(seeds[14], (D,), jnp.float32), 0.5, 1.5).astype(jnp.bfloat16),
        "second_shift": noise(seeds[15], (D,), 0.3, 2.0, ((0, 4),)),
    }


@jax.custom_vjp
def low(v):
    return lax.optimization_barrier(v.astype(jnp.bfloat16)).astype(jnp.float32)

@jax.custom_vjp
def low_back(v):
    return v

def low_keep(v):
    return (low(v), None)

def low_pass(kept, grad):
    return (grad,)

def back_keep(v):
    return (v, None)

def back_low(kept, grad):
    return (low(grad),)
low.defvjp(low_keep, low_pass)
low_back.defvjp(back_keep, back_low)
highest = lax.Precision.HIGHEST
norm_epsilon = 1e-12

def layer_norm(matrix, gain, shift):
    average = lax.optimization_barrier(jnp.mean(matrix, axis=-1, keepdims=True))
    centred = matrix - average
    variance = lax.optimization_barrier(jnp.mean(centred * centred, axis=-1, keepdims=True))
    return centred * lax.rsqrt(variance + norm_epsilon) * gain + shift

def attend_sequence(queries, key_rows, value_rows, segment):
    positions = queries.shape[0]
    query_heads = queries.reshape(positions, HEADS, HEAD_DIM).transpose(1, 0, 2)
    key_heads = key_rows.reshape(positions, HEADS, HEAD_DIM).transpose(1, 0, 2)
    value_heads = value_rows.reshape(positions, HEADS, HEAD_DIM).transpose(1, 0, 2)
    scores = jnp.einsum('hqd,hkd->hqk', query_heads, key_heads, precision=highest) * HEAD_DIM ** (-0.5)
    scores = low_back(scores)
    allowed = segment[:, None] == segment[None, :]
    scores = jnp.where(allowed[None], scores, -1e+30)
    weights = low(jax.nn.softmax(scores, axis=-1))
    mixed_heads = jnp.einsum('hqk,hkd->hqd', weights, value_heads, precision=highest)
    return mixed_heads.transpose(1, 0, 2).reshape(positions, HEADS * HEAD_DIM)

def forward(hidden, qkv_weight, query_bias, value_bias, out_weight, out_bias, first_gain, first_shift, inner_weight, inner_bias, outer_weight, outer_bias, second_gain, second_shift, segments):
    token_rows = hidden.reshape(SEQS * LEN, D)
    projected = jnp.dot(token_rows, qkv_weight, precision=highest)
    queries = low(low_back(projected[:, :D] + query_bias))
    key_rows = low(low_back(projected[:, D:2 * D]))
    value_rows = low(low_back(projected[:, 2 * D:] + value_bias))
    checked = jax.checkpoint(attend_sequence)

    def one_sequence(carried, entries):
        return (carried, checked(*entries))
    _, context = lax.scan(one_sequence, jnp.zeros((), jnp.float32), (queries.reshape(SEQS, LEN, D), key_rows.reshape(SEQS, LEN, D), value_rows.reshape(SEQS, LEN, D), segments))
    context = low(low_back(context.reshape(SEQS * LEN, D)))
    attended = low_back(jnp.dot(context, out_weight, precision=highest) + out_bias)
    first = layer_norm(token_rows + attended, first_gain, first_shift)
    inner = low_back(jnp.dot(low(first), inner_weight, precision=highest) + inner_bias)
    active = low(jax.nn.gelu(inner, approximate=False))
    branch = low_back(jnp.dot(active, outer_weight, precision=highest) + outer_bias)
    return layer_norm(first + branch, second_gain, second_shift)

def reference(hidden_in, cotangent, segments, qkv_weight, query_bias, value_bias, out_weight, out_bias, first_gain, first_shift, inner_weight, inner_bias, outer_weight, outer_bias, second_gain, second_shift):
    floats = [a.astype(jnp.float32) for a in (hidden_in, qkv_weight, query_bias, value_bias, out_weight, out_bias, first_gain, first_shift, inner_weight, inner_bias, outer_weight, outer_bias, second_gain, second_shift)]

    def run_layer(*arrays):
        return forward(*arrays, segments)
    result, pullback = jax.vjp(run_layer, *floats)
    gradients = pullback(cotangent.astype(jnp.float32).reshape(SEQS * LEN, D))
    return (result.reshape(SEQS, LEN, D).astype(jnp.bfloat16), gradients[0].reshape(SEQS, LEN, D), gradients[1], gradients[2], gradients[3], gradients[4], gradients[5], gradients[6], gradients[7], gradients[8], gradients[9], gradients[10], gradients[11], gradients[12], gradients[13])
```

```python
import functools

import jax
import jax.numpy as jnp
from jax import lax
from jax.experimental import pallas as pl
from jax.experimental.pallas import tpu as pltpu
from jax.sharding import PartitionSpec as P

HEAD_DIM = 64
EPS = 1e-12
NEG = -1e30
RB = 64
ROOT_HALF = 0.7071067811865476
PDF_SCALE = 0.3989422804014327
f32 = jnp.float32
bf16 = jnp.bfloat16
MESH = pl.DeviceIdType.MESH
ANY = pl.BlockSpec(memory_space=pl.ANY)
VMEM = pl.BlockSpec(memory_space=pltpu.VMEM)

QB, VB, OB, FG, FS, UB, SG, SS, IB = 0, 1, 2, 3, 4, 5, 6, 7, 8


def tile(i, width):
    return pl.ds(pl.multiple_of(i * width, width), width)


def span(start, width, unit=128):
    return pl.ds(pl.multiple_of(start, unit), width)


def dotf(a, b):
    return jnp.dot(a, b, preferred_element_type=f32)


def dotg(a, b, ca, cb):
    return lax.dot_general(a, b, (((ca,), (cb,)), ((), ())), preferred_element_type=f32)


def remote(src, dst, send_sem, recv_sem, **where):
    return pltpu.make_async_remote_copy(
        src_ref=src,
        dst_ref=dst,
        send_sem=send_sem,
        recv_sem=recv_sem,
        device_id=where,
        device_id_type=MESH,
    )


def enter(S, C):
    s, c = lax.axis_index("seq"), lax.axis_index("ctx")
    barrier = pltpu.get_barrier_semaphore()
    for d in range(1, S):
        pl.semaphore_signal(
            barrier, inc=1, device_id={"seq": lax.rem(s + d, S)}, device_id_type=MESH
        )

    def greet(d, carry):
        pl.semaphore_signal(
            barrier, inc=1, device_id={"ctx": lax.rem(c + d, C)}, device_id_type=MESH
        )
        return carry

    lax.fori_loop(1, C, greet, 0)
    pl.semaphore_wait(barrier, S - 1 + C - 1)


def bit_orders(S):
    bits = [1 << k for k in range(S.bit_length() - 1)]
    return (bits, bits[1:] + bits[:1])


def subsets(bits):
    out = [0]
    for b in bits:
        out = out + [o | b for o in out]
    return out


class Gather:
    def __init__(self, S, shard, full, send, recv, local):
        self.S, self.shard, self.full = S, shard, full
        self.send, self.recv, self.local = send, recv, local
        self.R, self.N = shard.shape
        self.s, self.c = lax.axis_index("seq"), lax.axis_index("ctx")
        self.core = lax.rem(self.c, 2)
        self.cols = span(self.core * (self.N // 2), self.N // 2)
        self.orders = bit_orders(S)
        self.half = self.R // 2

    def block(self, owner, p):
        return self.full.at[span(owner * self.R + p * self.half, self.half, 16), self.cols]

    def own(self, p):
        return self.shard.at[pl.ds(p * self.half, self.half), self.cols]

    def copy_own(self):
        return pltpu.make_async_copy(
            self.shard.at[:, self.cols],
            self.full.at[span(self.s * self.R, self.R, 16), self.cols],
            self.local,
        )

    def copies(self, t):
        out = []
        for p in range(2):
            order = self.orders[p]
            peer = jnp.bitwise_xor(self.s, order[t])
            for i, mask in enumerate(subsets(order[:t])):
                owner = jnp.bitwise_xor(self.s, mask)
                src = self.own(p) if mask == 0 else self.block(owner, p)
                k = (1 << t) - 1 + i
                out.append(
                    remote(src, self.block(owner, p), self.send.at[p, k], self.recv.at[p, k], seq=peer)
                )
        return out

    def swap(self):
        k = self.S - 1
        half = self.full.at[:, self.cols]
        other = jnp.bitwise_xor(self.c, 1)
        return remote(half, half, self.send.at[0, k], self.recv.at[0, k], ctx=other)

    def start(self, t):
        if t == 0:
            self.copy_own().start()
        for copy in self.copies(t):
            copy.start()

    def finish(self, t):
        for copy in self.copies(t):
            copy.wait_recv()

    def start_swap(self):
        self.copy_own().wait()
        self.swap().start()

    def finish_swap(self):
        self.swap().wait_recv()

    def drain(self):
        for t in range(len(self.orders[0])):
            for copy in self.copies(t):
                copy.wait_send()
        self.swap().wait_send()


class Regroup:
    def __init__(self, src, dst, send, recv, local, C, G):
        self.src, self.dst, self.send, self.recv, self.local = src, dst, send, recv, local
        self.G, self.M = G, C // G
        self.c = lax.axis_index("ctx")

    def dst_at(self, j):
        if len(self.dst.shape) == 2:
            rows = self.src.shape[1]
            return self.dst.at[tile(j, rows), :]
        return self.dst.at[j]

    def each(self, on_remote, on_local):
        place = lax.rem(self.c, self.G)
        for g in range(self.G):
            target = g * self.M + lax.div(self.c, self.G)
            far = remote(
                self.src.at[g], self.dst_at(place), self.send.at[g], self.recv.at[place], ctx=target
            )
            near = pltpu.make_async_copy(self.src.at[g], self.dst_at(place), self.local)

            @pl.when(target != self.c)
            def _():
                on_remote(far)

            @pl.when(target == self.c)
            def _():
                on_local(near)

    def start(self):
        self.each(lambda far: far.start(), lambda near: near.start())

    def drain(self):
        self.each(lambda far: far.wait_send(), lambda near: None)

    def finish(self):
        m = lax.rem(self.c, self.M)
        for j in range(self.G):
            source = m * self.G + j

            @pl.when(source != self.c)
            def _():
                remote(
                    self.src.at[0], self.dst_at(j), self.send.at[0], self.recv.at[j], ctx=source
                ).wait_recv()

            @pl.when(source == self.c)
            def _():
                pltpu.make_async_copy(self.src.at[0], self.dst_at(j), self.local).wait()


class Ungroup:
    def __init__(self, src, dst, send, recv, local, C, G):
        self.src, self.dst, self.send, self.recv, self.local = src, dst, send, recv, local
        self.G, self.M, self.P = G, C // G, dst.shape[1]
        self.c = lax.axis_index("ctx")

    def each(self, on_remote, on_local):
        g, m = lax.div(self.c, self.M), lax.rem(self.c, self.M)
        for j in range(self.G):
            target = m * self.G + j
            rows = self.src.at[pl.ds(j * self.P, self.P), :]
            far = remote(rows, self.dst.at[g], self.send.at[j], self.recv.at[g], ctx=target)
            near = pltpu.make_async_copy(rows, self.dst.at[g], self.local)

            @pl.when(target != self.c)
            def _():
                on_remote(far)

            @pl.when(target == self.c)
            def _():
                on_local(near)

    def start(self):
        self.each(lambda far: far.start(), lambda near: near.start())

    def drain(self):
        self.each(lambda far: far.wait_send(), lambda near: None)

    def finish(self):
        rows = self.src.at[pl.ds(0, self.P), :]
        for g in range(self.G):
            source = g * self.M + lax.div(self.c, self.G)

            @pl.when(source != self.c)
            def _():
                remote(
                    rows, self.dst.at[g], self.send.at[0], self.recv.at[g], ctx=source
                ).wait_recv()

            @pl.when(source == self.c)
            def _():
                pltpu.make_async_copy(rows, self.dst.at[g], self.local).wait()


def mask_bias(seg_keys, seg_queries, bias, G, PP):
    rows = [seg_queries[i].astype(f32) for i in range(G)]
    for a in range(G):
        column = jnp.broadcast_to(seg_keys[a].astype(f32), (PP, PP)).T
        for b in range(G):
            bias[a * PP : (a + 1) * PP, b * PP : (b + 1) * PP] = jnp.where(
                column == rows[b], jnp.zeros((PP, PP), f32), jnp.full((PP, PP), NEG, f32)
            ).astype(bias.dtype)


def norm_rows(x):
    centred = x - jnp.mean(x, axis=-1, keepdims=True)
    factor = lax.rsqrt(jnp.mean(centred * centred, axis=-1, keepdims=True) + EPS)
    return centred * factor, factor


def norm_back(g, gain, normed, factor):
    h = g * gain
    return factor * (
        h
        - jnp.mean(h, axis=-1, keepdims=True)
        - normed * jnp.mean(h * normed, axis=-1, keepdims=True)
    )


def loop(n, body):
    def step(i, carry):
        body(i)
        return carry

    lax.fori_loop(0, n, step, 0)


def colsum(x):
    return jnp.sum(x, axis=0, keepdims=True)


def forward_kernel(
    dims,
    hid, cot, seg, wq_s, wo_s, wi_s, wu_s, small,
    xs_o, wq_o, wo_o, wi_o, wu_o, k_o, v_o, q_o, qt_o, seg_o, lse_o, ctxt_o, ctx_o,
    n1_o, f1_o, flow_o, act_o, dgel_o, gsec_o, gb_o, out_o, smg_o, sm_o,
    xs, ct, wq, wo, wi, wu, small_all, segc, segk, q, qt, kown, vown, kc, vc, bias, m_s, l_s, ctxt, ctx,
    first, n1, f1, flow, h, act, dgel, n2, gsec, gb, outv,
    ag_send, ag_recv, ag_local, rg_send, rg_recv, rg_local, sm_send, sm_recv,
    kv_send, kv_recv, kv_local, kc_sem, out_sem,
):
    S, C, G, PP = dims
    M, L, D = C // G, G * PP, hid.shape[2]
    FF = wi.shape[1]
    NP = D // 128
    T = 256
    s, c = lax.axis_index("seq"), lax.axis_index("ctx")
    m = lax.rem(c, M)

    gathers = [
        Gather(S, shard, full, ag_send.at[w], ag_recv.at[w], ag_local.at[w])
        for w, (shard, full) in enumerate(((wq_s, wq), (wo_s, wo), (wi_s, wi), (wu_s, wu)))
    ]
    full_out = [wq_o, wo_o, wi_o, wu_o]
    steps = S.bit_length() - 1
    events = [(w, t) for w in range(4) for t in range(steps)]
    pending = []

    def put(src, dst):
        copy = pltpu.make_async_copy(src, dst, out_sem.at[len(pending)])
        copy.start()
        pending.append(copy)

    def tick(w, t):
        gathers[w].finish(t)
        k = events.index((w, t))
        if t + 1 < steps:
            gathers[w].start(t + 1)
        else:
            gathers[w].start_swap()
        for ahead in (k + 1, k + 2):
            if ahead < len(events) and events[ahead][1] == 0 and (ahead == k + 2 or steps == 1):
                gathers[events[ahead][0]].start(0)

    def ready(w):
        gathers[w].finish_swap()
        put(gathers[w].full, full_out[w])

    enter(S, C)
    hid_move = Regroup(hid, xs, rg_send.at[0], rg_recv.at[0], rg_local.at[0], C, G)
    cot_move = Regroup(cot, ct, rg_send.at[1], rg_recv.at[1], rg_local.at[1], C, G)
    seg_move = Regroup(seg, segc, rg_send.at[2], rg_recv.at[2], rg_local.at[2], C, G)
    seg_move.start()
    hid_move.start()
    gathers[0].start(0)
    small_copies = [
        remote(small, small_all.at[d - 1], sm_send.at[d - 1], sm_recv.at[d - 1], seq=jnp.bitwise_xor(s, d))
        for d in range(1, S)
    ]
    for copy in small_copies:
        copy.start()
    for t in range(steps):
        tick(0, t)
    seg_move.finish()

    group = lax.div(c, M) * M
    seg_own = pltpu.make_async_copy(segc, seg_o.at[m], kv_local.at[2])
    seg_own.start()

    def peer(d):
        return group + lax.rem(m + d, M)

    def kv_copies(d):
        return [
            remote(src, dst.at[m], kv_send.at[i, d], kv_recv.at[i, m], ctx=peer(d))
            for i, (src, dst) in enumerate(((kown, k_o), (vown, v_o), (segc, seg_o)))
        ]

    def kv_arrivals(d):
        j = lax.rem(m + d, M)
        return [
            remote(src, dst.at[j], kv_send.at[i, d], kv_recv.at[i, j], ctx=peer(d))
            for i, (src, dst) in enumerate(((kown, k_o), (vown, v_o), (segc, seg_o)))
        ]

    for d in range(1, M):
        kv_copies(d)[2].start()

    total = small[...].astype(f32)
    for copy in small_copies:
        copy.wait_recv()
    for d in range(1, S):
        total = total + small_all[d - 1].astype(f32)
    sm_o[...] = total
    hid_move.finish()
    cot_move.start()
    put(xs, xs_o)
    mask_bias(segc, segc, bias, G, PP)
    ready(0)

    def project(i):
        cols = tile(i, T)
        qv = dotf(xs[...], wq[:, cols]) + sm_o[QB : QB + 1, cols]
        kv = dotf(xs[...], wq[:, span(D + i * T, T)])
        vv = dotf(xs[...], wq[:, span(2 * D + i * T, T)]) + sm_o[VB : VB + 1, cols]
        qs = (qv.astype(bf16).astype(f32) * HEAD_DIM**-0.5).astype(bf16)
        kv, vv = kv.astype(bf16), vv.astype(bf16)
        for u in range(T // 128):
            lanes = slice(u * 128, (u + 1) * 128)
            hp = i * (T // 128) + u
            q[hp] = qs[:, lanes]
            qt[hp] = qs[:, lanes].T
            kown[hp] = kv[:, lanes]
            vown[hp] = vv[:, lanes]

    loop(D // T, project)
    for d in range(1, M):
        for copy in kv_copies(d)[:2]:
            copy.start()
    own_kv = [
        pltpu.make_async_copy(kown, k_o.at[m], kv_local.at[0]),
        pltpu.make_async_copy(vown, v_o.at[m], kv_local.at[1]),
    ]
    for copy in own_kv:
        copy.start()
    put(q, q_o)
    put(qt, qt_o)
    for t in range(steps):
        tick(1, t)

    row_of = lax.broadcasted_iota(jnp.int32, (128, L), 0)

    def attend(keys, values, fresh, extra):
        def pair(hp):
            extra(hp)
            qv, kv, vt, b = qt[hp], keys[hp], values[hp].T, bias[...]
            for e in range(2):
                head = slice(e * HEAD_DIM, (e + 1) * HEAD_DIM)
                mine = (row_of < HEAD_DIM) if e == 0 else (row_of >= HEAD_DIM)
                scores = dotf(kv, jnp.where(mine, qv, jnp.zeros_like(qv))) + b
                top = jnp.max(scores, axis=0, keepdims=True)
                if fresh:
                    weights = jnp.exp(scores - top)
                    m_s[hp, e : e + 1, :] = top
                    l_s[hp, e : e + 1, :] = colsum(weights)
                    ctxt[hp, head, :] = dotf(vt[head], weights.astype(bf16))
                else:
                    old = m_s[hp, e : e + 1, :]
                    top = jnp.maximum(old, top)
                    keep = jnp.exp(old - top)
                    weights = jnp.exp(scores - top)
                    m_s[hp, e : e + 1, :] = top
                    l_s[hp, e : e + 1, :] = l_s[hp, e : e + 1, :] * keep + colsum(weights)
                    ctxt[hp, head, :] = ctxt[hp, head, :] * keep + dotf(vt[head], weights.astype(bf16))

        loop(NP, pair)

    def in_own(hp):
        @pl.when(hp == NP - 2)
        def _():
            tick(2, 0)

    attend(kown, vown, True, in_own)

    def far_chunk(d, carry):
        j = lax.rem(m + d, M)
        for copy in kv_arrivals(d):
            copy.wait_recv()
        loads = [
            pltpu.make_async_copy(k_o.at[j], kc, kc_sem.at[0]),
            pltpu.make_async_copy(v_o.at[j], vc, kc_sem.at[1]),
            pltpu.make_async_copy(seg_o.at[j], segk, kc_sem.at[2]),
        ]
        for copy in loads:
            copy.start()
        for copy in loads:
            copy.wait()
        mask_bias(segk, segc, bias, G, PP)
        attend(kc, vc, False, lambda hp: None)
        return carry

    lax.fori_loop(1, M, far_chunk, 0)

    def close(hp):
        for e in range(2):
            head = slice(e * HEAD_DIM, (e + 1) * HEAD_DIM)
            ctxt[hp, head, :] = ctxt[hp, head, :] / l_s[hp, e : e + 1, :]
            l_s[hp, e : e + 1, :] = m_s[hp, e : e + 1, :] + jnp.log(l_s[hp, e : e + 1, :])
        ctx[:, tile(hp, 128)] = ctxt[hp].T.astype(bf16)

    loop(NP, close)

    put(ctxt, ctxt_o)
    put(ctx, ctx_o)
    put(l_s, lse_o)
    ready(1)

    def project_out(i):
        cols = tile(i, T)
        first[:, cols] = dotf(ctx[...], wo[:, cols]) + sm_o[OB : OB + 1, cols]

    loop(D // T, project_out)

    def first_norm(r):
        rows = tile(r, RB)
        normed, factor = norm_rows(first[rows, :] + xs[rows, :].astype(f32))
        y = normed * sm_o[FG : FG + 1, :] + sm_o[FS : FS + 1, :]
        n1[rows, :] = normed
        f1[rows, :] = factor
        first[rows, :] = y
        flow[rows, :] = y.astype(bf16)

    loop(L // RB, first_norm)
    put(n1, n1_o)
    put(f1, f1_o)
    put(flow, flow_o)
    for t in range(1, steps):
        tick(2, t)
    tick(3, 0)
    ready(2)

    def feed_in(i):
        cols = tile(i, D)
        h[...] = dotf(flow[...], wi[:, cols]) + sm_o[pl.ds(IB + i, 1), :]

        def gelu(k):
            rows, lanes = tile(lax.div(k, D // T), RB), lax.rem(k, D // T) * T
            x = h[rows, span(lanes, T)]
            share = 0.5 * (1.0 + lax.erf(x * ROOT_HALF))
            act[rows, span(i * D + lanes, T)] = (x * share).astype(bf16)
            dgel[rows, span(i * D + lanes, T)] = (
                share + x * (PDF_SCALE * jnp.exp(-0.5 * x * x))
            ).astype(bf16)

        loop(L // RB * (D // T), gelu)

    loop(FF // D, feed_in)
    put(act, act_o)
    put(dgel, dgel_o)
    for t in range(1, steps):
        tick(3, t)
    ready(3)

    def feed_out(i):
        cols = tile(i, T)
        n2[:, cols] = dotf(act[...], wu[:, cols]) + sm_o[UB : UB + 1, cols]

    loop(D // T, feed_out)
    cot_move.finish()
    smg_o[...] = jnp.zeros(smg_o.shape, f32)

    def second_norm(r):
        rows = tile(r, RB)
        normed, factor = norm_rows(first[rows, :] + n2[rows, :])
        gain = sm_o[SG : SG + 1, :]
        outv[rows, :] = (normed * gain + sm_o[SS : SS + 1, :]).astype(bf16)
        g = ct[rows, :].astype(f32)
        smg_o[SG : SG + 1, :] += colsum(g * normed)
        smg_o[SS : SS + 1, :] += colsum(g)
        back = norm_back(g, gain, normed, factor)
        gsec[rows, :] = back
        low = back.astype(bf16)
        gb[rows, :] = low
        smg_o[UB : UB + 1, :] += colsum(low.astype(f32))

    loop(L // RB, second_norm)
    put(outv, out_o)
    put(gsec, gsec_o)
    put(gb, gb_o)

    for gather in gathers:
        gather.drain()
    for move in (hid_move, cot_move, seg_move):
        move.drain()
    for copy in small_copies:
        copy.wait_send()
    for d in range(1, M):
        for copy in kv_copies(d):
            copy.wait_send()
    for copy in own_kv + [seg_own] + pending:
        copy.wait()


def forward_call(S, C, hid, cot, seg, wq_s, wo_s, wi_s, wu_s, small):
    G, PP, D = hid.shape
    L, M, NP, FF = G * PP, C // G, D // 128, wi_s.shape[1]
    sds = jax.ShapeDtypeStruct
    outs = [
        ((L, D), bf16), ((D, 3 * D), bf16), ((D, D), bf16), ((D, FF), bf16), ((FF, D), bf16),
        ((M, NP, L, 128), bf16), ((M, NP, L, 128), bf16), ((NP, L, 128), bf16), ((NP, 128, L), bf16),
        ((M, G, 1, PP), jnp.int32), ((NP, 2, L), f32), ((NP, 128, L), f32), ((L, D), bf16),
        ((L, D), f32), ((L, 1), f32), ((L, D), bf16), ((L, FF), bf16), ((L, FF), bf16),
        ((L, D), f32), ((L, D), bf16), ((L, D), bf16),
    ]
    scratch = [
        ((L, D), bf16), ((L, D), bf16), ((D, 3 * D), bf16), ((D, D), bf16), ((D, FF), bf16), ((FF, D), bf16),
        ((S - 1, 16, D), bf16), ((G, 1, PP), jnp.int32), ((G, 1, PP), jnp.int32),
        ((NP, L, 128), bf16), ((NP, 128, L), bf16), ((NP, L, 128), bf16), ((NP, L, 128), bf16),
        ((NP, L, 128), bf16), ((NP, L, 128), bf16), ((L, L), f32), ((NP, 2, L), f32), ((NP, 2, L), f32),
        ((NP, 128, L), f32), ((L, D), bf16),
        ((L, D), f32), ((L, D), f32), ((L, 1), f32), ((L, D), bf16), ((L, D), f32), ((L, FF), bf16),
        ((L, FF), bf16), ((L, D), f32), ((L, D), f32), ((L, D), bf16), ((L, D), bf16),
    ]
    dma = pltpu.SemaphoreType.DMA
    sems = [
        dma((4, 2, S)), dma((4, 2, S)), dma((4,)), dma((3, G)), dma((3, G)), dma((3,)),
        dma((S - 1,)), dma((S - 1,)), dma((3, M)), dma((3, M)), dma((3,)), dma((3,)), dma((24,)),
    ]
    return pl.pallas_call(
        functools.partial(forward_kernel, (S, C, G, PP)),
        out_shape=[sds(*o) for o in outs] + [sds((16, D), f32), sds((16, D), f32)],
        in_specs=[ANY] * 7 + [VMEM],
        out_specs=[ANY] * len(outs) + [VMEM, VMEM],
        scratch_shapes=[pltpu.VMEM(*x) for x in scratch] + sems,
        compiler_params=pltpu.CompilerParams(
            collective_id=0, has_side_effects=True, vmem_limit_bytes=62 << 20
        ),
        name="forward",
    )(hid, cot, seg, wq_s, wo_s, wi_s, wu_s, small)


def pack_small(S, vectors, inner_bias, D):
    s = lax.axis_index("seq")
    width = D // S
    owner = lax.broadcasted_iota(jnp.int32, (1, D), 1) // width
    rows = [jnp.where(owner == s, jnp.tile(v, S)[None, :], 0) for v in vectors]
    share = inner_bias.shape[0]
    flat = jnp.tile(inner_bias, S)
    where = lax.broadcasted_iota(jnp.int32, (1, share * S), 1) // share
    full = jnp.where(where == s, flat[None, :], 0).reshape(share * S // D, D)
    used = len(vectors) + share * S // D
    return jnp.concatenate(rows + [full, jnp.zeros((16 - used, D), bf16)], axis=0).astype(bf16)


def add_rows(dst, src):
    rows = dst.shape[0]
    unit = next(u for u in (96, 48, 16) if rows % u == 0)

    def step(r):
        at = tile(r, unit)
        dst[at, :] = (dst[at, :].astype(f32) + src[at, :].astype(f32)).astype(bf16)

    loop(rows // unit, step)


class Reduce:
    def __init__(self, S, C, part, far, rx, zl, zr, sems, places):
        self.S, self.K, self.part, self.far, self.rx, self.zl, self.zr = S, C // 2, part, far, rx, zl, zr
        self.c_send, self.c_recv, self.x_send, self.x_recv, self.z_send, self.z_recv, self.l_send = sems
        self.places = places
        self.R = part.shape[1] // S
        self.half = self.R // 2
        self.s, self.c = lax.axis_index("seq"), lax.axis_index("ctx")
        self.core = lax.rem(self.c, 2)
        self.k = lax.div(self.c, 2)
        self.root = self.K // 2
        self.orders = bit_orders(S)
        self.steps = len(self.orders[0])
        self.levels = max(self.root, self.K - 1 - self.root)
        self.mine = part.at[self.core]

    def block(self, owner, p):
        return self.part.at[self.core, span(owner * self.R + p * self.half, self.half, 16), :]

    def result(self, core):
        return self.part.at[core, span(self.s * self.R, self.R, 16), :]

    def core_copy(self):
        other = 1 - self.core
        return remote(
            self.part.at[other], self.far, self.c_send.at[0], self.c_recv.at[0], ctx=jnp.bitwise_xor(self.c, 1)
        )

    def core_start(self):
        self.core_copy().start()

    def copies(self, t):
        out, base = [], self.S - (1 << (self.steps - t))
        for p in range(2):
            order = self.orders[p]
            peer = jnp.bitwise_xor(self.s, order[t])
            for i, mask in enumerate(subsets(order[t + 1 :])):
                copy = remote(
                    self.block(jnp.bitwise_xor(peer, mask), p),
                    self.rx.at[p, base + i],
                    self.x_send.at[p, base + i],
                    self.x_recv.at[p, base + i],
                    seq=peer,
                )
                out.append((copy, p, base + i, mask))
        return out

    def cross_start(self, t):
        if t == 0:
            self.core_copy().wait_recv()
            add_rows(self.mine, self.far)
        else:
            self.cross_add(t - 1)
        for copy, _, _, _ in self.copies(t):
            copy.start()

    def cross_add(self, t):
        for copy, p, slot, mask in self.copies(t):
            copy.wait_recv()
            add_rows(self.block(jnp.bitwise_xor(self.s, mask), p), self.rx.at[p, slot])

    def up(self, side):
        src = self.result(self.core)
        if side == 0:
            return remote(src, self.zl, self.z_send.at[0], self.z_recv.at[0], ctx=self.c + 2)
        return remote(src, self.zr, self.z_send.at[0], self.z_recv.at[1], ctx=self.c - 2)

    def take(self, side):
        self.up(side).wait_recv()
        add_rows(self.result(self.core), self.zl if side == 0 else self.zr)

    def down(self, side, src):
        target = self.c - 2 if side == 0 else self.c + 2
        dst = self.zr if side == 0 else self.zl
        return remote(src, dst, self.z_send.at[1 + side], self.z_recv.at[2], ctx=target)

    def chain_up(self, level):
        if level == 0:
            self.cross_add(self.steps - 1)
        if level < self.root:

            @pl.when(self.k == level)
            def _():
                if level > 0:
                    self.take(0)
                self.up(0).start()

        if level < self.K - 1 - self.root:

            @pl.when(self.k == self.K - 1 - level)
            def _():
                if level > 0:
                    self.take(1)
                self.up(1).start()

    def chain_root(self):
        @pl.when(self.k == self.root)
        def _():
            if self.root > 0:
                self.take(0)
            if self.root < self.K - 1:
                self.take(1)
            src = self.result(self.core)
            if self.root > 0:
                self.down(0, src).start()
            if self.root < self.K - 1:
                self.down(1, src).start()
            self.deliver(src)

    def chain_down(self, distance):
        if self.root - distance >= 0:

            @pl.when(self.k == self.root - distance)
            def _():
                self.down(0, self.zr).wait_recv()
                if self.root - distance > 0:
                    self.down(0, self.zr).start()
                self.deliver(self.zr)

        if self.root + distance < self.K:

            @pl.when(self.k == self.root + distance)
            def _():
                self.down(1, self.zl).wait_recv()
                if self.root + distance < self.K - 1:
                    self.down(1, self.zl).start()
                self.deliver(self.zl)

    def deliveries(self, src):
        out = []
        for i, (cols, place) in enumerate(self.places):
            dst = place(self.core)
            out.append(
                (
                    pltpu.make_async_copy(src.at[:, cols], dst, self.l_send.at[i]),
                    remote(
                        src.at[:, cols], dst, self.c_send.at[1 + i], self.c_recv.at[1 + i], ctx=jnp.bitwise_xor(self.c, 1)
                    ),
                )
            )
        return out

    def deliver(self, src):
        for near, far in self.deliveries(src):
            near.start()
            far.start()

    def finish(self):
        for near, far in self.deliveries(self.zl):
            near.wait()
            far.wait_recv()

    def stages(self):
        out = [functools.partial(self.cross_start, t) for t in range(self.steps)]
        out += [functools.partial(self.chain_up, v) for v in range(self.levels)]
        out += [self.chain_root]
        out += [functools.partial(self.chain_down, d) for d in range(1, self.levels + 1)]
        return out + [self.finish]

    def drain(self):
        self.core_copy().wait_send()
        for t in range(self.steps):
            for copy, _, _, _ in self.copies(t):
                copy.wait_send()
        last = self.K - 1

        @pl.when(self.k != self.root)
        def _():
            self.up(0).wait_send()

        @pl.when(jnp.logical_and(self.k <= self.root, self.k > 0))
        def _():
            self.down(0, self.zr).wait_send()

        @pl.when(jnp.logical_and(self.k >= self.root, self.k < last))
        def _():
            self.down(1, self.zl).wait_send()

        for _, far in self.deliveries(self.zl):
            far.wait_send()


def backward_kernel(
    dims,
    outv, gsec_i, gb_i, act_i, dgel_i, wu_i, wi_i, wo_i, wq_i, flow_i, n1_i, f1_i, xs_i, ctx_i, ctxt_i,
    q_i, qt_i, k_i, v_i, seg_i, lse_i, smg_i, sm,
    out_o, gin_o, gq_o, go_o, gi_o, gu_o, land_o, small_o,
    pu, pi, po, pq, ps, fu, fi, fo, fq, fs, ru, ri, ro, rq, rs, zlu, zli, zlo, zlq, zls, zru, zri, zro, zrq, zrs,
    gsec, gb, grad_o, grad_ot, delta, smg,
    c_send, c_recv, x_send, x_recv, z_send, z_recv, rg_send, rg_recv, rg_local, in_sem, kv_sem, dkv_send, dkv_recv,
    land_sem, l_send,
):
    S, C, G, PP = dims
    M, L, D = C // G, G * PP, gsec.shape[1]
    FF = act_i.shape[1]
    NP = D // 128
    T = 256
    s, c = lax.axis_index("seq"), lax.axis_index("ctx")
    m, core = lax.rem(c, M), lax.rem(c, 2)
    group = lax.div(c, M) * M

    def piece(n, places, *refs):
        sems = [a.at[n] for a in (c_send, c_recv, x_send, x_recv, z_send, z_recv, l_send)]
        return Reduce(S, C, *refs, sems, places)

    H = D // 2
    sum_u = piece(0, [(pl.ds(0, H), lambda e: gu_o.at[:, span(e * H, H)])], pu, fu, ru, zlu, zru)
    sum_i = [
        piece(
            1 + i, [(pl.ds(0, D), lambda e, i=i: gi_o.at[:, span(e * (FF // 2) + i * D, D)])],
            pi.at[i], fi.at[i], ri.at[i], zli.at[i], zri.at[i],
        )
        for i in range(2)
    ]
    sum_o = piece(3, [(pl.ds(0, H), lambda e: go_o.at[:, span(e * H, H)])], po, fo, ro, zlo, zro)
    sum_q = [
        piece(
            4 + i,
            [
                (pl.ds(a * 128, 128), lambda e, i=i, a=a: gq_o.at[:, span(a * D + (2 * i + e) * 128, 128)])
                for a in range(3)
            ],
            pq.at[i], fq.at[i], rq.at[i], zlq.at[i], zrq.at[i],
        )
        for i in range(3)
    ]
    sum_s = piece(7, [(pl.ds(0, ps.shape[2]), lambda e: small_o.at[e])], ps, fs, rs, zls, zrs)

    def stages_of(item):
        return item.stages()

    steps = S.bit_length() - 1
    ticks = {
        "u": stages_of(sum_u), "i0": stages_of(sum_i[0]), "i1": stages_of(sum_i[1]), "o": stages_of(sum_o),
        "q0": stages_of(sum_q[0]), "q1": stages_of(sum_q[1]), "q2": stages_of(sum_q[2]), "s": stages_of(sum_s),
    }
    at = {name: 0 for name in ticks}

    def tick(name, until):
        while at[name] < min(until, len(ticks[name])):
            ticks[name][at[name]]()
            at[name] += 1

    enter(S, C)
    out_move = Ungroup(outv, out_o, rg_send.at[0], rg_recv.at[0], rg_local.at[0], C, G)
    out_move.start()
    smg[...] = smg_i[...]

    def feed_forward(act, dgel, wu, wi, h, n1, f1, flow):
        loads = [
            pltpu.make_async_copy(src, dst, in_sem.at[i])
            for i, (src, dst) in enumerate(
                ((gb_i, gb), (act_i, act), (wu_i, wu), (dgel_i, dgel), (flow_i, flow), (wi_i, wi), (gsec_i, gsec),
                 (n1_i, n1), (f1_i, f1))
            )
        ]
        for copy in loads:
            copy.start()
        loads[0].wait()
        loads[1].wait()

        def outer_grad(i):
            rows = tile(i, 512)
            block = dotg(act[:, rows], gb[...], 0, 0).astype(bf16)
            for e in range(2):
                pu[e, rows, :] = block[:, e * (D // 2) : (e + 1) * (D // 2)]

        loop(FF // 512, outer_grad)
        sum_u.core_start()
        for copy in loads[2:5]:
            copy.wait()

        def inner_grad(i, half):
            where = half * (FF // 2) + i * D
            cols = span(where, D)
            h[...] = dotg(gb[...], wu[span(where, D), :], 1, 1)

            def through(k, sums):
                rows = tile(k, RB)
                low = (h[rows, :] * dgel[rows, cols].astype(f32)).astype(bf16)
                act[rows, cols] = low
                return sums + colsum(low.astype(f32))

            sums = lax.fori_loop(0, L // RB, through, jnp.zeros((1, D), f32))
            smg[pl.ds(IB + half * (FF // 2 // D) + i, 1), :] = sums

            def grad(k):
                rows = tile(k, T)
                pi[i, half, rows, :] = dotg(flow[:, rows], act[:, cols], 0, 0).astype(bf16)

            loop(D // T, grad)

        inner_grad(0, 1 - core)
        inner_grad(0, core)
        sum_i[0].core_start()
        tick("u", 1)
        inner_grad(1, 1 - core)
        inner_grad(1, core)
        sum_i[1].core_start()
        tick("i0", 1)
        loads[5].wait()
        loads[6].wait()

        def first_grad(i):
            cols = tile(i, T)
            gsec[:, cols] += dotg(act[...], wi[cols, :], 1, 1)

        loop(D // T, first_grad)
        tick("i1", 1)
        loads[7].wait()
        loads[8].wait()

        def first_back(k):
            rows = tile(k, RB)
            g, normed = gsec[rows, :], n1[rows, :]
            smg[FG : FG + 1, :] += colsum(g * normed)
            smg[FS : FS + 1, :] += colsum(g)
            back = norm_back(g, sm[FG : FG + 1, :], normed, f1[rows, :])
            gsec[rows, :] = back
            low = back.astype(bf16)
            gb[rows, :] = low
            smg[OB : OB + 1, :] += colsum(low.astype(f32))

        loop(L // RB, first_back)

    V = pltpu.VMEM
    pl.run_scoped(
        feed_forward, V((L, FF), bf16), V((L, FF), bf16), V((FF, D), bf16), V((D, FF), bf16), V((L, D), f32),
        V((L, D), f32), V((L, 1), f32), V((L, D), bf16),
    )
    tick("u", steps)

    def context_back(wo, ctx, ctxt):
        loads = [
            pltpu.make_async_copy(src, dst, in_sem.at[i])
            for i, (src, dst) in enumerate(((ctx_i, ctx), (wo_i, wo), (ctxt_i, ctxt)))
        ]
        for copy in loads:
            copy.start()
        loads[0].wait()

        def out_grad(k):
            rows = tile(k, T)
            block = dotg(ctx[:, rows], gb[...], 0, 0).astype(bf16)
            for e in range(2):
                po[e, rows, :] = block[:, e * (D // 2) : (e + 1) * (D // 2)]

        loop(D // T, out_grad)
        sum_o.core_start()
        loads[1].wait()
        loads[2].wait()

        def back(k):
            grad = dotg(gb[...], wo[tile(k, T), :], 1, 1).astype(bf16)
            for u in range(T // 128):
                hp = k * (T // 128) + u
                mine = grad[:, u * 128 : (u + 1) * 128]
                turned = mine.T
                grad_o[hp] = mine
                grad_ot[hp] = turned
                both = turned.astype(f32) * ctxt[hp]
                for e in range(2):
                    delta[hp, e : e + 1, :] = colsum(both[e * HEAD_DIM : (e + 1) * HEAD_DIM])

        loop(D // T, back)

    pl.run_scoped(context_back, V((D, D), bf16), V((L, D), bf16), V((NP, 128, L), f32))

    def attention(wq, xs, q, qt, kb, vb, bias, lse, own_k, own_v, stage, land, segs, grads, dqt, turned_q):
        loads = [
            pltpu.make_async_copy(src, dst, in_sem.at[i])
            for i, (src, dst) in enumerate(
                ((seg_i, segs), (q_i, q), (qt_i, qt), (lse_i, lse), (xs_i, xs), (wq_i, wq))
            )
        ]

        def kv_load(hp):
            slot = lax.rem(hp, 2)
            return [
                pltpu.make_async_copy(src.at[:, hp], dst.at[slot], kv_sem.at[i, slot])
                for i, (src, dst) in enumerate(((k_i, kb), (v_i, vb)))
            ]

        for copy in kv_load(0) + loads:
            copy.start()
        for copy in loads[:4]:
            copy.wait()
        for j in range(M):
            mask_bias(segs.at[j], segs.at[m], bias.at[j], G, PP)
        row_of = lax.broadcasted_iota(jnp.int32, (128, L), 0)
        lane_of = lax.broadcasted_iota(jnp.int32, (L, 128), 1)

        def send_back(hp, d):
            slot = lax.rem(hp, 2)
            return remote(
                stage.at[slot, d - 1], land_o.at[hp, d - 1], dkv_send.at[slot, d - 1], dkv_recv.at[hp, d - 1],
                ctx=group + lax.rem(m + d, M),
            )

        def chunk(hp, slot, j):
            key, value, b = kb[slot, j], vb[slot, j], bias[j].astype(f32)
            turned = key.T
            query, query_t, up, up_t = q[hp], qt[hp], grad_o[hp], grad_ot[hp]
            sums = []
            for e in range(2):
                rows = (row_of < HEAD_DIM) if e == 0 else (row_of >= HEAD_DIM)
                lanes = (lane_of < HEAD_DIM) if e == 0 else (lane_of >= HEAD_DIM)
                zero, zero_t = jnp.zeros_like(query), jnp.zeros_like(query_t)
                scores = dotf(key, jnp.where(rows, query_t, zero_t)) + b
                probs = jnp.exp(scores - lse[hp, e : e + 1, :])
                dprobs = dotf(value, jnp.where(rows, up_t, zero_t))
                dscores = (probs * (dprobs - delta[hp, e : e + 1, :])).astype(bf16)
                sums.append(
                    (
                        dotf(dscores, jnp.where(lanes, query, zero)),
                        dotf(probs.astype(bf16), jnp.where(lanes, up, zero)),
                    )
                )
                head = slice(e * HEAD_DIM, (e + 1) * HEAD_DIM)
                dqt[head, :] += dotf(turned[head], dscores)
            return sums[0][0] + sums[1][0], sums[0][1] + sums[1][1]

        def pair(hp):
            slot = lax.rem(hp, 2)
            for copy in kv_load(hp):
                copy.wait()

            @pl.when(hp + 1 < NP)
            def _():
                for copy in kv_load(hp + 1):
                    copy.start()

            dqt[...] = jnp.zeros(dqt.shape, f32)

            def far(d, carry):
                @pl.when(hp >= 2)
                def _():
                    send_back(hp - 2, d).wait_send()

                dk, dv = chunk(hp, slot, lax.rem(m + d, M))
                stage[slot, d - 1, 0] = dk.astype(bf16)
                stage[slot, d - 1, 1] = dv.astype(bf16)
                send_back(hp, d).start()
                return carry

            lax.fori_loop(1, M, far, 0)
            dk, dv = chunk(hp, slot, m)
            own_k[slot] = dk
            own_v[slot] = dv
            turned_q[slot] = (dqt[...] * HEAD_DIM**-0.5).T.astype(bf16)

        def fetch(i):
            for u in range(2):
                for d in range(1, M):
                    send_back(2 * i + u, d).wait_recv()
            if M > 1:
                pltpu.make_async_copy(land_o.at[pl.ds(2 * i, 2)], land, land_sem.at[0]).start()

        def project_back(i):
            if M > 1:
                pltpu.make_async_copy(land_o.at[pl.ds(2 * i, 2)], land, land_sem.at[0]).wait()
            for u in range(2):
                dk, dv = own_k[u], own_v[u]
                for d in range(1, M):
                    dk = dk + land[u, d - 1, 0].astype(f32)
                    dv = dv + land[u, d - 1, 1].astype(f32)
                grads[:, u * 128 : (u + 1) * 128] = turned_q[u]
                grads[:, T + u * 128 : T + (u + 1) * 128] = dk.astype(bf16)
                grads[:, 2 * T + u * 128 : 2 * T + (u + 1) * 128] = dv.astype(bf16)
            cols = tile(i, T)
            smg[QB : QB + 1, cols] = colsum(grads[:, 0:T].astype(f32))
            smg[VB : VB + 1, cols] = colsum(grads[:, 2 * T : 3 * T].astype(f32))

            def weight(k):
                rows = tile(k, T)
                block = dotg(xs[:, rows], grads[...], 0, 0).astype(bf16)
                for a in range(3):
                    for e in range(2):
                        pq[i, e, rows, a * 128 : (a + 1) * 128] = block[:, a * T + e * 128 : a * T + (e + 1) * 128]

            loop(D // T, weight)

        def input_back(i):
            def back(k):
                rows = tile(k, T)
                total = gsec[:, rows]
                for a in range(3):
                    total = total + dotg(grads[:, a * T : (a + 1) * T], wq[rows, span(a * D + i * T, T)], 1, 1)
                gsec[:, rows] = total

            loop(D // T, back)

        def drain_stage():
            for hp in (NP - 2, NP - 1):
                for d in range(1, M):
                    send_back(hp, d).wait_send()

        def pair_group(i):
            loop(2, lambda u: pair(2 * i + u))

        pair_group(0)
        tick("o", 1)
        tick("i0", steps)
        fetch(0)
        tick("i1", steps)
        tick("u", steps + 1)
        loads[4].wait()
        loads[5].wait()
        project_back(0)
        sum_q[0].core_start()
        input_back(0)
        tick("o", steps)
        tick("i0", steps + 1)
        tick("q0", 1)
        pair_group(1)
        tick("u", steps + 2)
        tick("i1", steps + 1)
        tick("o", steps + 1)
        fetch(1)
        tick("i0", steps + 2)
        tick("q0", steps)
        project_back(1)
        sum_q[1].core_start()
        input_back(1)
        tick("i1", steps + 2)
        tick("o", steps + 2)
        tick("u", steps + 3)
        tick("q1", 1)
        pair_group(2)
        for name in ("i0", "i1", "o"):
            tick(name, steps + 3)
        tick("q0", steps + 1)
        tick("u", steps + 4)
        fetch(2)
        tick("q1", steps)
        tick("q0", steps + 2)
        project_back(2)
        sum_q[2].core_start()

        W = ps.shape[2]
        width = D // S
        ps[...] = jnp.zeros(ps.shape, bf16)
        share = FF // S
        for owner in range(S):
            base = owner * ps.shape[1] // S
            ps[0, base : base + 8, 0:width] = smg[0:8, owner * width : (owner + 1) * width].astype(bf16)
            for r in range(share // width):
                start = owner * share + r * width
                a, b = start // D, start % D
                ps[0, base + 16 + r : base + 17 + r, 0:width] = smg[IB + a : IB + a + 1, b : b + width].astype(bf16)
        sum_s.core_start()
        input_back(2)
        tick("q2", 1)
        tick("s", 1)
        for r in range(L // PP):
            rows = pl.ds(r * PP, PP)
            grads[rows, :] = gsec[rows, :].astype(bf16)
        gin_move = Ungroup(grads, gin_o, rg_send.at[1], rg_recv.at[1], rg_local.at[1], C, G)
        gin_move.start()
        order = ("u", "i0", "i1", "o", "q0", "q1", "q2", "s")
        for stage_no in range(2, len(ticks["u"])):
            for name in ("q2", "s", "q1", "q0", "o", "i1", "i0", "u"):
                tick(name, stage_no)
        for name in order:
            tick(name, len(ticks[name]))
        gin_move.finish()
        gin_move.drain()
        drain_stage()

    pl.run_scoped(
        attention, V((D, 3 * D), bf16), V((L, D), bf16), V((NP, L, 128), bf16), V((NP, 128, L), bf16),
        V((2, M, L, 128), bf16), V((2, M, L, 128), bf16), V((M, L, L), f32 if M <= 2 else bf16), V((NP, 2, L), f32),
        V((2, L, 128), f32), V((2, L, 128), f32), V((2, max(M - 1, 1), 2, L, 128), bf16),
        V((2, max(M - 1, 1), 2, L, 128), bf16), V((M, G, 1, PP), jnp.int32), V((L, 3 * T), bf16), V((128, L), f32),
        V((2, L, 128), bf16),
    )
    out_move.finish()
    out_move.drain()
    for item in [sum_u] + sum_i + [sum_o] + sum_q + [sum_s]:
        item.drain()


def backward_call(S, C, G, PP, saved):
    (xs, wq, wo, wi, wu, k, v, q, qt, seg, lse, ctxt, ctx, n1, f1, flow, act, dgel, gsec, gb, outv, smg, sm) = saved
    L, D = xs.shape
    M, NP, FF = C // G, D // 128, wi.shape[1]
    R, RU = D // S, FF // S
    sds = jax.ShapeDtypeStruct
    land = max(M - 1, 1)
    H, SR, SW = D // 2, 32, 256
    outs = [
        ((G, PP, D), bf16), ((G, PP, D), bf16), ((R, 3 * D), bf16), ((R, D), bf16), ((R, FF), bf16), ((RU, D), bf16),
        ((NP, land, 2, L, 128), bf16), ((2, SR, SW), bf16),
    ]
    scratch = [
        (2, FF, H), (2, 2, D, D), (2, D, H), (3, 2, D, H), (2, S * SR, SW),
        (FF, H), (2, D, D), (D, H), (3, D, H), (S * SR, SW),
        (2, S - 1, RU // 2, H), (2, 2, S - 1, R // 2, D), (2, S - 1, R // 2, H), (3, 2, S - 1, R // 2, H),
        (2, S - 1, SR // 2, SW),
        (RU, H), (2, R, D), (R, H), (3, R, H), (SR, SW),
        (RU, H), (2, R, D), (R, H), (3, R, H), (SR, SW),
    ]
    scratch = [(x, bf16) for x in scratch] + [
        ((L, D), f32), ((L, D), bf16), ((NP, L, 128), bf16), ((NP, 128, L), bf16), ((NP, 2, L), f32), ((16, D), f32),
    ]
    dma = pltpu.SemaphoreType.DMA
    sems = [
        dma((8, 4)), dma((8, 4)), dma((8, 2, S - 1)), dma((8, 2, S - 1)), dma((8, 3)), dma((8, 3)),
        dma((2, G)), dma((2, G)), dma((2,)), dma((10,)), dma((2, 2)), dma((2, land)), dma((NP, land)), dma((1,)),
        dma((8, 3)),
    ]
    results = pl.pallas_call(
        functools.partial(backward_kernel, (S, C, G, PP)),
        out_shape=[sds(*o) for o in outs],
        in_specs=[ANY] * 21 + [VMEM, VMEM],
        out_specs=[ANY] * len(outs),
        scratch_shapes=[pltpu.VMEM(*x) for x in scratch] + sems,
        compiler_params=pltpu.CompilerParams(
            collective_id=1, has_side_effects=True, vmem_limit_bytes=62 << 20
        ),
        name="backward",
    )(outv, gsec, gb, act, dgel, wu, wi, wo, wq, flow, n1, f1, xs, ctx, ctxt, q, qt, k, v, seg, lse, smg, sm)
    return results


def solution(mesh):
    S, C = mesh.shape["seq"], mesh.shape["ctx"]

    def on_device(
        hid, cot, seg, wq, qb, vb, wo, ob, fg, fs, wi, ib, wu, ub, sg, ss
    ):
        G, PP, D = hid.shape
        small = pack_small(S, [qb, vb, ob, fg, fs, ub, sg, ss], ib, D)
        saved = forward_call(S, C, hid, cot, seg.reshape(G, 1, PP), wq, wo, wi, wu, small)
        out, gin, gq, go, gi, gu, _, gs = backward_call(S, C, G, PP, saved)
        gs = gs[0].astype(f32)
        width = D // S
        row = lambda r: gs[r, :width]
        grad_ib = gs[16 : 16 + ib.shape[0] // width, :width].reshape(-1)
        return (
            out, gin.astype(f32), gq.astype(f32), row(QB), row(VB), go.astype(f32), row(OB), row(FG), row(FS),
            gi.astype(f32), grad_ib, gu.astype(f32), row(UB), row(SG), row(SS),
        )

    rows, matrix, vector = P("seq", "ctx", None), P("seq", None), P("seq")
    return jax.shard_map(
        on_device,
        mesh=mesh,
        in_specs=(
            rows, rows, P("seq", "ctx"), matrix, vector, vector, matrix, vector, vector, vector, matrix, vector,
            matrix, vector, vector, vector,
        ),
        out_specs=(
            rows, rows, matrix, vector, vector, matrix, vector, vector, vector, matrix, vector, matrix, vector,
            vector, vector,
        ),
        check_vma=False,
    )
```

```python
import functools

import jax
import jax.numpy as jnp
from jax import lax
from jax.experimental import pallas as pl
from jax.experimental.pallas import tpu as pltpu
from jax.sharding import PartitionSpec as P

HEAD_DIM = 64
EPS = 1e-12
NEG = -1e30
RB = 64
ROOT_HALF = 0.7071067811865476
PDF_SCALE = 0.3989422804014327
f32 = jnp.float32
bf16 = jnp.bfloat16
MESH = pl.DeviceIdType.MESH
ANY = pl.BlockSpec(memory_space=pl.ANY)
VMEM = pl.BlockSpec(memory_space=pltpu.VMEM)

QB, VB, OB, FG, FS, UB, SG, SS, IB = 0, 1, 2, 3, 4, 5, 6, 7, 8


def tile(i, width):
    return pl.ds(pl.multiple_of(i * width, width), width)


def span(start, width, unit=128):
    return pl.ds(pl.multiple_of(start, unit), width)


def dotf(a, b):
    return jnp.dot(a, b, preferred_element_type=f32)


def dotg(a, b, ca, cb):
    return lax.dot_general(a, b, (((ca,), (cb,)), ((), ())), preferred_element_type=f32)


def remote(src, dst, send_sem, recv_sem, **where):
    return pltpu.make_async_remote_copy(
        src_ref=src,
        dst_ref=dst,
        send_sem=send_sem,
        recv_sem=recv_sem,
        device_id=where,
        device_id_type=MESH,
    )


def enter(S, C):
    s, c = lax.axis_index("seq"), lax.axis_index("ctx")
    barrier = pltpu.get_barrier_semaphore()
    for d in range(1, S):
        pl.semaphore_signal(
            barrier, inc=1, device_id={"seq": lax.rem(s + d, S)}, device_id_type=MESH
        )

    def greet(d, carry):
        pl.semaphore_signal(
            barrier, inc=1, device_id={"ctx": lax.rem(c + d, C)}, device_id_type=MESH
        )
        return carry

    lax.fori_loop(1, C, greet, 0)
    pl.semaphore_wait(barrier, S - 1 + C - 1)


def bit_orders(S):
    bits = [1 << k for k in range(S.bit_length() - 1)]
    return (bits, bits[1:] + bits[:1])


def subsets(bits):
    out = [0]
    for b in bits:
        out = out + [o | b for o in out]
    return out


class Gather:
    def __init__(self, S, shard, full, send, recv, swap_send, swap_recv, local):
        self.S, self.shard, self.full = S, shard, full
        self.send, self.recv, self.local = send, recv, local
        self.swap_send, self.swap_recv = swap_send, swap_recv
        self.R, self.N = shard.shape
        self.s, self.c = lax.axis_index("seq"), lax.axis_index("ctx")
        self.cols = span(lax.rem(self.c, 2) * (self.N // 2), self.N // 2)
        self.orders = bit_orders(S)
        self.steps = len(self.orders[0])
        self.half = self.R // 2

    def block(self, owner, p):
        return self.full.at[span(owner * self.R + p * self.half, self.half, 16), self.cols]

    def copy_own(self):
        return pltpu.make_async_copy(
            self.shard, self.full.at[span(self.s * self.R, self.R, 16), :], self.local
        )

    def copies(self, t, direct):
        out = []
        for p in range(2):
            order = self.orders[p]
            for i, mask in enumerate(subsets(order[:t])):
                if (mask == 0) == direct:
                    owner = jnp.bitwise_xor(self.s, mask)
                    src = self.block(owner, p)
                    if mask == 0:
                        src = self.shard.at[pl.ds(p * self.half, self.half), self.cols]
                    k = (1 << t) - 1 + i
                    peer = jnp.bitwise_xor(self.s, order[t])
                    out.append(remote(src, self.block(owner, p), self.send.at[p, k], self.recv.at[p, k], seq=peer))
        return out

    def swaps(self, t, direct):
        out = []
        for p in range(2):
            order = self.orders[p]
            for i, mask in enumerate(subsets(order[:t])):
                if (mask == 0) == direct:
                    got = self.block(jnp.bitwise_xor(self.s, order[t] ^ mask), p)
                    k = (1 << t) - 1 + i
                    out.append(
                        remote(
                            got, got, self.swap_send.at[p, k], self.swap_recv.at[p, k], ctx=jnp.bitwise_xor(self.c, 1)
                        )
                    )
        return out

    def start(self):
        for t in range(self.steps):
            for copy in self.copies(t, True):
                copy.start()
        self.copy_own().start()

    def pass_on(self, t):
        for copy in self.copies(t, False):
            copy.start()

    def arrive(self, t, direct):
        for copy in self.copies(t, direct):
            copy.wait_recv()
        for copy in self.swaps(t, direct):
            copy.start()

    def first(self):
        self.arrive(0, True)
        self.pass_on(1)

    def middle(self):
        for t in range(1, self.steps):
            self.arrive(t, True)
            if t + 1 < self.steps:
                self.arrive(t, False)
                self.pass_on(t + 1)

    def last(self):
        self.arrive(self.steps - 1, False)

    def ready(self, early, late):
        if early:
            self.copy_own().wait()
        for t in range(self.steps):
            for direct in (True, False):
                final = t == self.steps - 1 and not direct
                if late if final else early:
                    for copy in self.swaps(t, direct):
                        copy.wait_recv()

    def drain(self):
        for t in range(self.steps):
            for direct in (True, False):
                for copy in self.copies(t, direct) + self.swaps(t, direct):
                    copy.wait_send()


class Regroup:
    def __init__(self, src, dst, send, recv, local, C, G):
        self.src, self.dst, self.send, self.recv, self.local = src, dst, send, recv, local
        self.G, self.M = G, C // G
        self.c = lax.axis_index("ctx")

    def dst_at(self, j):
        if len(self.dst.shape) == 2:
            rows = self.src.shape[1]
            return self.dst.at[tile(j, rows), :]
        return self.dst.at[j]

    def each(self, on_remote, on_local):
        place = lax.rem(self.c, self.G)
        for g in range(self.G):
            target = g * self.M + lax.div(self.c, self.G)
            far = remote(
                self.src.at[g], self.dst_at(place), self.send.at[g], self.recv.at[place], ctx=target
            )
            near = pltpu.make_async_copy(self.src.at[g], self.dst_at(place), self.local)

            @pl.when(target != self.c)
            def _():
                on_remote(far)

            @pl.when(target == self.c)
            def _():
                on_local(near)

    def start(self):
        self.each(lambda far: far.start(), lambda near: near.start())

    def drain(self):
        self.each(lambda far: far.wait_send(), lambda near: None)

    def finish(self):
        m = lax.rem(self.c, self.M)
        for j in range(self.G):
            source = m * self.G + j

            @pl.when(source != self.c)
            def _():
                remote(
                    self.src.at[0], self.dst_at(j), self.send.at[0], self.recv.at[j], ctx=source
                ).wait_recv()

            @pl.when(source == self.c)
            def _():
                pltpu.make_async_copy(self.src.at[0], self.dst_at(j), self.local).wait()


class Ungroup:
    def __init__(self, src, dst, send, recv, local, C, G):
        self.src, self.dst, self.send, self.recv, self.local = src, dst, send, recv, local
        self.G, self.M, self.P = G, C // G, dst.shape[1]
        self.c = lax.axis_index("ctx")

    def each(self, on_remote, on_local):
        g, m = lax.div(self.c, self.M), lax.rem(self.c, self.M)
        for j in range(self.G):
            target = m * self.G + j
            rows = self.src.at[pl.ds(j * self.P, self.P), :]
            far = remote(rows, self.dst.at[g], self.send.at[j], self.recv.at[g], ctx=target)
            near = pltpu.make_async_copy(rows, self.dst.at[g], self.local)

            @pl.when(target != self.c)
            def _():
                on_remote(far)

            @pl.when(target == self.c)
            def _():
                on_local(near)

    def start(self):
        self.each(lambda far: far.start(), lambda near: near.start())

    def drain(self):
        self.each(lambda far: far.wait_send(), lambda near: None)

    def finish(self):
        rows = self.src.at[pl.ds(0, self.P), :]
        for g in range(self.G):
            source = g * self.M + lax.div(self.c, self.G)

            @pl.when(source != self.c)
            def _():
                remote(
                    rows, self.dst.at[g], self.send.at[0], self.recv.at[g], ctx=source
                ).wait_recv()

            @pl.when(source == self.c)
            def _():
                pltpu.make_async_copy(rows, self.dst.at[g], self.local).wait()


def mask_bias(seg_keys, seg_queries, bias, G, PP):
    rows = [seg_queries[i].astype(f32) for i in range(G)]
    for a in range(G):
        column = jnp.broadcast_to(seg_keys[a].astype(f32), (PP, PP)).T
        for b in range(G):
            bias[a * PP : (a + 1) * PP, b * PP : (b + 1) * PP] = jnp.where(
                column == rows[b], jnp.zeros((PP, PP), f32), jnp.full((PP, PP), NEG, f32)
            ).astype(bias.dtype)


def norm_rows(x):
    centred = x - jnp.mean(x, axis=-1, keepdims=True)
    factor = lax.rsqrt(jnp.mean(centred * centred, axis=-1, keepdims=True) + EPS)
    return centred * factor, factor


def norm_back(g, gain, normed, factor):
    h = g * gain
    return factor * (
        h
        - jnp.mean(h, axis=-1, keepdims=True)
        - normed * jnp.mean(h * normed, axis=-1, keepdims=True)
    )


def loop(n, body):
    def step(i, carry):
        body(i)
        return carry

    lax.fori_loop(0, n, step, 0)


def colsum(x):
    return jnp.sum(x, axis=0, keepdims=True)


def forward_kernel(
    dims,
    hid, cot, seg, wq_s, wo_s, wi_s, wu_s, small,
    xs_o, wq_o, wo_o, wi_o, wu_o, k_o, v_o, q_o, qt_o, seg_o, lse_o, ctxt_o, ctx_o,
    n1_o, f1_o, flow_o, act_o, dgel_o, gsec_o, gb_o, out_o, smg_o, sm_o,
    xs, ct, wq, wo, wi, wu, small_all, segc, segk, q, qt, kown, vown, kc, vc, bias, m_s, l_s, ctxt, ctx,
    first, n1, f1, flow, h, act, dgel, n2, gsec, gb, outv,
    ag_send, ag_recv, sw_send, sw_recv, ag_local, rg_send, rg_recv, rg_local, sm_send, sm_recv,
    kv_send, kv_recv, kv_local, kc_sem, out_sem,
):
    S, C, G, PP = dims
    M, L, D = C // G, G * PP, hid.shape[2]
    FF = wi.shape[1]
    NP = D // 128
    T = 256
    s, c = lax.axis_index("seq"), lax.axis_index("ctx")
    m = lax.rem(c, M)

    gathers = [
        Gather(S, shard, full, *[a.at[w] for a in (ag_send, ag_recv, sw_send, sw_recv, ag_local)])
        for w, (shard, full) in enumerate(((wq_s, wq), (wo_s, wo), (wi_s, wi), (wu_s, wu)))
    ]
    gq, go, gi, gu = gathers
    pending = []

    def put(src, dst):
        copy = pltpu.make_async_copy(src, dst, out_sem.at[len(pending)])
        copy.start()
        pending.append(copy)

    enter(S, C)
    hid_move = Regroup(hid, xs, rg_send.at[0], rg_recv.at[0], rg_local.at[0], C, G)
    cot_move = Regroup(cot, ct, rg_send.at[1], rg_recv.at[1], rg_local.at[1], C, G)
    seg_move = Regroup(seg, segc, rg_send.at[2], rg_recv.at[2], rg_local.at[2], C, G)
    seg_move.start()
    hid_move.start()
    gq.start()
    small_copies = [
        remote(small, small_all.at[d - 1], sm_send.at[d - 1], sm_recv.at[d - 1], seq=jnp.bitwise_xor(s, d))
        for d in range(1, S)
    ]
    for copy in small_copies:
        copy.start()
    seg_move.finish()

    group = lax.div(c, M) * M
    seg_own = pltpu.make_async_copy(segc, seg_o.at[m], kv_local.at[2])
    seg_own.start()

    def peer(d):
        return group + lax.rem(m + d, M)

    def kv_copies(d):
        return [
            remote(src, dst.at[m], kv_send.at[i, d], kv_recv.at[i, m], ctx=peer(d))
            for i, (src, dst) in enumerate(((kown, k_o), (vown, v_o), (segc, seg_o)))
        ]

    def kv_arrivals(d):
        j = lax.rem(m + d, M)
        return [
            remote(src, dst.at[j], kv_send.at[i, d], kv_recv.at[i, j], ctx=peer(d))
            for i, (src, dst) in enumerate(((kown, k_o), (vown, v_o), (segc, seg_o)))
        ]

    for d in range(1, M):
        kv_copies(d)[2].start()

    total = small[...].astype(f32)
    for copy in small_copies:
        copy.wait_recv()
    for d in range(1, S):
        total = total + small_all[d - 1].astype(f32)
    sm_o[...] = total
    mask_bias(segc, segc, bias, G, PP)
    gq.first()
    go.start()
    gi.start()
    gq.middle()
    gq.last()
    hid_move.finish()
    cot_move.start()
    put(xs, xs_o)
    gq.ready(True, True)
    put(wq, wq_o)

    def project(i):
        cols = tile(i, T)
        qv = dotf(xs[...], wq[:, cols]) + sm_o[QB : QB + 1, cols]
        kv = dotf(xs[...], wq[:, span(D + i * T, T)])
        vv = dotf(xs[...], wq[:, span(2 * D + i * T, T)]) + sm_o[VB : VB + 1, cols]
        qs = (qv.astype(bf16).astype(f32) * HEAD_DIM**-0.5).astype(bf16)
        kv, vv = kv.astype(bf16), vv.astype(bf16)
        for u in range(T // 128):
            lanes = slice(u * 128, (u + 1) * 128)
            hp = i * (T // 128) + u
            q[hp] = qs[:, lanes]
            qt[hp] = qs[:, lanes].T
            kown[hp] = kv[:, lanes]
            vown[hp] = vv[:, lanes]

    loop(D // T, project)
    for d in range(1, M):
        for copy in kv_copies(d)[:2]:
            copy.start()
    own_kv = [
        pltpu.make_async_copy(kown, k_o.at[m], kv_local.at[0]),
        pltpu.make_async_copy(vown, v_o.at[m], kv_local.at[1]),
    ]
    for copy in own_kv:
        copy.start()
    put(q, q_o)
    put(qt, qt_o)
    go.first()
    gi.first()
    gu.start()

    row_of = lax.broadcasted_iota(jnp.int32, (128, L), 0)

    def attend(keys, values, fresh, extra):
        def pair(hp):
            extra(hp)
            qv, kv, vt, b = qt[hp], keys[hp], values[hp].T, bias[...]
            for e in range(2):
                head = slice(e * HEAD_DIM, (e + 1) * HEAD_DIM)
                mine = (row_of < HEAD_DIM) if e == 0 else (row_of >= HEAD_DIM)
                scores = dotf(kv, jnp.where(mine, qv, jnp.zeros_like(qv))) + b
                top = jnp.max(scores, axis=0, keepdims=True)
                if fresh:
                    weights = jnp.exp(scores - top)
                    m_s[hp, e : e + 1, :] = top
                    l_s[hp, e : e + 1, :] = colsum(weights)
                    ctxt[hp, head, :] = dotf(vt[head], weights.astype(bf16))
                else:
                    old = m_s[hp, e : e + 1, :]
                    top = jnp.maximum(old, top)
                    keep = jnp.exp(old - top)
                    weights = jnp.exp(scores - top)
                    m_s[hp, e : e + 1, :] = top
                    l_s[hp, e : e + 1, :] = l_s[hp, e : e + 1, :] * keep + colsum(weights)
                    ctxt[hp, head, :] = ctxt[hp, head, :] * keep + dotf(vt[head], weights.astype(bf16))

        loop(NP, pair)

    def in_own(hp):
        @pl.when(hp == NP - 2)
        def _():
            go.middle()
            go.last()

    attend(kown, vown, True, in_own)

    def far_chunk(d, carry):
        j = lax.rem(m + d, M)
        for copy in kv_arrivals(d):
            copy.wait_recv()
        loads = [
            pltpu.make_async_copy(k_o.at[j], kc, kc_sem.at[0]),
            pltpu.make_async_copy(v_o.at[j], vc, kc_sem.at[1]),
            pltpu.make_async_copy(seg_o.at[j], segk, kc_sem.at[2]),
        ]
        for copy in loads:
            copy.start()
        for copy in loads:
            copy.wait()
        mask_bias(segk, segc, bias, G, PP)
        attend(kc, vc, False, lambda hp: None)
        return carry

    lax.fori_loop(1, M, far_chunk, 0)

    def close(hp):
        for e in range(2):
            head = slice(e * HEAD_DIM, (e + 1) * HEAD_DIM)
            ctxt[hp, head, :] = ctxt[hp, head, :] / l_s[hp, e : e + 1, :]
            l_s[hp, e : e + 1, :] = m_s[hp, e : e + 1, :] + jnp.log(l_s[hp, e : e + 1, :])
        ctx[:, tile(hp, 128)] = ctxt[hp].T.astype(bf16)

    loop(NP, close)

    put(ctxt, ctxt_o)
    put(ctx, ctx_o)
    put(l_s, lse_o)
    gi.middle()
    gi.last()
    go.ready(True, True)
    put(wo, wo_o)

    def project_out(i):
        cols = tile(i, T)
        first[:, cols] = dotf(ctx[...], wo[:, cols]) + sm_o[OB : OB + 1, cols]

    loop(D // T, project_out)

    def first_norm(r):
        rows = tile(r, RB)
        normed, factor = norm_rows(first[rows, :] + xs[rows, :].astype(f32))
        y = normed * sm_o[FG : FG + 1, :] + sm_o[FS : FS + 1, :]
        n1[rows, :] = normed
        f1[rows, :] = factor
        first[rows, :] = y
        flow[rows, :] = y.astype(bf16)

    loop(L // RB, first_norm)
    put(n1, n1_o)
    put(f1, f1_o)
    put(flow, flow_o)
    gu.first()
    gi.ready(True, True)
    put(wi, wi_o)

    def feed_in(i):
        cols = tile(i, D)
        h[...] = dotf(flow[...], wi[:, cols]) + sm_o[pl.ds(IB + i, 1), :]

        def gelu(k):
            rows, lanes = tile(lax.div(k, D // T), RB), lax.rem(k, D // T) * T
            x = h[rows, span(lanes, T)]
            share = 0.5 * (1.0 + lax.erf(x * ROOT_HALF))
            act[rows, span(i * D + lanes, T)] = (x * share).astype(bf16)
            dgel[rows, span(i * D + lanes, T)] = (
                share + x * (PDF_SCALE * jnp.exp(-0.5 * x * x))
            ).astype(bf16)

        loop(L // RB * (D // T), gelu)

    loop(FF // D, feed_in)
    put(act, act_o)
    put(dgel, dgel_o)
    RU = FF // S

    def feed_out(masks, fresh):
        owners = [jnp.bitwise_xor(s, k) for k in masks]

        def step(i):
            cols = tile(i, T)
            total = sm_o[UB : UB + 1, cols] if fresh else n2[:, cols]
            for owner in owners:
                total = total + dotf(act[:, span(owner * RU, RU)], wu[span(owner * RU, RU), cols])
            n2[:, cols] = total

        loop(D // T, step)

    gu.middle()
    gu.ready(True, False)
    feed_out([k for k in range(S) if k & (k - 1) == 0], True)
    gu.last()
    gu.ready(False, True)
    put(wu, wu_o)
    feed_out([k for k in range(S) if k & (k - 1)], False)
    cot_move.finish()
    smg_o[...] = jnp.zeros(smg_o.shape, f32)

    def second_norm(r):
        rows = tile(r, RB)
        normed, factor = norm_rows(first[rows, :] + n2[rows, :])
        gain = sm_o[SG : SG + 1, :]
        outv[rows, :] = (normed * gain + sm_o[SS : SS + 1, :]).astype(bf16)
        g = ct[rows, :].astype(f32)
        smg_o[SG : SG + 1, :] += colsum(g * normed)
        smg_o[SS : SS + 1, :] += colsum(g)
        back = norm_back(g, gain, normed, factor)
        gsec[rows, :] = back
        low = back.astype(bf16)
        gb[rows, :] = low
        smg_o[UB : UB + 1, :] += colsum(low.astype(f32))

    loop(L // RB, second_norm)
    put(outv, out_o)
    put(gsec, gsec_o)
    put(gb, gb_o)

    for gather in gathers:
        gather.drain()
    for move in (hid_move, cot_move, seg_move):
        move.drain()
    for copy in small_copies:
        copy.wait_send()
    for d in range(1, M):
        for copy in kv_copies(d):
            copy.wait_send()
    for copy in own_kv + [seg_own] + pending:
        copy.wait()


def forward_call(S, C, hid, cot, seg, wq_s, wo_s, wi_s, wu_s, small):
    G, PP, D = hid.shape
    L, M, NP, FF = G * PP, C // G, D // 128, wi_s.shape[1]
    sds = jax.ShapeDtypeStruct
    outs = [
        ((L, D), bf16), ((D, 3 * D), bf16), ((D, D), bf16), ((D, FF), bf16), ((FF, D), bf16),
        ((M, NP, L, 128), bf16), ((M, NP, L, 128), bf16), ((NP, L, 128), bf16), ((NP, 128, L), bf16),
        ((M, G, 1, PP), jnp.int32), ((NP, 2, L), f32), ((NP, 128, L), f32), ((L, D), bf16),
        ((L, D), f32), ((L, 1), f32), ((L, D), bf16), ((L, FF), bf16), ((L, FF), bf16),
        ((L, D), f32), ((L, D), bf16), ((L, D), bf16),
    ]
    scratch = [
        ((L, D), bf16), ((L, D), bf16), ((D, 3 * D), bf16), ((D, D), bf16), ((D, FF), bf16), ((FF, D), bf16),
        ((S - 1, 16, D), bf16), ((G, 1, PP), jnp.int32), ((G, 1, PP), jnp.int32),
        ((NP, L, 128), bf16), ((NP, 128, L), bf16), ((NP, L, 128), bf16), ((NP, L, 128), bf16),
        ((NP, L, 128), bf16), ((NP, L, 128), bf16), ((L, L), f32), ((NP, 2, L), f32), ((NP, 2, L), f32),
        ((NP, 128, L), f32), ((L, D), bf16),
        ((L, D), f32), ((L, D), f32), ((L, 1), f32), ((L, D), bf16), ((L, D), f32), ((L, FF), bf16),
        ((L, FF), bf16), ((L, D), f32), ((L, D), f32), ((L, D), bf16), ((L, D), bf16),
    ]
    dma = pltpu.SemaphoreType.DMA
    sems = [
        dma((4, 2, S)), dma((4, 2, S)), dma((4, 2, S)), dma((4, 2, S)), dma((4,)), dma((3, G)), dma((3, G)), dma((3,)),
        dma((S - 1,)), dma((S - 1,)), dma((3, M)), dma((3, M)), dma((3,)), dma((3,)), dma((24,)),
    ]
    return pl.pallas_call(
        functools.partial(forward_kernel, (S, C, G, PP)),
        out_shape=[sds(*o) for o in outs] + [sds((16, D), f32), sds((16, D), f32)],
        in_specs=[ANY] * 7 + [VMEM],
        out_specs=[ANY] * len(outs) + [VMEM, VMEM],
        scratch_shapes=[pltpu.VMEM(*x) for x in scratch] + sems,
        compiler_params=pltpu.CompilerParams(
            collective_id=0, has_side_effects=True, vmem_limit_bytes=62 << 20
        ),
        name="forward",
    )(hid, cot, seg, wq_s, wo_s, wi_s, wu_s, small)


def pack_small(S, vectors, inner_bias, D):
    s = lax.axis_index("seq")
    width = D // S
    owner = lax.broadcasted_iota(jnp.int32, (1, D), 1) // width
    rows = [jnp.where(owner == s, jnp.tile(v, S)[None, :], 0) for v in vectors]
    share = inner_bias.shape[0]
    flat = jnp.tile(inner_bias, S)
    where = lax.broadcasted_iota(jnp.int32, (1, share * S), 1) // share
    full = jnp.where(where == s, flat[None, :], 0).reshape(share * S // D, D)
    used = len(vectors) + share * S // D
    return jnp.concatenate(rows + [full, jnp.zeros((16 - used, D), bf16)], axis=0).astype(bf16)


def add_rows(dst, src):
    rows = dst.shape[0]
    unit = next(u for u in (96, 48, 16) if rows % u == 0)

    def step(r):
        at = tile(r, unit)
        dst[at, :] = (dst[at, :].astype(f32) + src[at, :].astype(f32)).astype(bf16)

    loop(rows // unit, step)


class CoreSwap:
    def __init__(self, part, far, rows, send, recv):
        self.part, self.far, self.rows, self.send, self.recv = part, far, rows, send, recv
        self.c = lax.axis_index("ctx")
        self.core = lax.rem(self.c, 2)
        self.count = part.shape[1] // rows

    def copy(self, i):
        rows = tile(i, self.rows)
        return remote(
            self.part.at[1 - self.core, rows, :], self.far.at[rows, :], self.send.at[i], self.recv.at[i],
            ctx=jnp.bitwise_xor(self.c, 1),
        )

    def start(self, i):
        self.copy(i).start()

    def add(self):
        loop(self.count, lambda i: self.copy(i).wait_recv())
        add_rows(self.part.at[self.core], self.far)

    def drain(self):
        loop(self.count, lambda i: self.copy(i).wait_send())


class Reduce:
    def __init__(self, S, C, part, stride, offset, R, cols, rx, zl, zr, sems, places):
        self.S, self.K, self.part, self.rx, self.zl, self.zr = S, C // 2, part, rx, zl, zr
        self.c_send, self.c_recv, self.x_send, self.x_recv, self.z_send, self.z_recv, self.l_send = sems
        self.places, self.stride, self.offset, self.R, self.cols = places, stride, offset, R, cols
        self.half = R // 2
        self.s, self.c = lax.axis_index("seq"), lax.axis_index("ctx")
        self.core = lax.rem(self.c, 2)
        self.k = lax.div(self.c, 2)
        self.left, self.right = self.K // 2 - 1, self.K // 2
        self.orders = bit_orders(S)
        self.steps = len(self.orders[0])

    def rows(self, owner, start, count):
        return self.part.at[self.core, span(owner * self.stride + self.offset + start, count, 16), self.cols]

    def block(self, owner, p):
        return self.rows(owner, p * self.half, self.half)

    def result(self):
        return self.rows(self.s, 0, self.R)

    def copies(self, t):
        out, base = [], self.S - (1 << (self.steps - t))
        for p in range(2):
            order = self.orders[p]
            peer = jnp.bitwise_xor(self.s, order[t])
            for i, mask in reversed(list(enumerate(subsets(order[t + 1 :])))):
                copy = remote(
                    self.block(jnp.bitwise_xor(peer, mask), p),
                    self.rx.at[p, base + i],
                    self.x_send.at[p, base + i],
                    self.x_recv.at[p, base + i],
                    seq=peer,
                )
                out.append((copy, p, base + i, mask))
        return out

    def cross_start(self, t):
        if t > 0:
            self.cross_add(t - 1, False)
        for copy, _, _, _ in self.copies(t):
            copy.start()

    def cross_add(self, t, last):
        for copy, p, slot, mask in self.copies(t):
            if (mask == 0) == last:
                copy.wait_recv()
                add_rows(self.block(jnp.bitwise_xor(self.s, mask), p), self.rx.at[p, slot])

    def from_left(self):
        return remote(self.result(), self.zl, self.z_send.at[0], self.z_recv.at[0], ctx=self.c + 2)

    def from_right(self):
        return remote(self.result(), self.zr, self.z_send.at[0], self.z_recv.at[1], ctx=self.c - 2)

    def out_left(self):
        return remote(self.zr, self.zr, self.z_send.at[1], self.z_recv.at[1], ctx=self.c - 2)

    def out_right(self):
        return remote(self.zl, self.zl, self.z_send.at[1], self.z_recv.at[0], ctx=self.c + 2)

    def inward(self, level):
        if level == 0:
            for t in range(self.steps):
                self.cross_add(t, True)

        @pl.when(self.k == level)
        def _():
            if level > 0:
                self.from_left().wait_recv()
                add_rows(self.result(), self.zl)
            self.from_left().start()

        @pl.when(self.k == self.K - 1 - level)
        def _():
            if level > 0:
                self.from_right().wait_recv()
                add_rows(self.result(), self.zr)
            self.from_right().start()

    def outward(self, distance):
        @pl.when(self.k == self.left - distance)
        def _():
            self.from_right().wait_recv()
            if distance == 0:
                add_rows(self.zr, self.result())
            if distance < self.left:
                self.out_left().start()
            self.deliver(self.zr)

        @pl.when(self.k == self.right + distance)
        def _():
            self.from_left().wait_recv()
            if distance == 0:
                add_rows(self.zl, self.result())
            if distance < self.left:
                self.out_right().start()
            self.deliver(self.zl)

    def deliveries(self, src):
        out = []
        for i, (cols, place) in enumerate(self.places):
            dst = place(self.core)
            out.append(
                (
                    pltpu.make_async_copy(src.at[:, cols], dst, self.l_send.at[i]),
                    remote(
                        src.at[:, cols], dst, self.c_send.at[i], self.c_recv.at[i], ctx=jnp.bitwise_xor(self.c, 1)
                    ),
                )
            )
        return out

    def deliver(self, src):
        for near, far in self.deliveries(src):
            near.start()
            far.start()

    def finish(self):
        for near, far in self.deliveries(self.zl):
            near.wait()
            far.wait_recv()

    def stages(self):
        out = [functools.partial(self.cross_start, t) for t in range(self.steps)]
        out += [functools.partial(self.inward, v) for v in range(self.left + 1)]
        out += [functools.partial(self.outward, d) for d in range(self.left + 1)]
        return out

    def drain(self):
        for t in range(self.steps):
            for copy, _, _, _ in self.copies(t):
                copy.wait_send()

        @pl.when(self.k <= self.left)
        def _():
            self.from_left().wait_send()

        @pl.when(self.k >= self.right)
        def _():
            self.from_right().wait_send()

        @pl.when(jnp.logical_and(self.k <= self.left, self.k > 0))
        def _():
            self.out_left().wait_send()

        @pl.when(jnp.logical_and(self.k >= self.right, self.k < self.K - 1))
        def _():
            self.out_right().wait_send()

        for _, far in self.deliveries(self.zl):
            far.wait_send()


SCHEDULE = {
    "ffn0": (('u0', 1), ('u1', 1), ('u2', 1)),
    "ffn2": (('u0', 2), ('i0', 1), ('i1', 1)),
    "ffn3": (('u1', 2), ('i2', 1)),
    "first": (('u2', 2), ('i3', 1)),
    "norm": (('u0', 3),),
    "context": (('i0', 2), ('o', 1)),
    "pair0": (('u0', 4), ('u1', 3), ('i1', 2), ('i2', 2)),
    "pair1": (('u2', 3),),
    "project0": (('u0', 5), ('u1', 4), ('i3', 2)),
    "input0": (('i0', 3), ('q0', 1), ('o', 2)),
    "pair2": (('u2', 4), ('u0', 6), ('i1', 3), ('u1', 5), ('i2', 3), ('i0', 4)),
    "pair3": (('i3', 3), ('q0', 2)),
    "project1": (('u1', 6), ('u2', 5), ('i1', 4), ('o', 3)),
    "input1": (('i0', 5), ('i2', 4), ('q0', 3), ('q1', 1)),
    "pair4": (('u2', 6), ('i1', 5), ('i3', 4), ('o', 4), ('q1', 2)),
    "pair5": (('i0', 6), ('i2', 5), ('q0', 4), ('q1', 3)),
    "project2": (('i1', 6), ('i3', 5)),
    "input2": (('o', 5), ('q2', 1), ('s', 1)),
    "end": (('i2', 6), ('q1', 4), ('q0', 5), ('i3', 6), ('q2', 2), ('s', 2), ('q2', 3), ('s', 3), ('q2', 4), ('s', 4), ('o', 6), ('q1', 5), ('q0', 6), ('q2', 5), ('s', 5), ('q1', 6), ('q2', 6), ('s', 6)),
}


def backward_kernel(
    dims,
    outv, gsec_i, gb_i, act_i, dgel_i, wu_i, wi_i, wo_i, wq_i, flow_i, n1_i, f1_i, xs_i, ctx_i, ctxt_i,
    q_i, qt_i, k_i, v_i, seg_i, lse_i, smg_i, sm,
    out_o, gin_o, gq_o, go_o, gi_o, gu_o, land_o, small_o,
    pu, pi, po, pq, ps, fu, fi, fo, fq, fs, rxu, rxi, rxs, zlu, zli, zls, zru, zri, zrs,
    gsec, gb, grad_o, grad_ot, delta, smg,
    cs_send, cs_recv, c_send, c_recv, x_send, x_recv, z_send, z_recv, rg_send, rg_recv, rg_local, in_sem, kv_sem, dkv_send, dkv_recv,
    land_sem, l_send,
):
    S, C, G, PP = dims
    M, L, D = C // G, G * PP, gsec.shape[1]
    FF = act_i.shape[1]
    NP = D // 128
    T = 256
    s, c = lax.axis_index("seq"), lax.axis_index("ctx")
    m, core = lax.rem(c, M), lax.rem(c, 2)
    group = lax.div(c, M) * M

    H = D // 2
    R, RU = D // S, FF // S
    cut = RU // 3
    items = {}

    def piece(name, places, *refs):
        n = len(items)
        sems = [a.at[n] for a in (c_send, c_recv, x_send, x_recv, z_send, z_recv, l_send)]
        items[name] = Reduce(S, C, *refs, sems, places)

    for i in range(3):
        piece(
            f"u{i}", [(pl.ds(0, H), lambda e, i=i: gu_o.at[pl.ds(i * cut, cut), span(e * H, H)])],
            pu, RU, i * cut, cut, pl.ds(0, H), rxu.at[i], zlu.at[i], zru.at[i],
        )

    def narrow_piece(name, places, part, cols):
        n = len(items) - 3
        piece(name, places, part, R, 0, R, cols, rxi.at[n], zli.at[n], zri.at[n])

    for i in range(2):
        for j in range(2):
            narrow_piece(
                f"i{2 * i + j}",
                [(pl.ds(0, H), lambda e, i=i, j=j: gi_o.at[:, span(e * (FF // 2) + i * D + j * H, H)])],
                pi.at[i], pl.ds(j * H, H),
            )
    narrow_piece("o", [(pl.ds(0, H), lambda e: go_o.at[:, span(e * H, H)])], po, pl.ds(0, H))
    for i in range(3):
        narrow_piece(
            f"q{i}",
            [
                (pl.ds(a * 128, 128), lambda e, i=i, a=a: gq_o.at[:, span(a * D + (2 * i + e) * 128, 128)])
                for a in range(3)
            ],
            pq.at[i], pl.ds(0, H),
        )
    SR, SW = ps.shape[1] // S, ps.shape[2]
    piece(
        "s", [(pl.ds(0, SW), lambda e: small_o.at[e])], ps, SR, 0, SR, pl.ds(0, SW), rxs, zls, zrs
    )
    swap_u = CoreSwap(pu, fu, 512, cs_send.at[0], cs_recv.at[0])
    swap_i = [CoreSwap(pi.at[i], fi.at[i], T, cs_send.at[1 + i], cs_recv.at[1 + i]) for i in range(2)]
    swap_o = CoreSwap(po, fo, T, cs_send.at[3], cs_recv.at[3])
    swap_q = [CoreSwap(pq.at[i], fq.at[i], T, cs_send.at[4 + i], cs_recv.at[4 + i]) for i in range(3)]
    swap_s = CoreSwap(ps, fs, ps.shape[1], cs_send.at[7], cs_recv.at[7])

    ticks = {name: item.stages() for name, item in items.items()}
    at = {name: 0 for name in items}
    last = len(ticks["s"])

    def tick(name, until):
        while at[name] < min(until, last):
            ticks[name][at[name]]()
            at[name] += 1

    def point(name):
        for chunk, until in SCHEDULE.get(name, ()):
            tick(chunk, until)

    enter(S, C)
    out_move = Ungroup(outv, out_o, rg_send.at[0], rg_recv.at[0], rg_local.at[0], C, G)
    out_move.start()
    smg[...] = smg_i[...]

    def feed_forward(act, dgel, wu, wi, h, n1, f1, flow):
        loads = [
            pltpu.make_async_copy(src, dst, in_sem.at[i])
            for i, (src, dst) in enumerate(
                ((gb_i, gb), (act_i, act), (wu_i, wu), (dgel_i, dgel), (flow_i, flow), (wi_i, wi), (gsec_i, gsec),
                 (n1_i, n1), (f1_i, f1))
            )
        ]
        for copy in loads:
            copy.start()
        loads[0].wait()
        loads[1].wait()

        def outer_grad(i):
            rows = tile(i, 512)
            block = dotg(act[:, rows], gb[...], 0, 0).astype(bf16)
            for e in range(2):
                pu[e, rows, :] = block[:, e * (D // 2) : (e + 1) * (D // 2)]
            swap_u.start(i)

        loop(FF // 512, outer_grad)
        for copy in loads[2:5]:
            copy.wait()

        def inner_grad(i, half, send):
            where = half * (FF // 2) + i * D
            cols = span(where, D)
            h[...] = dotg(gb[...], wu[span(where, D), :], 1, 1)

            def through(k, sums):
                rows = tile(k, RB)
                low = (h[rows, :] * dgel[rows, cols].astype(f32)).astype(bf16)
                act[rows, cols] = low
                return sums + colsum(low.astype(f32))

            sums = lax.fori_loop(0, L // RB, through, jnp.zeros((1, D), f32))
            smg[pl.ds(IB + half * (FF // 2 // D) + i, 1), :] = sums

            def grad(k):
                rows = tile(k, T)
                pi[i, half, rows, :] = dotg(flow[:, rows], act[:, cols], 0, 0).astype(bf16)
                if send:
                    swap_i[i].start(k)

            loop(D // T, grad)

        inner_grad(0, 1 - core, True)
        swap_u.add()
        point("ffn0")
        inner_grad(0, core, False)
        point("ffn1")
        inner_grad(1, 1 - core, True)
        swap_i[0].add()
        point("ffn2")
        inner_grad(1, core, False)
        swap_i[1].add()
        point("ffn3")
        loads[5].wait()
        loads[6].wait()

        def first_grad(i):
            cols = tile(i, T)
            gsec[:, cols] += dotg(act[...], wi[cols, :], 1, 1)

        loop(D // T, first_grad)
        point("first")
        loads[7].wait()
        loads[8].wait()

        def first_back(k):
            rows = tile(k, RB)
            g, normed = gsec[rows, :], n1[rows, :]
            smg[FG : FG + 1, :] += colsum(g * normed)
            smg[FS : FS + 1, :] += colsum(g)
            back = norm_back(g, sm[FG : FG + 1, :], normed, f1[rows, :])
            gsec[rows, :] = back
            low = back.astype(bf16)
            gb[rows, :] = low
            smg[OB : OB + 1, :] += colsum(low.astype(f32))

        loop(L // RB, first_back)

    V = pltpu.VMEM
    pl.run_scoped(
        feed_forward, V((L, FF), bf16), V((L, FF), bf16), V((FF, D), bf16), V((D, FF), bf16), V((L, D), f32),
        V((L, D), f32), V((L, 1), f32), V((L, D), bf16),
    )
    point("norm")

    def context_back(wo, ctx, ctxt):
        loads = [
            pltpu.make_async_copy(src, dst, in_sem.at[i])
            for i, (src, dst) in enumerate(((ctx_i, ctx), (wo_i, wo), (ctxt_i, ctxt)))
        ]
        for copy in loads:
            copy.start()
        loads[0].wait()

        def out_grad(k):
            rows = tile(k, T)
            block = dotg(ctx[:, rows], gb[...], 0, 0).astype(bf16)
            for e in range(2):
                po[e, rows, :] = block[:, e * (D // 2) : (e + 1) * (D // 2)]
            swap_o.start(k)

        loop(D // T, out_grad)
        loads[1].wait()
        loads[2].wait()

        def back(k):
            grad = dotg(gb[...], wo[tile(k, T), :], 1, 1).astype(bf16)
            for u in range(T // 128):
                hp = k * (T // 128) + u
                mine = grad[:, u * 128 : (u + 1) * 128]
                turned = mine.T
                grad_o[hp] = mine
                grad_ot[hp] = turned
                both = turned.astype(f32) * ctxt[hp]
                for e in range(2):
                    delta[hp, e : e + 1, :] = colsum(both[e * HEAD_DIM : (e + 1) * HEAD_DIM])

        loop(D // T, back)

    pl.run_scoped(context_back, V((D, D), bf16), V((L, D), bf16), V((NP, 128, L), f32))
    swap_o.add()
    point("context")

    def attention(wq, xs, q, qt, kb, vb, bias, lse, own_k, own_v, stage, land, segs, grads, dqt, turned_q):
        loads = [
            pltpu.make_async_copy(src, dst, in_sem.at[i])
            for i, (src, dst) in enumerate(
                ((seg_i, segs), (q_i, q), (qt_i, qt), (lse_i, lse), (xs_i, xs), (wq_i, wq))
            )
        ]

        def kv_load(hp):
            slot = lax.rem(hp, 2)
            return [
                pltpu.make_async_copy(src.at[:, hp], dst.at[slot], kv_sem.at[i, slot])
                for i, (src, dst) in enumerate(((k_i, kb), (v_i, vb)))
            ]

        for copy in kv_load(0) + loads:
            copy.start()
        for copy in loads[:4]:
            copy.wait()
        for j in range(M):
            mask_bias(segs.at[j], segs.at[m], bias.at[j], G, PP)
        row_of = lax.broadcasted_iota(jnp.int32, (128, L), 0)
        lane_of = lax.broadcasted_iota(jnp.int32, (L, 128), 1)

        def send_back(hp, d):
            slot = lax.rem(hp, 2)
            return remote(
                stage.at[slot, d - 1], land_o.at[hp, d - 1], dkv_send.at[slot, d - 1], dkv_recv.at[hp, d - 1],
                ctx=group + lax.rem(m + d, M),
            )

        def chunk(hp, slot, j):
            key, value, b = kb[slot, j], vb[slot, j], bias[j].astype(f32)
            turned = key.T
            query, query_t, up, up_t = q[hp], qt[hp], grad_o[hp], grad_ot[hp]
            sums = []
            for e in range(2):
                rows = (row_of < HEAD_DIM) if e == 0 else (row_of >= HEAD_DIM)
                lanes = (lane_of < HEAD_DIM) if e == 0 else (lane_of >= HEAD_DIM)
                zero, zero_t = jnp.zeros_like(query), jnp.zeros_like(query_t)
                scores = dotf(key, jnp.where(rows, query_t, zero_t)) + b
                probs = jnp.exp(scores - lse[hp, e : e + 1, :])
                dprobs = dotf(value, jnp.where(rows, up_t, zero_t))
                dscores = (probs * (dprobs - delta[hp, e : e + 1, :])).astype(bf16)
                sums.append(
                    (
                        dotf(dscores, jnp.where(lanes, query, zero)),
                        dotf(probs.astype(bf16), jnp.where(lanes, up, zero)),
                    )
                )
                head = slice(e * HEAD_DIM, (e + 1) * HEAD_DIM)
                dqt[head, :] += dotf(turned[head], dscores)
            return sums[0][0] + sums[1][0], sums[0][1] + sums[1][1]

        def pair(hp):
            slot = lax.rem(hp, 2)
            for copy in kv_load(hp):
                copy.wait()

            @pl.when(hp + 1 < NP)
            def _():
                for copy in kv_load(hp + 1):
                    copy.start()

            dqt[...] = jnp.zeros(dqt.shape, f32)

            def far(d, carry):
                @pl.when(hp >= 2)
                def _():
                    send_back(hp - 2, d).wait_send()

                dk, dv = chunk(hp, slot, lax.rem(m + d, M))
                stage[slot, d - 1, 0] = dk.astype(bf16)
                stage[slot, d - 1, 1] = dv.astype(bf16)
                send_back(hp, d).start()
                return carry

            lax.fori_loop(1, M, far, 0)
            dk, dv = chunk(hp, slot, m)
            own_k[slot] = dk
            own_v[slot] = dv
            turned_q[slot] = (dqt[...] * HEAD_DIM**-0.5).T.astype(bf16)

        def fetch(i):
            for u in range(2):
                for d in range(1, M):
                    send_back(2 * i + u, d).wait_recv()
            if M > 1:
                pltpu.make_async_copy(land_o.at[pl.ds(2 * i, 2)], land, land_sem.at[0]).start()

        def project_back(i):
            if M > 1:
                pltpu.make_async_copy(land_o.at[pl.ds(2 * i, 2)], land, land_sem.at[0]).wait()
            for u in range(2):
                dk, dv = own_k[u], own_v[u]
                for d in range(1, M):
                    dk = dk + land[u, d - 1, 0].astype(f32)
                    dv = dv + land[u, d - 1, 1].astype(f32)
                grads[:, u * 128 : (u + 1) * 128] = turned_q[u]
                grads[:, T + u * 128 : T + (u + 1) * 128] = dk.astype(bf16)
                grads[:, 2 * T + u * 128 : 2 * T + (u + 1) * 128] = dv.astype(bf16)
            cols = tile(i, T)
            smg[QB : QB + 1, cols] = colsum(grads[:, 0:T].astype(f32))
            smg[VB : VB + 1, cols] = colsum(grads[:, 2 * T : 3 * T].astype(f32))

            def weight(k):
                rows = tile(k, T)
                block = dotg(xs[:, rows], grads[...], 0, 0).astype(bf16)
                for a in range(3):
                    for e in range(2):
                        pq[i, e, rows, a * 128 : (a + 1) * 128] = block[:, a * T + e * 128 : a * T + (e + 1) * 128]
                swap_q[i].start(k)

            loop(D // T, weight)

        def input_back(i):
            def back(k):
                rows = tile(k, T)
                total = gsec[:, rows]
                for a in range(3):
                    total = total + dotg(grads[:, a * T : (a + 1) * T], wq[rows, span(a * D + i * T, T)], 1, 1)
                gsec[:, rows] = total

            loop(D // T, back)

        def drain_stage():
            for hp in (NP - 2, NP - 1):
                for d in range(1, M):
                    send_back(hp, d).wait_send()

        def pair_group(i):
            def body(u):
                pair(2 * i + u)
                for k in range(2):

                    @pl.when(u == k)
                    def _():
                        point(f"pair{2 * i + k}")

            loop(2, body)

        pair_group(0)
        fetch(0)
        loads[4].wait()
        loads[5].wait()
        project_back(0)
        point("project0")
        input_back(0)
        swap_q[0].add()
        point("input0")
        pair_group(1)
        fetch(1)
        project_back(1)
        point("project1")
        input_back(1)
        swap_q[1].add()
        point("input1")
        pair_group(2)
        fetch(2)
        project_back(2)

        width = D // S
        ps[...] = jnp.zeros(ps.shape, bf16)
        share = FF // S
        for owner in range(S):
            base = owner * ps.shape[1] // S
            ps[0, base : base + 8, 0:width] = smg[0:8, owner * width : (owner + 1) * width].astype(bf16)
            for r in range(share // width):
                start = owner * share + r * width
                a, b = start // D, start % D
                ps[0, base + 16 + r : base + 17 + r, 0:width] = smg[IB + a : IB + a + 1, b : b + width].astype(bf16)
        swap_s.start(0)
        point("project2")
        input_back(2)
        for r in range(L // PP):
            rows = pl.ds(r * PP, PP)
            grads[rows, :] = gsec[rows, :].astype(bf16)
        gin_move = Ungroup(grads, gin_o, rg_send.at[1], rg_recv.at[1], rg_local.at[1], C, G)
        gin_move.start()
        swap_q[2].add()
        swap_s.add()
        point("input2")
        point("end")
        for name in items:
            tick(name, last)
        gin_move.finish()
        gin_move.drain()
        drain_stage()

    pl.run_scoped(
        attention, V((D, 3 * D), bf16), V((L, D), bf16), V((NP, L, 128), bf16), V((NP, 128, L), bf16),
        V((2, M, L, 128), bf16), V((2, M, L, 128), bf16), V((M, L, L), f32 if M <= 2 else bf16), V((NP, 2, L), f32),
        V((2, L, 128), f32), V((2, L, 128), f32), V((2, max(M - 1, 1), 2, L, 128), bf16),
        V((2, max(M - 1, 1), 2, L, 128), bf16), V((M, G, 1, PP), jnp.int32), V((L, 3 * T), bf16), V((128, L), f32),
        V((2, L, 128), bf16),
    )
    out_move.finish()
    out_move.drain()
    for item in items.values():
        item.finish()
        item.drain()
    for swap in [swap_u] + swap_i + [swap_o] + swap_q + [swap_s]:
        swap.drain()


def backward_call(S, C, G, PP, saved):
    (xs, wq, wo, wi, wu, k, v, q, qt, seg, lse, ctxt, ctx, n1, f1, flow, act, dgel, gsec, gb, outv, smg, sm) = saved
    L, D = xs.shape
    M, NP, FF = C // G, D // 128, wi.shape[1]
    R, RU = D // S, FF // S
    sds = jax.ShapeDtypeStruct
    land = max(M - 1, 1)
    H, SR, SW = D // 2, 32, 256
    outs = [
        ((G, PP, D), bf16), ((G, PP, D), bf16), ((R, 3 * D), bf16), ((R, D), bf16), ((R, FF), bf16), ((RU, D), bf16),
        ((NP, land, 2, L, 128), bf16), ((2, SR, SW), bf16),
    ]
    cut = RU // 3
    scratch = [
        (2, FF, H), (2, 2, D, D), (2, D, H), (3, 2, D, H), (2, S * SR, SW),
        (FF, H), (2, D, D), (D, H), (3, D, H), (S * SR, SW),
        (3, 2, S - 1, cut // 2, H), (8, 2, S - 1, R // 2, H), (2, S - 1, SR // 2, SW),
        (3, cut, H), (8, R, H), (SR, SW),
        (3, cut, H), (8, R, H), (SR, SW),
    ]
    scratch = [(x, bf16) for x in scratch] + [
        ((L, D), f32), ((L, D), bf16), ((NP, L, 128), bf16), ((NP, 128, L), bf16), ((NP, 2, L), f32), ((16, D), f32),
    ]
    dma = pltpu.SemaphoreType.DMA
    sems = [
        dma((8, 8)), dma((8, 8)), dma((12, 3)), dma((12, 3)), dma((12, 2, S - 1)), dma((12, 2, S - 1)), dma((12, 2)),
        dma((12, 2)),
        dma((2, G)), dma((2, G)), dma((2,)), dma((10,)), dma((2, 2)), dma((2, land)), dma((NP, land)), dma((1,)),
        dma((12, 3)),
    ]
    results = pl.pallas_call(
        functools.partial(backward_kernel, (S, C, G, PP)),
        out_shape=[sds(*o) for o in outs],
        in_specs=[ANY] * 21 + [VMEM, VMEM],
        out_specs=[ANY] * len(outs),
        scratch_shapes=[pltpu.VMEM(*x) for x in scratch] + sems,
        compiler_params=pltpu.CompilerParams(
            collective_id=1, has_side_effects=True, vmem_limit_bytes=62 << 20
        ),
        name="backward",
    )(outv, gsec, gb, act, dgel, wu, wi, wo, wq, flow, n1, f1, xs, ctx, ctxt, q, qt, k, v, seg, lse, smg, sm)
    return results


def solution(mesh):
    S, C = mesh.shape["seq"], mesh.shape["ctx"]

    def on_device(
        hid, cot, seg, wq, qb, vb, wo, ob, fg, fs, wi, ib, wu, ub, sg, ss
    ):
        G, PP, D = hid.shape
        small = pack_small(S, [qb, vb, ob, fg, fs, ub, sg, ss], ib, D)
        saved = forward_call(S, C, hid, cot, seg.reshape(G, 1, PP), wq, wo, wi, wu, small)
        out, gin, gq, go, gi, gu, _, gs = backward_call(S, C, G, PP, saved)
        gs = gs[0].astype(f32)
        width = D // S
        row = lambda r: gs[r, :width]
        grad_ib = gs[16 : 16 + ib.shape[0] // width, :width].reshape(-1)
        return (
            out, gin.astype(f32), gq.astype(f32), row(QB), row(VB), go.astype(f32), row(OB), row(FG), row(FS),
            gi.astype(f32), grad_ib, gu.astype(f32), row(UB), row(SG), row(SS),
        )

    rows, matrix, vector = P("seq", "ctx", None), P("seq", None), P("seq")
    return jax.shard_map(
        on_device,
        mesh=mesh,
        in_specs=(
            rows, rows, P("seq", "ctx"), matrix, vector, vector, matrix, vector, vector, vector, matrix, vector,
            matrix, vector, vector, vector,
        ),
        out_specs=(
            rows, rows, matrix, vector, vector, matrix, vector, vector, vector, matrix, vector, matrix, vector,
            vector, vector,
        ),
        check_vma=False,
    )
```

```python
import functools

import jax
import jax.numpy as jnp
from jax import lax
from jax.experimental import pallas as pl
from jax.experimental.pallas import tpu as pltpu
from jax.sharding import PartitionSpec as P

HEAD_DIM = 64
EPS = 1e-12
NEG = -1e30
RB = 64
ROOT_HALF = 0.7071067811865476
PDF_SCALE = 0.3989422804014327
f32 = jnp.float32
bf16 = jnp.bfloat16
MESH = pl.DeviceIdType.MESH
ANY = pl.BlockSpec(memory_space=pl.ANY)
VMEM = pl.BlockSpec(memory_space=pltpu.VMEM)

QB, VB, OB, FG, FS, UB, SG, SS, IB = 0, 1, 2, 3, 4, 5, 6, 7, 8


def tile(i, width):
    return pl.ds(pl.multiple_of(i * width, width), width)


def span(start, width, unit=128):
    return pl.ds(pl.multiple_of(start, unit), width)


def dotf(a, b):
    return jnp.dot(a, b, preferred_element_type=f32)


def dotg(a, b, ca, cb):
    return lax.dot_general(a, b, (((ca,), (cb,)), ((), ())), preferred_element_type=f32)


def remote(src, dst, send_sem, recv_sem, **where):
    return pltpu.make_async_remote_copy(
        src_ref=src,
        dst_ref=dst,
        send_sem=send_sem,
        recv_sem=recv_sem,
        device_id=where,
        device_id_type=MESH,
    )


def enter(S, C):
    s, c = lax.axis_index("seq"), lax.axis_index("ctx")
    barrier = pltpu.get_barrier_semaphore()
    for d in range(1, S):
        pl.semaphore_signal(
            barrier, inc=1, device_id={"seq": lax.rem(s + d, S)}, device_id_type=MESH
        )

    def greet(d, carry):
        pl.semaphore_signal(
            barrier, inc=1, device_id={"ctx": lax.rem(c + d, C)}, device_id_type=MESH
        )
        return carry

    lax.fori_loop(1, C, greet, 0)
    pl.semaphore_wait(barrier, S - 1 + C - 1)


def bit_orders(S):
    bits = [1 << k for k in range(S.bit_length() - 1)]
    return (bits, bits[1:] + bits[:1])


def subsets(bits):
    out = [0]
    for b in bits:
        out = out + [o | b for o in out]
    return out


class Gather:
    def __init__(self, S, shard, full, send, recv, swap_send, swap_recv, local):
        self.S, self.shard, self.full = S, shard, full
        self.send, self.recv, self.local = send, recv, local
        self.swap_send, self.swap_recv = swap_send, swap_recv
        self.R, self.N = shard.shape
        self.s, self.c = lax.axis_index("seq"), lax.axis_index("ctx")
        self.cols = span(lax.rem(self.c, 2) * (self.N // 2), self.N // 2)
        self.orders = bit_orders(S)
        self.steps = len(self.orders[0])
        self.half = self.R // 2

    def block(self, owner, p):
        return self.full.at[span(owner * self.R + p * self.half, self.half, 16), self.cols]

    def copy_own(self):
        return pltpu.make_async_copy(
            self.shard, self.full.at[span(self.s * self.R, self.R, 16), :], self.local
        )

    def copies(self, t, direct):
        out = []
        for p in range(2):
            order = self.orders[p]
            for i, mask in enumerate(subsets(order[:t])):
                if (mask == 0) == direct:
                    owner = jnp.bitwise_xor(self.s, mask)
                    src = self.block(owner, p)
                    if mask == 0:
                        src = self.shard.at[pl.ds(p * self.half, self.half), self.cols]
                    k = (1 << t) - 1 + i
                    peer = jnp.bitwise_xor(self.s, order[t])
                    out.append(remote(src, self.block(owner, p), self.send.at[p, k], self.recv.at[p, k], seq=peer))
        return out

    def swaps(self, t, direct):
        out = []
        for p in range(2):
            order = self.orders[p]
            for i, mask in enumerate(subsets(order[:t])):
                if (mask == 0) == direct:
                    got = self.block(jnp.bitwise_xor(self.s, order[t] ^ mask), p)
                    k = (1 << t) - 1 + i
                    out.append(
                        remote(
                            got, got, self.swap_send.at[p, k], self.swap_recv.at[p, k], ctx=jnp.bitwise_xor(self.c, 1)
                        )
                    )
        return out

    def start(self):
        for t in range(self.steps):
            for copy in self.copies(t, True):
                copy.start()
        self.copy_own().start()

    def pass_on(self, t):
        for copy in self.copies(t, False):
            copy.start()

    def arrive(self, t, direct):
        for copy in self.copies(t, direct):
            copy.wait_recv()
        for copy in self.swaps(t, direct):
            copy.start()

    def first(self):
        self.arrive(0, True)
        self.pass_on(1)

    def middle(self):
        for t in range(1, self.steps):
            self.arrive(t, True)
            if t + 1 < self.steps:
                self.arrive(t, False)
                self.pass_on(t + 1)

    def last(self):
        self.arrive(self.steps - 1, False)

    def ready(self, early, late):
        if early:
            self.copy_own().wait()
        for t in range(self.steps):
            for direct in (True, False):
                final = t == self.steps - 1 and not direct
                if late if final else early:
                    for copy in self.swaps(t, direct):
                        copy.wait_recv()

    def drain(self):
        for t in range(self.steps):
            for direct in (True, False):
                for copy in self.copies(t, direct) + self.swaps(t, direct):
                    copy.wait_send()


class Regroup:
    def __init__(self, src, dst, send, recv, local, C, G):
        self.src, self.dst, self.send, self.recv, self.local = src, dst, send, recv, local
        self.G, self.M = G, C // G
        self.c = lax.axis_index("ctx")

    def dst_at(self, j):
        if len(self.dst.shape) == 2:
            rows = self.src.shape[1]
            return self.dst.at[tile(j, rows), :]
        return self.dst.at[j]

    def each(self, on_remote, on_local):
        place = lax.rem(self.c, self.G)
        for g in range(self.G):
            target = g * self.M + lax.div(self.c, self.G)
            far = remote(
                self.src.at[g], self.dst_at(place), self.send.at[g], self.recv.at[place], ctx=target
            )
            near = pltpu.make_async_copy(self.src.at[g], self.dst_at(place), self.local)

            @pl.when(target != self.c)
            def _():
                on_remote(far)

            @pl.when(target == self.c)
            def _():
                on_local(near)

    def start(self):
        self.each(lambda far: far.start(), lambda near: near.start())

    def drain(self):
        self.each(lambda far: far.wait_send(), lambda near: None)

    def finish(self):
        m = lax.rem(self.c, self.M)
        for j in range(self.G):
            source = m * self.G + j

            @pl.when(source != self.c)
            def _():
                remote(
                    self.src.at[0], self.dst_at(j), self.send.at[0], self.recv.at[j], ctx=source
                ).wait_recv()

            @pl.when(source == self.c)
            def _():
                pltpu.make_async_copy(self.src.at[0], self.dst_at(j), self.local).wait()


class Ungroup:
    def __init__(self, src, dst, send, recv, local, C, G):
        self.src, self.dst, self.send, self.recv, self.local = src, dst, send, recv, local
        self.G, self.M, self.P = G, C // G, dst.shape[1]
        self.c = lax.axis_index("ctx")

    def each(self, on_remote, on_local, only=None):
        g, m = lax.div(self.c, self.M), lax.rem(self.c, self.M)
        for j in range(self.G) if only is None else (only,):
            target = m * self.G + j
            rows = self.src.at[pl.ds(j * self.P, self.P), :]
            far = remote(rows, self.dst.at[g], self.send.at[j], self.recv.at[g], ctx=target)
            near = pltpu.make_async_copy(rows, self.dst.at[g], self.local)

            @pl.when(target != self.c)
            def _():
                on_remote(far)

            @pl.when(target == self.c)
            def _():
                on_local(near)

    def start(self, only=None):
        self.each(lambda far: far.start(), lambda near: near.start(), only)

    def drain(self):
        self.each(lambda far: far.wait_send(), lambda near: None)

    def finish(self):
        rows = self.src.at[pl.ds(0, self.P), :]
        for g in range(self.G):
            source = g * self.M + lax.div(self.c, self.G)

            @pl.when(source != self.c)
            def _():
                remote(
                    rows, self.dst.at[g], self.send.at[0], self.recv.at[g], ctx=source
                ).wait_recv()

            @pl.when(source == self.c)
            def _():
                pltpu.make_async_copy(rows, self.dst.at[g], self.local).wait()


def mask_bias(seg_keys, seg_queries, bias, G, PP):
    rows = [seg_queries[i].astype(f32) for i in range(G)]
    for a in range(G):
        column = jnp.broadcast_to(seg_keys[a].astype(f32), (PP, PP)).T
        for b in range(G):
            bias[a * PP : (a + 1) * PP, b * PP : (b + 1) * PP] = jnp.where(
                column == rows[b], jnp.zeros((PP, PP), f32), jnp.full((PP, PP), NEG, f32)
            ).astype(bias.dtype)


def norm_rows(x):
    centred = x - jnp.mean(x, axis=-1, keepdims=True)
    factor = lax.rsqrt(jnp.mean(centred * centred, axis=-1, keepdims=True) + EPS)
    return centred * factor, factor


def norm_back(g, gain, normed, factor):
    h = g * gain
    return factor * (
        h
        - jnp.mean(h, axis=-1, keepdims=True)
        - normed * jnp.mean(h * normed, axis=-1, keepdims=True)
    )


def loop(n, body):
    def step(i, carry):
        body(i)
        return carry

    lax.fori_loop(0, n, step, 0)


def colsum(x):
    return jnp.sum(x, axis=0, keepdims=True)


def forward_kernel(
    dims,
    hid, cot, seg, wq_s, wo_s, wi_s, wu_s, qb, vb, ob, fg, fs, ub, sg, ss, ib,
    xs_o, wq_o, wo_o, wi_o, wu_o, k_o, v_o, q_o, seg_o, p_o, fac_o, ctxt_o, ctx_o,
    n1_o, f1_o, flow_o, act_o, dgel_o, gsec_o, gb_o, out_o, smg_o, sm_o,
    xs, ct, wq, wo, wi, wu, small_all, segc, segk, q, qt, kown, vown, kc, vc, bias, pst, m_s, l_s, ctxt, ctx,
    first, n1, f1, flow, h, act, dgel, n2, gsec, gb, outv,
    ag_send, ag_recv, sw_send, sw_recv, ag_local, rg_send, rg_recv, rg_local, sm_send, sm_recv,
    kv_send, kv_recv, kv_local, kc_sem, p_sem, out_sem,
):
    S, C, G, PP = dims
    M, L, D = C // G, G * PP, hid.shape[2]
    FF = wi.shape[1]
    NP = D // 128
    T = 256
    s, c = lax.axis_index("seq"), lax.axis_index("ctx")
    m = lax.rem(c, M)

    gathers = [
        Gather(S, shard, full, *[a.at[w] for a in (ag_send, ag_recv, sw_send, sw_recv, ag_local)])
        for w, (shard, full) in enumerate(((wq_s, wq), (wo_s, wo), (wi_s, wi), (wu_s, wu)))
    ]
    gq, go, gi, gu = gathers
    pending = []

    def put(src, dst):
        copy = pltpu.make_async_copy(src, dst, out_sem.at[len(pending)])
        copy.start()
        pending.append(copy)

    enter(S, C)
    hid_move = Regroup(hid, xs, rg_send.at[0], rg_recv.at[0], rg_local.at[0], C, G)
    cot_move = Regroup(cot, ct, rg_send.at[1], rg_recv.at[1], rg_local.at[1], C, G)
    seg_move = Regroup(seg, segc, rg_send.at[2], rg_recv.at[2], rg_local.at[2], C, G)
    seg_move.start()
    hid_move.start()
    gq.start()
    width, share = D // S, FF // S
    small = small_all.at[s]
    small[...] = jnp.zeros(small.shape, bf16)
    for r, vector in enumerate((qb, vb, ob, fg, fs, ub, sg, ss)):
        small[r : r + 1, 0:width] = vector[...].reshape(1, width)
    for r in range(share // width):
        small[IB + r : IB + r + 1, 0:width] = ib[r * width : (r + 1) * width].reshape(1, width)
    small_copies = [
        remote(small, small, sm_send.at[d - 1], sm_recv.at[s], seq=jnp.bitwise_xor(s, d))
        for d in range(1, S)
    ]
    for copy in small_copies:
        copy.start()
    seg_move.finish()

    group = lax.div(c, M) * M
    seg_own = pltpu.make_async_copy(segc, seg_o.at[m], kv_local.at[2])
    seg_own.start()

    def peer(d):
        return group + lax.rem(m + d, M)

    def kv_copies(d):
        return [
            remote(src, dst.at[m], kv_send.at[i, d], kv_recv.at[i, m], ctx=peer(d))
            for i, (src, dst) in enumerate(((kown, k_o), (vown, v_o), (segc, seg_o)))
        ]

    def kv_arrivals(d):
        j = lax.rem(m + d, M)
        return [
            remote(src, dst.at[j], kv_send.at[i, d], kv_recv.at[i, j], ctx=peer(d))
            for i, (src, dst) in enumerate(((kown, k_o), (vown, v_o), (segc, seg_o)))
        ]

    for d in range(1, M):
        kv_copies(d)[2].start()

    for d in range(1, S):
        far = jnp.bitwise_xor(s, d)
        remote(small, small_all.at[far], sm_send.at[d - 1], sm_recv.at[far], seq=far).wait_recv()
    sm_o[...] = jnp.zeros(sm_o.shape, f32)
    for owner in range(S):
        block = small_all[owner].astype(f32)
        sm_o[0:IB, owner * width : (owner + 1) * width] = block[0:IB, 0:width]
        for r in range(share // width):
            start = owner * share + r * width
            a, b = start // D, start % D
            sm_o[IB + a : IB + a + 1, b : b + width] = block[IB + r : IB + r + 1, 0:width]
    mask_bias(segc, segc, bias, G, PP)
    gq.first()
    go.start()
    gi.start()
    gq.middle()
    gq.last()
    hid_move.finish()
    cot_move.start()
    put(xs, xs_o)
    gq.ready(True, True)
    put(wq, wq_o)

    def project(i):
        cols = tile(i, T)
        qv = dotf(xs[...], wq[:, cols]) + sm_o[QB : QB + 1, cols]
        kv = dotf(xs[...], wq[:, span(D + i * T, T)])
        vv = dotf(xs[...], wq[:, span(2 * D + i * T, T)]) + sm_o[VB : VB + 1, cols]
        qs = (qv.astype(bf16).astype(f32) * HEAD_DIM**-0.5).astype(bf16)
        kv, vv = kv.astype(bf16), vv.astype(bf16)
        for u in range(T // 128):
            lanes = slice(u * 128, (u + 1) * 128)
            hp = i * (T // 128) + u
            q[hp] = qs[:, lanes]
            qt[hp] = qs[:, lanes].T
            kown[hp] = kv[:, lanes]
            vown[hp] = vv[:, lanes]

    loop(D // T, project)
    for d in range(1, M):
        for copy in kv_copies(d)[:2]:
            copy.start()
    own_kv = [
        pltpu.make_async_copy(kown, k_o.at[m], kv_local.at[0]),
        pltpu.make_async_copy(vown, v_o.at[m], kv_local.at[1]),
    ]
    for copy in own_kv:
        copy.start()
    put(q, q_o)
    go.first()
    gi.first()
    gu.start()

    row_of = lax.broadcasted_iota(jnp.int32, (128, L), 0)

    def keep_probs(hp, d):
        slot = lax.rem(hp, 2)
        return pltpu.make_async_copy(pst.at[slot], p_o.at[hp, d], p_sem.at[slot])

    def attend(keys, values, d, extra):
        fresh = isinstance(d, int)

        def pair(hp):
            extra(hp)
            slot = lax.rem(hp, 2)
            if fresh:

                @pl.when(hp >= 2)
                def _():
                    keep_probs(hp, d).wait()

            else:
                keep_probs(hp, d).wait()
            qv, kv, vt, b = qt[hp], keys[hp], values[hp].T, bias[...]
            for e in range(2):
                head = slice(e * HEAD_DIM, (e + 1) * HEAD_DIM)
                mine = (row_of < HEAD_DIM) if e == 0 else (row_of >= HEAD_DIM)
                scores = dotf(kv, jnp.where(mine, qv, jnp.zeros_like(qv))) + b
                top = jnp.max(scores, axis=0, keepdims=True)
                if fresh:
                    weights = jnp.exp(scores - top)
                    low = weights.astype(bf16)
                    m_s[d, hp, e : e + 1, :] = top
                    l_s[hp, e : e + 1, :] = colsum(weights)
                    ctxt[hp, head, :] = dotf(vt[head], low)
                else:
                    old = m_s[d - 1, hp, e : e + 1, :]
                    top = jnp.maximum(old, top)
                    keep = jnp.exp(old - top)
                    weights = jnp.exp(scores - top)
                    low = weights.astype(bf16)
                    m_s[d, hp, e : e + 1, :] = top
                    l_s[hp, e : e + 1, :] = l_s[hp, e : e + 1, :] * keep + colsum(weights)
                    ctxt[hp, head, :] = ctxt[hp, head, :] * keep + dotf(vt[head], low)
                pst[slot, e] = low
            keep_probs(hp, d).start()

        loop(NP, pair)

    def in_own(hp):
        @pl.when(hp == NP - 2)
        def _():
            go.middle()
            go.last()

    attend(kown, vown, 0, in_own)

    def far_chunk(d, carry):
        j = lax.rem(m + d, M)
        for copy in kv_arrivals(d):
            copy.wait_recv()
        loads = [
            pltpu.make_async_copy(k_o.at[j], kc, kc_sem.at[0]),
            pltpu.make_async_copy(v_o.at[j], vc, kc_sem.at[1]),
            pltpu.make_async_copy(seg_o.at[j], segk, kc_sem.at[2]),
        ]
        for copy in loads:
            copy.start()
        for copy in loads:
            copy.wait()
        mask_bias(segk, segc, bias, G, PP)
        attend(kc, vc, d, lambda hp: None)
        return carry

    lax.fori_loop(1, M, far_chunk, 0)

    def close(hp):
        for e in range(2):
            head = slice(e * HEAD_DIM, (e + 1) * HEAD_DIM)
            share = 1.0 / l_s[hp, e : e + 1, :]
            ctxt[hp, head, :] = ctxt[hp, head, :] * share
            for d in range(M):
                fac_o[d, hp, e : e + 1, :] = jnp.exp(m_s[d, hp, e : e + 1, :] - m_s[M - 1, hp, e : e + 1, :]) * share
        ctx[:, tile(hp, 128)] = ctxt[hp].T.astype(bf16)

    loop(NP, close)

    put(ctxt, ctxt_o)
    put(ctx, ctx_o)
    gi.middle()
    gi.last()
    go.ready(True, True)
    put(wo, wo_o)

    def project_out(i):
        cols = tile(i, T)
        first[:, cols] = dotf(ctx[...], wo[:, cols]) + sm_o[OB : OB + 1, cols]

    loop(D // T, project_out)

    def first_norm(r):
        rows = tile(r, RB)
        normed, factor = norm_rows(first[rows, :] + xs[rows, :].astype(f32))
        y = normed * sm_o[FG : FG + 1, :] + sm_o[FS : FS + 1, :]
        n1[rows, :] = normed
        f1[rows, :] = factor
        first[rows, :] = y
        flow[rows, :] = y.astype(bf16)

    loop(L // RB, first_norm)
    put(n1, n1_o)
    put(f1, f1_o)
    put(flow, flow_o)
    gu.first()
    gi.ready(True, True)
    put(wi, wi_o)

    def feed_in(i):
        cols = tile(i, D)
        h[...] = dotf(flow[...], wi[:, cols]) + sm_o[pl.ds(IB + i, 1), :]

        def gelu(k):
            rows, lanes = tile(lax.div(k, D // T), RB), lax.rem(k, D // T) * T
            x = h[rows, span(lanes, T)]
            share = 0.5 * (1.0 + lax.erf(x * ROOT_HALF))
            act[rows, span(i * D + lanes, T)] = (x * share).astype(bf16)
            dgel[rows, span(i * D + lanes, T)] = (
                share + x * (PDF_SCALE * jnp.exp(-0.5 * x * x))
            ).astype(bf16)

        loop(L // RB * (D // T), gelu)

    loop(FF // D, feed_in)
    put(act, act_o)
    put(dgel, dgel_o)
    RU = FF // S

    def feed_out(masks, fresh):
        owners = [jnp.bitwise_xor(s, k) for k in masks]

        def step(i):
            cols = tile(i, T)
            total = sm_o[UB : UB + 1, cols] if fresh else n2[:, cols]
            for owner in owners:
                total = total + dotf(act[:, span(owner * RU, RU)], wu[span(owner * RU, RU), cols])
            n2[:, cols] = total

        loop(D // T, step)

    gu.middle()
    gu.ready(True, False)
    feed_out([k for k in range(S) if k & (k - 1) == 0], True)
    gu.last()
    gu.ready(False, True)
    put(wu, wu_o)
    feed_out([k for k in range(S) if k & (k - 1)], False)
    cot_move.finish()
    smg_o[...] = jnp.zeros(smg_o.shape, f32)

    def second_norm(r):
        rows = tile(r, RB)
        normed, factor = norm_rows(first[rows, :] + n2[rows, :])
        gain = sm_o[SG : SG + 1, :]
        outv[rows, :] = (normed * gain + sm_o[SS : SS + 1, :]).astype(bf16)
        g = ct[rows, :].astype(f32)
        smg_o[SG : SG + 1, :] += colsum(g * normed)
        smg_o[SS : SS + 1, :] += colsum(g)
        back = norm_back(g, gain, normed, factor)
        gsec[rows, :] = back
        low = back.astype(bf16)
        gb[rows, :] = low
        smg_o[UB : UB + 1, :] += colsum(low.astype(f32))

    loop(L // RB, second_norm)
    put(outv, out_o)
    put(gsec, gsec_o)
    put(gb, gb_o)

    for u in range(2):
        keep_probs(NP - 2 + u, 0).wait()
    for gather in gathers:
        gather.drain()
    for move in (hid_move, cot_move, seg_move):
        move.drain()
    for copy in small_copies:
        copy.wait_send()
    for d in range(1, M):
        for copy in kv_copies(d):
            copy.wait_send()
    for copy in own_kv + [seg_own] + pending:
        copy.wait()


def forward_call(S, C, hid, cot, seg, wq_s, wo_s, wi_s, wu_s, vectors):
    G, PP, D = hid.shape
    L, M, NP, FF = G * PP, C // G, D // 128, wi_s.shape[1]
    sds = jax.ShapeDtypeStruct
    outs = [
        ((L, D), bf16), ((D, 3 * D), bf16), ((D, D), bf16), ((D, FF), bf16), ((FF, D), bf16),
        ((M, NP, L, 128), bf16), ((M, NP, L, 128), bf16), ((NP, L, 128), bf16),
        ((M, G, 1, PP), jnp.int32), ((NP, M, 2, L, L), bf16), None, ((NP, 128, L), f32), ((L, D), bf16),
        ((L, D), f32), ((L, 1), f32), ((L, D), bf16), ((L, FF), bf16), ((L, FF), bf16),
        ((L, D), f32), ((L, D), bf16), ((L, D), bf16),
    ]
    scratch = [
        ((L, D), bf16), ((L, D), bf16), ((D, 3 * D), bf16), ((D, D), bf16), ((D, FF), bf16), ((FF, D), bf16),
        ((S, 16, D // S + -(D // S) % 128), bf16), ((G, 1, PP), jnp.int32), ((G, 1, PP), jnp.int32),
        ((NP, L, 128), bf16), ((NP, 128, L), bf16), ((NP, L, 128), bf16), ((NP, L, 128), bf16),
        ((NP, L, 128), bf16), ((NP, L, 128), bf16), ((L, L), f32), ((2, 2, L, L), bf16), ((M, NP, 2, L), f32), ((NP, 2, L), f32),
        ((NP, 128, L), f32), ((L, D), bf16),
        ((L, D), f32), ((L, D), f32), ((L, 1), f32), ((L, D), bf16), ((L, D), f32), ((L, FF), bf16),
        ((L, FF), bf16), ((L, D), f32), ((L, D), f32), ((L, D), bf16), ((L, D), bf16),
    ]
    dma = pltpu.SemaphoreType.DMA
    sems = [
        dma((4, 2, S)), dma((4, 2, S)), dma((4, 2, S)), dma((4, 2, S)), dma((4,)), dma((3, G)), dma((3, G)), dma((3,)),
        dma((S,)), dma((S,)), dma((3, M)), dma((3, M)), dma((3,)), dma((3,)), dma((2,)), dma((24,)),
    ]
    return pl.pallas_call(
        functools.partial(forward_kernel, (S, C, G, PP)),
        out_shape=[sds(*(o or ((M, NP, 2, L), f32))) for o in outs] + [sds((16, D), f32), sds((16, D), f32)],
        in_specs=[ANY] * 7 + [VMEM] * len(vectors),
        out_specs=[ANY if o else VMEM for o in outs] + [VMEM, VMEM],
        scratch_shapes=[pltpu.VMEM(*x) for x in scratch] + sems,
        compiler_params=pltpu.CompilerParams(
            collective_id=0, has_side_effects=True, vmem_limit_bytes=62 << 20
        ),
        name="forward",
    )(hid, cot, seg, wq_s, wo_s, wi_s, wu_s, *vectors)


def widen_kernel(count, *refs):
    srcs, dsts = refs[: count + 1], refs[count + 1 : 2 * count + 2]
    lows, highs = refs[2 * count + 2 : 3 * count + 2], refs[3 * count + 2 : 4 * count + 2]
    plain, in_sem, out_sem = refs[4 * count + 2 :]
    loads, stores = [], []
    for i in range(count):
        loads.append(pltpu.make_async_copy(srcs[i], lows[i], in_sem.at[i]))
        stores.append(pltpu.make_async_copy(highs[i], dsts[i], out_sem.at[i]))
    loads.append(pltpu.make_async_copy(srcs[count], plain, in_sem.at[count]))
    stores.append(pltpu.make_async_copy(plain, dsts[count], out_sem.at[count]))
    for copy in loads:
        copy.start()
    for i in range(count):
        loads[i].wait()
        rows = lows[i].shape[0]
        unit = next(u for u in (64, 48, 32, 16) if rows % u == 0)

        def step(r, low=lows[i], high=highs[i], unit=unit):
            at = tile(r, unit)
            high[at, :] = low[at, :].astype(f32)

        loop(rows // unit, step)
        stores[i].start()
    loads[count].wait()
    stores[count].start()
    for copy in stores:
        copy.wait()


def widen(arrays, plain):
    count = len(arrays)
    sds = jax.ShapeDtypeStruct
    return pl.pallas_call(
        functools.partial(widen_kernel, count),
        out_shape=[sds(a.shape, f32) for a in arrays] + [sds(plain.shape, plain.dtype)],
        in_specs=[ANY] * (count + 1),
        out_specs=[ANY] * (count + 1),
        scratch_shapes=[pltpu.VMEM(a.shape, bf16) for a in arrays]
        + [pltpu.VMEM(a.shape, f32) for a in arrays]
        + [pltpu.VMEM(plain.shape, plain.dtype), pltpu.SemaphoreType.DMA((count + 1,)), pltpu.SemaphoreType.DMA((count + 1,))],
        compiler_params=pltpu.CompilerParams(vmem_limit_bytes=62 << 20),
        name="widen",
    )(*arrays, plain)


def add_rows(dst, src):
    rows = dst.shape[0]
    unit = next(u for u in (96, 48, 16) if rows % u == 0)

    def step(r):
        at = tile(r, unit)
        dst[at, :] = dst[at, :] + src[at, :]

    loop(rows // unit, step)


class CoreSwap:
    def __init__(self, part, far, rows, send, recv):
        self.part, self.far, self.rows, self.send, self.recv = part, far, rows, send, recv
        self.c = lax.axis_index("ctx")
        self.core = lax.rem(self.c, 2)
        self.count = part.shape[1] // rows

    def copy(self, i):
        rows = tile(i, self.rows)
        return remote(
            self.part.at[1 - self.core, rows, :], self.far.at[rows, :], self.send.at[i], self.recv.at[i],
            ctx=jnp.bitwise_xor(self.c, 1),
        )

    def start(self, i):
        self.copy(i).start()

    def add(self):
        loop(self.count, lambda i: self.copy(i).wait_recv())
        add_rows(self.part.at[self.core], self.far)

    def drain(self):
        loop(self.count, lambda i: self.copy(i).wait_send())


class Reduce:
    def __init__(self, S, C, part, stride, offset, R, cols, rx, zl, zr, sems, places):
        self.S, self.K, self.part, self.rx, self.zl, self.zr = S, C // 2, part, rx, zl, zr
        self.c_send, self.c_recv, self.x_send, self.x_recv, self.z_send, self.z_recv, self.l_send = sems
        self.places, self.stride, self.offset, self.R, self.cols = places, stride, offset, R, cols
        self.half = R // 2
        self.s, self.c = lax.axis_index("seq"), lax.axis_index("ctx")
        self.core = lax.rem(self.c, 2)
        self.k = lax.div(self.c, 2)
        self.left, self.right = self.K // 2 - 1, self.K // 2
        self.orders = bit_orders(S)
        self.steps = len(self.orders[0])

    def rows(self, owner, start, count):
        return self.part.at[self.core, span(owner * self.stride + self.offset + start, count, 16), self.cols]

    def block(self, owner, p):
        return self.rows(owner, p * self.half, self.half)

    def result(self):
        return self.rows(self.s, 0, self.R)

    def copies(self, t):
        out, base = [], self.S - (1 << (self.steps - t))
        for p in range(2):
            order = self.orders[p]
            peer = jnp.bitwise_xor(self.s, order[t])
            for i, mask in reversed(list(enumerate(subsets(order[t + 1 :])))):
                copy = remote(
                    self.block(jnp.bitwise_xor(peer, mask), p),
                    self.rx.at[p, base + i],
                    self.x_send.at[p, base + i],
                    self.x_recv.at[p, base + i],
                    seq=peer,
                )
                out.append((copy, p, base + i, mask))
        return out

    def cross_start(self, t):
        if t > 0:
            self.cross_add(t - 1, False)
        for copy, _, _, _ in self.copies(t):
            copy.start()

    def cross_add(self, t, last):
        for copy, p, slot, mask in self.copies(t):
            if (mask == 0) == last:
                copy.wait_recv()
                add_rows(self.block(jnp.bitwise_xor(self.s, mask), p), self.rx.at[p, slot])

    def from_left(self):
        return remote(self.result(), self.zl, self.z_send.at[0], self.z_recv.at[0], ctx=self.c + 2)

    def from_right(self):
        return remote(self.result(), self.zr, self.z_send.at[0], self.z_recv.at[1], ctx=self.c - 2)

    def out_left(self):
        return remote(self.zr, self.zr, self.z_send.at[1], self.z_recv.at[1], ctx=self.c - 2)

    def out_right(self):
        return remote(self.zl, self.zl, self.z_send.at[1], self.z_recv.at[0], ctx=self.c + 2)

    def inward(self, level):
        if level == 0:
            for t in range(self.steps):
                self.cross_add(t, True)

        @pl.when(self.k == level)
        def _():
            if level > 0:
                self.from_left().wait_recv()
                add_rows(self.result(), self.zl)
            self.from_left().start()

        @pl.when(self.k == self.K - 1 - level)
        def _():
            if level > 0:
                self.from_right().wait_recv()
                add_rows(self.result(), self.zr)
            self.from_right().start()

    def outward(self, distance):
        @pl.when(self.k == self.left - distance)
        def _():
            self.from_right().wait_recv()
            if distance == 0:
                add_rows(self.zr, self.result())
            if distance < self.left:
                self.out_left().start()
            self.deliver(self.zr)

        @pl.when(self.k == self.right + distance)
        def _():
            self.from_left().wait_recv()
            if distance == 0:
                add_rows(self.zl, self.result())
            if distance < self.left:
                self.out_right().start()
            self.deliver(self.zl)

    def deliveries(self, src):
        out = []
        for i, (cols, place) in enumerate(self.places):
            dst = place(self.core)
            out.append(
                (
                    pltpu.make_async_copy(src.at[:, cols], dst, self.l_send.at[i]),
                    remote(
                        src.at[:, cols], dst, self.c_send.at[i], self.c_recv.at[i], ctx=jnp.bitwise_xor(self.c, 1)
                    ),
                )
            )
        return out

    def deliver(self, src):
        for near, far in self.deliveries(src):
            near.start()
            far.start()

    def finish(self):
        for near, far in self.deliveries(self.zl):
            near.wait()
            far.wait_recv()

    def stages(self):
        def each(step, *which):
            for w in which:
                step(w)

        run = functools.partial
        return [
            run(each, self.cross_start, 0),
            run(each, self.cross_start, *range(1, self.steps)),
            run(each, self.inward, 0),
            run(each, self.inward, *range(1, self.left + 1)),
            run(each, self.outward, 0),
            run(each, self.outward, *range(1, self.left + 1)),
        ]

    def drain(self):
        for t in range(self.steps):
            for copy, _, _, _ in self.copies(t):
                copy.wait_send()

        @pl.when(self.k <= self.left)
        def _():
            self.from_left().wait_send()

        @pl.when(self.k >= self.right)
        def _():
            self.from_right().wait_send()

        @pl.when(jnp.logical_and(self.k <= self.left, self.k > 0))
        def _():
            self.out_left().wait_send()

        @pl.when(jnp.logical_and(self.k >= self.right, self.k < self.K - 1))
        def _():
            self.out_right().wait_send()

        for _, far in self.deliveries(self.zl):
            far.wait_send()


class DirectReduce:
    def __init__(self, S, C, part, far, rx, zx, done, sems, places):
        self.S, self.K, self.part, self.far, self.rx, self.zx, self.done = S, C // 2, part, far, rx, zx, done
        self.h_send, self.h_recv, self.x_send, self.x_recv, self.z_send, self.z_recv, self.c_send, self.c_recv, self.l_send = sems
        self.places = places
        self.s, self.c = lax.axis_index("seq"), lax.axis_index("ctx")
        self.core = lax.rem(self.c, 2)
        self.k = lax.div(self.c, 2)

    def other(self):
        return jnp.bitwise_xor(self.c, 1)

    def halves(self):
        return remote(
            self.part.at[:, 1 - self.core], self.far, self.h_send.at[0], self.h_recv.at[0], ctx=self.other()
        )

    def start(self):
        self.halves().start()

    def crossing(self):
        out = []
        for d in range(self.S - 1, 0, -1):
            peer = jnp.bitwise_xor(self.s, d)
            out.append(
                remote(
                    self.part.at[peer, self.core], self.rx.at[d - 1], self.x_send.at[d - 1], self.x_recv.at[d - 1],
                    seq=peer,
                )
            )
        return out

    def cross_start(self):
        self.halves().wait_recv()
        for owner in range(self.S):
            add_rows(self.part.at[owner, self.core], self.far.at[owner])
        for copy in self.crossing():
            copy.start()

    def along(self, d):
        chip = lax.rem(self.k + d, self.K)
        return remote(
            self.part.at[self.s, self.core], self.zx.at[self.k], self.z_send.at[d - 1], self.z_recv.at[self.k],
            ctx=2 * chip + self.core,
        )

    def arrival(self, d):
        chip = lax.rem(self.k + d, self.K)
        return remote(
            self.part.at[self.s, self.core], self.zx.at[chip], self.z_send.at[d - 1], self.z_recv.at[chip],
            ctx=2 * chip + self.core,
        )

    def along_start(self):
        mine = self.part.at[self.s, self.core]
        for copy in self.crossing():
            copy.wait_recv()
        total = mine[...].astype(f32)
        for d in range(1, self.S):
            total = total + self.rx[d - 1].astype(f32)
        total = total.astype(bf16)
        mine[...] = total
        self.zx[self.k] = total
        for d in range(self.K - 1, 0, -1):
            self.along(d).start()

    def outputs(self):
        out = []
        for i, (cols, place) in enumerate(self.places):
            dst = place(self.core)
            src = self.done.at[:, cols]
            out.append(
                (
                    pltpu.make_async_copy(src, dst, self.l_send.at[i]),
                    remote(src, dst, self.c_send.at[i], self.c_recv.at[i], ctx=self.other()),
                )
            )
        return out

    def deliver(self):
        for d in range(1, self.K):
            self.arrival(d).wait_recv()
        total = self.zx[0].astype(f32)
        for j in range(1, self.K):
            total = total + self.zx[j].astype(f32)
        self.done[...] = total.astype(bf16)
        for near, far in self.outputs():
            near.start()
            far.start()

    def stages(self):
        return [self.cross_start, self.along_start, self.deliver]

    def finish(self):
        for near, far in self.outputs():
            near.wait()
            far.wait_recv()

    def drain(self):
        self.halves().wait_send()
        for copy in self.crossing():
            copy.wait_send()
        for d in range(1, self.K):
            self.along(d).wait_send()
        for _, far in self.outputs():
            far.wait_send()


SCHEDULE = {
    "ffn0": (('u0', 1),),
    "ffn1": (('u1', 1),),
    "ffn2": (('u0', 2),),
    "ffn3": (('u2', 1), ('u1', 2)),
    "first": (('i0', 1),),
    "norm": (('u0', 3),),
    "context": (('u2', 2),),
    "pair0": (('u0', 4), ('u1', 3), ('i0', 2), ('i1', 1), ('i2', 1)),
    "pair1": (('u2', 3),),
    "project0": (('i0', 3), ('i3', 1), ('i1', 2)),
    "input0": (('u1', 4), ('u0', 5)),
    "far2": (('i2', 2),),
    "pair2": (('u2', 4),),
    "far3": (('i3', 2),),
    "pair3": (('i0', 4), ('i1', 3), ('u0', 6), ('u1', 5), ('o', 1)),
    "project1": (('i2', 3), ('q0', 1)),
    "input1": (('i3', 3), ('u2', 5)),
    "far4": (('o', 2),),
    "pair4": (('i1', 4), ('u1', 6), ('q0', 2), ('i0', 5), ('q1', 1)),
    "far5": (('i2', 4),),
    "pair5": (('o', 3), ('i3', 4), ('u2', 6), ('q0', 3)),
    "project2": (('q1', 2), ('i1', 5)),
    "input2": (('i0', 6), ('q2', 1)),
    "end": (('i2', 5), ('s', 1), ('g0', 1), ('o', 4), ('q1', 3), ('i3', 5), ('q2', 2), ('i1', 6), ('q0', 4), ('s', 2), ('i2', 6), ('q2', 3), ('o', 5), ('q1', 4), ('i3', 6), ('q0', 5), ('s', 3), ('q2', 4), ('o', 6), ('q1', 5), ('g1', 1), ('q0', 6), ('q2', 5), ('g2', 1), ('q1', 6), ('g3', 1), ('q2', 6)),
}


def backward_kernel(
    dims,
    outv, gsec_i, gb_i, act_i, dgel_i, wu_i, wi_i, wo_i, wq_i, flow_i, n1_i, f1_i, xs_i, ctx_i, ctxt_i,
    q_i, k_i, v_i, p_i, fac, smg_i, sm,
    out_o, gin_o, gq_o, go_o, gi_o, gu_o, land_o, small_o,
    pu, pi, po, pq, ps, fu, fi, fo, fq, fs, rxu, rxi, rxs, zlu, zli, zru, zri, zxs, dns,
    gsec, gb, grad_o, grad_ot, delta, smg,
    cs_send, cs_recv, h_send, h_recv, dx_send, dx_recv, dz_send, dz_recv, c_send, c_recv, x_send, x_recv, z_send, z_recv, rg_send, rg_recv, rg_local, in_sem, wq_sem, kv_sem, p_sem, dkv_send, dkv_recv,
    land_sem, l_send,
):
    S, C, G, PP = dims
    M, L, D = C // G, G * PP, gsec.shape[1]
    FF = act_i.shape[1]
    NP = D // 128
    T = 256
    s, c = lax.axis_index("seq"), lax.axis_index("ctx")
    m, core = lax.rem(c, M), lax.rem(c, 2)
    group = lax.div(c, M) * M

    H = D // 2
    R, RU = D // S, FF // S
    cut = RU // 3
    items = {}

    def piece(name, places, *refs):
        n = len(items)
        sems = [a.at[n] for a in (c_send, c_recv, x_send, x_recv, z_send, z_recv, l_send)]
        items[name] = Reduce(S, C, *refs, sems, places)

    for i in range(3):
        piece(
            f"u{i}", [(pl.ds(0, H), lambda e, i=i: gu_o.at[pl.ds(i * cut, cut), span(e * H, H)])],
            pu, RU, i * cut, cut, pl.ds(0, H), rxu.at[i], zlu.at[i], zru.at[i],
        )

    def narrow_piece(name, places, part, cols):
        n = len(items) - 3
        piece(name, places, part, R, 0, R, cols, rxi.at[n], zli.at[n], zri.at[n])

    for i in range(2):
        for j in range(2):
            narrow_piece(
                f"i{2 * i + j}",
                [(pl.ds(0, H), lambda e, i=i, j=j: gi_o.at[:, span(e * (FF // 2) + i * D + j * H, H)])],
                pi.at[i], pl.ds(j * H, H),
            )
    narrow_piece("o", [(pl.ds(0, H), lambda e: go_o.at[:, span(e * H, H)])], po, pl.ds(0, H))
    for i in range(3):
        narrow_piece(
            f"q{i}",
            [
                (pl.ds(a * 128, 128), lambda e, i=i, a=a: gq_o.at[:, span(a * D + (2 * i + e) * 128, 128)])
                for a in range(3)
            ],
            pq.at[i], pl.ds(0, H),
        )
    def direct_piece(name, n, places, *refs):
        m_ = len(items)
        sems = [a.at[n] for a in (h_send, h_recv, dx_send, dx_recv, dz_send, dz_recv)]
        items[name] = DirectReduce(S, C, *refs, sems + [a.at[m_] for a in (c_send, c_recv, l_send)], places)

    SW = ps.shape[3]
    direct_piece("s", 0, [(pl.ds(0, SW), lambda e: small_o.at[e])], ps, fs, rxs, zxs, dns)
    swap_u = CoreSwap(pu, fu, 512, cs_send.at[0], cs_recv.at[0])
    swap_i = [CoreSwap(pi.at[i], fi.at[i], T, cs_send.at[1 + i], cs_recv.at[1 + i]) for i in range(2)]
    swap_o = CoreSwap(po, fo, T, cs_send.at[3], cs_recv.at[3])
    swap_q = [CoreSwap(pq.at[i], fq.at[i], T, cs_send.at[4 + i], cs_recv.at[4 + i]) for i in range(3)]

    ticks = {name: item.stages() for name, item in items.items()}
    ran = set()

    def point(name):
        for step in SCHEDULE.get(name, ()):
            ran.add(step)
            ticks[step[0]][step[1] - 1]()

    enter(S, C)
    out_move = Ungroup(outv, out_o, rg_send.at[0], rg_recv.at[0], rg_local.at[0], C, G)
    out_move.start()
    smg[...] = smg_i[...]

    def feed_forward(act, dgel, wu, wi, h, n1, f1, flow):
        loads = [
            pltpu.make_async_copy(src, dst, in_sem.at[i])
            for i, (src, dst) in enumerate(
                ((gb_i, gb), (act_i, act), (wu_i, wu), (dgel_i, dgel), (flow_i, flow), (wi_i, wi), (gsec_i, gsec),
                 (n1_i, n1), (f1_i, f1))
            )
        ]
        for copy in loads:
            copy.start()
        loads[0].wait()
        loads[1].wait()

        def outer_grad(i):
            rows = tile(i, 512)
            block = dotg(act[:, rows], gb[...], 0, 0).astype(bf16)
            for e in range(2):
                pu[e, rows, :] = block[:, e * (D // 2) : (e + 1) * (D // 2)]
            swap_u.start(i)

        loop(FF // 512, outer_grad)
        for copy in loads[2:5]:
            copy.wait()

        def inner_grad(i, half, send):
            where = half * (FF // 2) + i * D
            cols = span(where, D)
            h[...] = dotg(gb[...], wu[span(where, D), :], 1, 1)

            def through(k, sums):
                rows = tile(k, RB)
                low = (h[rows, :] * dgel[rows, cols].astype(f32)).astype(bf16)
                act[rows, cols] = low
                return sums + colsum(low.astype(f32))

            sums = lax.fori_loop(0, L // RB, through, jnp.zeros((1, D), f32))
            smg[pl.ds(IB + half * (FF // 2 // D) + i, 1), :] = sums

            def grad(k):
                rows = tile(k, T)
                pi[i, half, rows, :] = dotg(flow[:, rows], act[:, cols], 0, 0).astype(bf16)
                if send:
                    swap_i[i].start(k)

            loop(D // T, grad)

        inner_grad(0, 1 - core, True)
        swap_u.add()
        point("ffn0")
        inner_grad(0, core, False)
        point("ffn1")
        inner_grad(1, 1 - core, True)
        swap_i[0].add()
        point("ffn2")
        inner_grad(1, core, False)
        swap_i[1].add()
        point("ffn3")
        loads[5].wait()
        loads[6].wait()

        def first_grad(i):
            cols = tile(i, T)
            gsec[:, cols] += dotg(act[...], wi[cols, :], 1, 1)

        loop(D // T, first_grad)
        point("first")
        loads[7].wait()
        loads[8].wait()

        def first_back(k):
            rows = tile(k, RB)
            g, normed = gsec[rows, :], n1[rows, :]
            smg[FG : FG + 1, :] += colsum(g * normed)
            smg[FS : FS + 1, :] += colsum(g)
            back = norm_back(g, sm[FG : FG + 1, :], normed, f1[rows, :])
            gsec[rows, :] = back
            low = back.astype(bf16)
            gb[rows, :] = low
            smg[OB : OB + 1, :] += colsum(low.astype(f32))

        loop(L // RB, first_back)

    V = pltpu.VMEM
    pl.run_scoped(
        feed_forward, V((L, FF), bf16), V((L, FF), bf16), V((FF, D), bf16), V((D, FF), bf16), V((L, D), f32),
        V((L, D), f32), V((L, 1), f32), V((L, D), bf16),
    )
    point("norm")

    def context_back(wo, ctx, ctxt):
        loads = [
            pltpu.make_async_copy(src, dst, in_sem.at[i])
            for i, (src, dst) in enumerate(((ctx_i, ctx), (wo_i, wo), (ctxt_i, ctxt)))
        ]
        for copy in loads:
            copy.start()
        loads[0].wait()

        def out_grad(k):
            rows = tile(k, T)
            block = dotg(ctx[:, rows], gb[...], 0, 0).astype(bf16)
            for e in range(2):
                po[e, rows, :] = block[:, e * (D // 2) : (e + 1) * (D // 2)]
            swap_o.start(k)

        loop(D // T, out_grad)
        loads[1].wait()
        loads[2].wait()

        def back(k):
            grad = dotg(gb[...], wo[tile(k, T), :], 1, 1).astype(bf16)
            for u in range(T // 128):
                hp = k * (T // 128) + u
                mine = grad[:, u * 128 : (u + 1) * 128]
                turned = mine.T
                grad_o[hp] = mine
                grad_ot[hp] = turned
                both = turned.astype(f32) * ctxt[hp]
                for e in range(2):
                    delta[hp, e : e + 1, :] = colsum(both[e * HEAD_DIM : (e + 1) * HEAD_DIM])

        loop(D // T, back)

    pl.run_scoped(context_back, V((D, D), bf16), V((L, D), bf16), V((NP, 128, L), f32))
    swap_o.add()
    point("context")

    def attention(wq, xs, q, kb, vb, pb, own_k, own_v, stage, land, grads, dqt, turned_q):
        loads = [
            pltpu.make_async_copy(src, dst, in_sem.at[i])
            for i, (src, dst) in enumerate(
                ((q_i, q), (xs_i, xs))
            )
        ]
        groups = [(0, 2), (2, 2), (4, 2)]

        def weight_cols(first, count):
            return [
                pltpu.make_async_copy(
                    wq_i.at[:, pl.ds(a * D + first * 128, count * 128)],
                    wq.at[:, pl.ds(3 * first * 128 + a * count * 128, count * 128)],
                    wq_sem.at[first, a],
                )
                for a in range(3)
            ]

        def kv_load(hp):
            slot = lax.rem(hp, 2)
            return [
                pltpu.make_async_copy(src.at[:, hp], dst.at[slot], kv_sem.at[i, slot])
                for i, (src, dst) in enumerate(((k_i, kb), (v_i, vb)))
            ]

        def p_load(t):
            d = lax.rem(lax.rem(t, M) + 1, M)
            return pltpu.make_async_copy(p_i.at[lax.div(t, M), d], pb.at[lax.rem(t, 2)], p_sem.at[lax.rem(t, 2)])

        for copy in kv_load(0) + [p_load(0)] + loads:
            copy.start()
        for first, count in groups:
            for copy in weight_cols(first, count):
                copy.start()
        loads[0].wait()
        row_of = lax.broadcasted_iota(jnp.int32, (128, L), 0)
        lane_of = lax.broadcasted_iota(jnp.int32, (L, 128), 1)

        def send_back(hp, d):
            slot = lax.rem(hp, 2)
            return remote(
                stage.at[slot, d - 1], land_o.at[hp, d - 1], dkv_send.at[slot, d - 1], dkv_recv.at[hp, d - 1],
                ctx=group + lax.rem(m + d, M),
            )

        def chunk(hp, slot, d):
            j = lax.rem(m + d, M)
            t = hp * M + lax.rem(d - 1 + M, M)
            p_load(t).wait()

            @pl.when(t + 1 < NP * M)
            def _():
                p_load(t + 1).start()

            key, value = kb[slot, j], vb[slot, j]
            turned = key.T
            query, up, up_t = q[hp], grad_o[hp], grad_ot[hp]
            sums = []
            for e in range(2):
                rows = (row_of < HEAD_DIM) if e == 0 else (row_of >= HEAD_DIM)
                lanes = (lane_of < HEAD_DIM) if e == 0 else (lane_of >= HEAD_DIM)
                zero, zero_t = jnp.zeros_like(query), jnp.zeros_like(up_t)
                probs = pb[lax.rem(t, 2), e].astype(f32) * fac[d, hp, e : e + 1, :]
                dprobs = dotf(value, jnp.where(rows, up_t, zero_t))
                dscores = (probs * (dprobs - delta[hp, e : e + 1, :])).astype(bf16)
                sums.append(
                    (
                        dotf(dscores, jnp.where(lanes, query, zero)),
                        dotf(probs.astype(bf16), jnp.where(lanes, up, zero)),
                    )
                )
                head = slice(e * HEAD_DIM, (e + 1) * HEAD_DIM)
                dqt[head, :] += dotf(turned[head], dscores)
            return sums[0][0] + sums[1][0], sums[0][1] + sums[1][1]

        def pair(hp, between):
            slot = lax.rem(hp, 2)
            for copy in kv_load(hp):
                copy.wait()

            @pl.when(hp + 1 < NP)
            def _():
                for copy in kv_load(hp + 1):
                    copy.start()

            dqt[...] = jnp.zeros(dqt.shape, f32)

            def far(d, carry):
                @pl.when(hp >= 2)
                def _():
                    send_back(hp - 2, d).wait_send()

                dk, dv = chunk(hp, slot, d)
                stage[slot, d - 1, 0] = dk.astype(bf16)
                stage[slot, d - 1, 1] = dv.astype(bf16)
                send_back(hp, d).start()
                return carry

            lax.fori_loop(1, M, far, 0)
            between()
            dk, dv = chunk(hp, slot, 0)
            own_k[slot] = dk
            own_v[slot] = dv
            turned_q[slot] = (dqt[...] * HEAD_DIM**-0.5).T.astype(bf16)

        def fetched(first, count):
            return pltpu.make_async_copy(land_o.at[pl.ds(first, count)], land.at[pl.ds(0, count)], land_sem.at[0])

        def fetch(first, count):
            for u in range(count):
                for d in range(1, M):
                    send_back(first + u, d).wait_recv()
            if M > 1:
                fetched(first, count).start()

        def project_back(first, count):
            if M > 1:
                fetched(first, count).wait()
            W = count * 128
            for u in range(count):
                slot = (first + u) % 2
                dk, dv = own_k[slot], own_v[slot]
                for d in range(1, M):
                    dk = dk + land[u, d - 1, 0].astype(f32)
                    dv = dv + land[u, d - 1, 1].astype(f32)
                grads[:, u * 128 : (u + 1) * 128] = turned_q[slot]
                grads[:, W + u * 128 : W + (u + 1) * 128] = dk.astype(bf16)
                grads[:, 2 * W + u * 128 : 2 * W + (u + 1) * 128] = dv.astype(bf16)
            cols = slice(first * 128, first * 128 + W)
            smg[QB : QB + 1, cols] = colsum(grads[:, 0:W].astype(f32))
            smg[VB : VB + 1, cols] = colsum(grads[:, 2 * W : 3 * W].astype(f32))

            def weight(k):
                rows = tile(k, T)
                block = dotg(xs[:, rows], grads[...], 0, 0).astype(bf16)
                for a in range(3):
                    for e in range(2):
                        pq[first // 2, e, rows, a * 128 : (a + 1) * 128] = block[
                            :, a * W + e * 128 : a * W + (e + 1) * 128
                        ]
                swap_q[first // 2].start(k)

            loop(D // T, weight)

        def input_back(first, count):
            for copy in weight_cols(first, count):
                copy.wait()
            W = 3 * count * 128
            base = 3 * first * 128

            def back(k):
                rows = tile(k, T)
                gsec[:, rows] += dotg(grads[:, 0:W], wq[rows, base : base + W], 1, 1)

            loop(D // T, back)

        def drain_stage():
            for hp in (NP - 2, NP - 1):
                for d in range(1, M):
                    send_back(hp, d).wait_send()

        def pair_group(first, count):
            def body(u):
                def here(name):
                    for k in range(count):

                        @pl.when(u == k)
                        def _():
                            point(f"{name}{first + k}")

                pair(first + u, lambda: here("far"))
                here("pair")

            loop(count, body)

        for g, (first, count) in enumerate(groups[:2]):
            pair_group(first, count)
            fetch(first, count)
            if g == 0:
                loads[1].wait()
            project_back(first, count)
            point(f"project{g}")
            input_back(first, count)
            swap_q[g].add()
            point(f"input{g}")
        pair_group(*groups[2])
        fetch(*groups[2])
        project_back(*groups[2])

        width = D // S
        ps[...] = jnp.zeros(ps.shape, bf16)
        share = FF // S
        for owner in range(S):
            ps[owner, 0, 0:8, 0:width] = smg[0:8, owner * width : (owner + 1) * width].astype(bf16)
            for r in range(share // width):
                start = owner * share + r * width
                a, b = start // D, start % D
                ps[owner, 1, r : r + 1, 0:width] = smg[IB + a : IB + a + 1, b : b + width].astype(bf16)
        items["s"].start()
        point("project2")
        input_back(*groups[2])
        for r in range(L // PP):
            rows = pl.ds(r * PP, PP)
            grads[rows, :] = gsec[rows, :].astype(bf16)
        swap_q[2].add()
        gin_move = Ungroup(grads, gin_o, rg_send.at[1], rg_recv.at[1], rg_local.at[1], C, G)
        for j in range(G):
            ticks[f"g{j}"] = [functools.partial(gin_move.start, j)]
        point("input2")
        point("end")
        assert ran == {(name, i + 1) for name in ticks for i in range(len(ticks[name]))}
        gin_move.finish()
        gin_move.drain()
        drain_stage()

    pl.run_scoped(
        attention, V((D, 3 * D), bf16), V((L, D), bf16), V((NP, L, 128), bf16),
        V((2, M, L, 128), bf16), V((2, M, L, 128), bf16), V((2, 2, L, L), bf16),
        V((2, L, 128), f32), V((2, L, 128), f32), V((2, max(M - 1, 1), 2, L, 128), bf16),
        V((2, max(M - 1, 1), 2, L, 128), bf16), V((L, 3 * T), bf16), V((128, L), f32),
        V((2, L, 128), bf16),
    )
    out_move.finish()
    out_move.drain()
    for item in items.values():
        item.finish()
        item.drain()
    for swap in [swap_u] + swap_i + [swap_o] + swap_q:
        swap.drain()


def backward_call(S, C, G, PP, saved):
    (xs, wq, wo, wi, wu, k, v, q, _, p, fac, ctxt, ctx, n1, f1, flow, act, dgel, gsec, gb, outv, smg, sm) = saved
    L, D = xs.shape
    M, NP, FF = C // G, D // 128, wi.shape[1]
    R, RU = D // S, FF // S
    sds = jax.ShapeDtypeStruct
    land = max(M - 1, 1)
    H, SR, SW = D // 2, 32, 256
    outs = [
        ((G, PP, D), bf16), ((G, PP, D), bf16), ((R, 3 * D), bf16), ((R, D), bf16), ((R, FF), bf16), ((RU, D), bf16),
        ((NP, land, 2, L, 128), bf16), ((2, SR // 2, SW), bf16),
    ]
    cut = RU // 3
    scratch = [
        (2, FF, H), (2, 2, D, D), (2, D, H), (3, 2, D, H), (S, 2, SR // 2, SW),
        (FF, H), (2, D, D), (D, H), (3, D, H), (S, SR // 2, SW),
        (3, 2, S - 1, cut // 2, H), (8, 2, S - 1, R // 2, H), (S - 1, SR // 2, SW),
        (3, cut, H), (8, R, H), (3, cut, H), (8, R, H),
        (C // 2, SR // 2, SW), (SR // 2, SW),
    ]
    scratch = [(x, bf16) for x in scratch] + [
        ((L, D), f32), ((L, D), bf16), ((NP, L, 128), bf16), ((NP, 128, L), bf16), ((NP, 2, L), f32), ((16, D), f32),
    ]
    dma = pltpu.SemaphoreType.DMA
    sems = [
        dma((8, 8)), dma((8, 8)), dma((1, 1)), dma((1, 1)), dma((1, S - 1)), dma((1, S - 1)), dma((1, C // 2)), dma((1, C // 2)),
        dma((13, 3)), dma((13, 3)), dma((12, 2, S - 1)), dma((12, 2, S - 1)), dma((12, 2)),
        dma((12, 2)),
        dma((2, G)), dma((2, G)), dma((2,)), dma((10,)), dma((NP, 3)), dma((2, 2)), dma((2,)), dma((2, land)), dma((NP, land)), dma((1,)),
        dma((13, 3)),
    ]
    results = pl.pallas_call(
        functools.partial(backward_kernel, (S, C, G, PP)),
        out_shape=[sds(*o) for o in outs],
        in_specs=[ANY] * 19 + [VMEM] * 3,
        out_specs=[ANY] * len(outs),
        scratch_shapes=[pltpu.VMEM(*x) for x in scratch] + sems,
        compiler_params=pltpu.CompilerParams(
            collective_id=1, has_side_effects=True, vmem_limit_bytes=62 << 20
        ),
        name="backward",
    )(outv, gsec, gb, act, dgel, wu, wi, wo, wq, flow, n1, f1, xs, ctx, ctxt, q, k, v, p, fac, smg, sm)
    return results


def solution(mesh):
    S, C = mesh.shape["seq"], mesh.shape["ctx"]

    def on_device(
        hid, cot, seg, wq, qb, vb, wo, ob, fg, fs, wi, ib, wu, ub, sg, ss
    ):
        G, PP, D = hid.shape
        saved = forward_call(S, C, hid, cot, seg.reshape(G, 1, PP), wq, wo, wi, wu, [qb, vb, ob, fg, fs, ub, sg, ss, ib])
        out, gin, gq, go, gi, gu, _, gs = backward_call(S, C, G, PP, saved)
        gu, gi, gq, go, gin, out = widen([gu, gi, gq, go, gin.reshape(G * PP, D)], out.reshape(G * PP, D))
        gs = gs.reshape(-1, gs.shape[-1]).astype(f32)
        width = D // S
        row = lambda r: gs[r, :width]
        grad_ib = gs[16 : 16 + ib.shape[0] // width, :width].reshape(-1)
        return (
            out.reshape(G, PP, D), gin.reshape(G, PP, D), gq, row(QB), row(VB), go, row(OB), row(FG), row(FS), gi,
            grad_ib, gu, row(UB), row(SG), row(SS),
        )

    rows, matrix, vector = P("seq", "ctx", None), P("seq", None), P("seq")
    return jax.shard_map(
        on_device,
        mesh=mesh,
        in_specs=(
            rows, rows, P("seq", "ctx"), matrix, vector, vector, matrix, vector, vector, vector, matrix, vector,
            matrix, vector, vector, vector,
        ),
        out_specs=(
            rows, rows, matrix, vector, vector, matrix, vector, vector, vector, matrix, vector, matrix, vector,
            vector, vector,
        ),
        check_vma=False,
    )
```

```python
import functools

import jax
import jax.numpy as jnp
from jax import lax
from jax.experimental import pallas as pl
from jax.experimental.pallas import tpu as pltpu
from jax.sharding import PartitionSpec as P

HEAD_DIM = 64
EPS = 1e-12
NEG = -1e30
RB = 64
ROOT_HALF = 0.7071067811865476
PDF_SCALE = 0.3989422804014327
f32 = jnp.float32
bf16 = jnp.bfloat16
MESH = pl.DeviceIdType.MESH
ANY = pl.BlockSpec(memory_space=pl.ANY)
VMEM = pl.BlockSpec(memory_space=pltpu.VMEM)

QB, VB, OB, FG, FS, UB, SG, SS, IB = 0, 1, 2, 3, 4, 5, 6, 7, 8


def tile(i, width):
    return pl.ds(pl.multiple_of(i * width, width), width)


def span(start, width, unit=128):
    return pl.ds(pl.multiple_of(start, unit), width)


def dotf(a, b):
    return jnp.dot(a, b, preferred_element_type=f32)


def dotg(a, b, ca, cb):
    return lax.dot_general(a, b, (((ca,), (cb,)), ((), ())), preferred_element_type=f32)


def remote(src, dst, send_sem, recv_sem, **where):
    return pltpu.make_async_remote_copy(
        src_ref=src,
        dst_ref=dst,
        send_sem=send_sem,
        recv_sem=recv_sem,
        device_id=where,
        device_id_type=MESH,
    )


def enter(S, C):
    s, c = lax.axis_index("seq"), lax.axis_index("ctx")
    barrier = pltpu.get_barrier_semaphore()
    for d in range(1, S):
        pl.semaphore_signal(
            barrier, inc=1, device_id={"seq": lax.rem(s + d, S)}, device_id_type=MESH
        )

    def greet(d, carry):
        pl.semaphore_signal(
            barrier, inc=1, device_id={"ctx": lax.rem(c + d, C)}, device_id_type=MESH
        )
        return carry

    lax.fori_loop(1, C, greet, 0)

    def wait():
        pl.semaphore_wait(barrier, S - 1 + C - 1)

    return wait


def bit_orders(S):
    bits = [1 << k for k in range(S.bit_length() - 1)]
    return (bits, bits[1:] + bits[:1])


def subsets(bits):
    out = [0]
    for b in bits:
        out = out + [o | b for o in out]
    return out


class Gather:
    def __init__(self, S, shard, full, send, recv, swap_send, swap_recv, local):
        self.S, self.shard, self.full = S, shard, full
        self.send, self.recv, self.local = send, recv, local
        self.swap_send, self.swap_recv = swap_send, swap_recv
        self.R, self.N = shard.shape
        self.s, self.c = lax.axis_index("seq"), lax.axis_index("ctx")
        self.cols = span(lax.rem(self.c, 2) * (self.N // 2), self.N // 2)
        self.orders = bit_orders(S)
        self.steps = len(self.orders[0])
        self.half = self.R // 2

    def block(self, owner, p):
        return self.full.at[span(owner * self.R + p * self.half, self.half, 16), self.cols]

    def copy_own(self):
        return pltpu.make_async_copy(
            self.shard, self.full.at[span(self.s * self.R, self.R, 16), :], self.local
        )

    def copies(self, t, direct):
        out = []
        for p in range(2):
            order = self.orders[p]
            for i, mask in enumerate(subsets(order[:t])):
                if (mask == 0) == direct:
                    owner = jnp.bitwise_xor(self.s, mask)
                    src = self.block(owner, p)
                    if mask == 0:
                        src = self.shard.at[pl.ds(p * self.half, self.half), self.cols]
                    k = (1 << t) - 1 + i
                    peer = jnp.bitwise_xor(self.s, order[t])
                    out.append(remote(src, self.block(owner, p), self.send.at[p, k], self.recv.at[p, k], seq=peer))
        return out

    def swaps(self, t, direct):
        out = []
        for p in range(2):
            order = self.orders[p]
            for i, mask in enumerate(subsets(order[:t])):
                if (mask == 0) == direct:
                    got = self.block(jnp.bitwise_xor(self.s, order[t] ^ mask), p)
                    k = (1 << t) - 1 + i
                    out.append(
                        remote(
                            got, got, self.swap_send.at[p, k], self.swap_recv.at[p, k], ctx=jnp.bitwise_xor(self.c, 1)
                        )
                    )
        return out

    def start(self):
        for t in range(self.steps):
            for copy in self.copies(t, True):
                copy.start()
        self.copy_own().start()

    def pass_on(self, t):
        for copy in self.copies(t, False):
            copy.start()

    def arrive(self, t, direct):
        for copy in self.copies(t, direct):
            copy.wait_recv()
        for copy in self.swaps(t, direct):
            copy.start()

    def first(self):
        self.arrive(0, True)
        self.pass_on(1)

    def middle(self):
        for t in range(1, self.steps):
            self.arrive(t, True)
            if t + 1 < self.steps:
                self.arrive(t, False)
                self.pass_on(t + 1)

    def last(self):
        self.arrive(self.steps - 1, False)

    def ready(self, early, late):
        if early:
            self.copy_own().wait()
        for t in range(self.steps):
            for direct in (True, False):
                final = t == self.steps - 1 and not direct
                if late if final else early:
                    for copy in self.swaps(t, direct):
                        copy.wait_recv()

    def drain(self):
        for t in range(self.steps):
            for direct in (True, False):
                for copy in self.copies(t, direct) + self.swaps(t, direct):
                    copy.wait_send()


class PairGather(Gather):
    def __init__(self, S, shard, full, send, recv, swap_send, swap_recv, local, pair_sems):
        super().__init__(S, shard, full, send, recv, swap_send, swap_recv, local)
        self.pair_send, self.pair_recv, self.late_send, self.late_recv = pair_sems
        core, odd, width = lax.rem(self.c, 2), lax.rem(lax.div(self.c, 2), 2), self.N // 4
        self.cols = span((2 * core + odd) * width, width)
        self.late_cols = span((2 * core + 1 - odd) * width, width)
        self.quarters = [2 * core + odd, 2 * (1 - core) + odd, 2 * core + 1 - odd, 2 * (1 - core) + 1 - odd]

    def late_block(self, owner, p):
        return self.full.at[span(owner * self.R + p * self.half, self.half, 16), self.late_cols]

    def arrived(self, t, direct):
        for p in range(2):
            order = self.orders[p]
            for i, mask in enumerate(subsets(order[:t])):
                if (mask == 0) == direct:
                    yield p, (1 << t) - 1 + i, jnp.bitwise_xor(self.s, order[t] ^ mask)

    def pair_copies(self, t, direct):
        return [
            remote(
                self.block(owner, p), self.block(owner, p), self.pair_send.at[p, k], self.pair_recv.at[p, k],
                ctx=jnp.bitwise_xor(self.c, 2),
            )
            for p, k, owner in self.arrived(t, direct)
        ]

    def late_swaps(self, t, direct):
        return [
            remote(
                self.late_block(owner, p), self.late_block(owner, p), self.late_send.at[p, k], self.late_recv.at[p, k],
                ctx=jnp.bitwise_xor(self.c, 1),
            )
            for p, k, owner in self.arrived(t, direct)
        ]

    def arrive(self, t, direct):
        super().arrive(t, direct)
        for copy in self.pair_copies(t, direct):
            copy.start()

    def every(self):
        return [(t, direct) for t in range(self.steps) for direct in (True, False)]

    def late(self):
        for which in self.every():
            for copy in self.pair_copies(*which):
                copy.wait_recv()
            for copy in self.late_swaps(*which):
                copy.start()

    def late_ready(self):
        for which in self.every():
            for copy in self.late_swaps(*which):
                copy.wait_recv()

    def drain(self):
        super().drain()
        for which in self.every():
            for copy in self.pair_copies(*which) + self.late_swaps(*which):
                copy.wait_send()


class Regroup:
    def __init__(self, src, dst, send, recv, local, C, G):
        self.src, self.dst, self.send, self.recv, self.local = src, dst, send, recv, local
        self.G, self.M = G, C // G
        self.c = lax.axis_index("ctx")

    def dst_at(self, j):
        if len(self.dst.shape) == 2:
            rows = self.src.shape[1]
            return self.dst.at[tile(j, rows), :]
        return self.dst.at[j]

    def each(self, on_remote, on_local):
        place = lax.rem(self.c, self.G)
        for g in range(self.G):
            target = g * self.M + lax.div(self.c, self.G)
            far = remote(
                self.src.at[g], self.dst_at(place), self.send.at[g], self.recv.at[place], ctx=target
            )
            near = pltpu.make_async_copy(self.src.at[g], self.dst_at(place), self.local)

            @pl.when(target != self.c)
            def _():
                on_remote(far)

            @pl.when(target == self.c)
            def _():
                on_local(near)

    def start(self):
        self.each(lambda far: far.start(), lambda near: near.start())

    def drain(self):
        self.each(lambda far: far.wait_send(), lambda near: None)

    def finish(self):
        m = lax.rem(self.c, self.M)
        for j in range(self.G):
            source = m * self.G + j

            @pl.when(source != self.c)
            def _():
                remote(
                    self.src.at[0], self.dst_at(j), self.send.at[0], self.recv.at[j], ctx=source
                ).wait_recv()

            @pl.when(source == self.c)
            def _():
                pltpu.make_async_copy(self.src.at[0], self.dst_at(j), self.local).wait()


class Ungroup:
    def __init__(self, src, dst, send, recv, local, C, G):
        self.src, self.dst, self.send, self.recv, self.local = src, dst, send, recv, local
        self.G, self.M, self.P = G, C // G, dst.shape[1]
        self.c = lax.axis_index("ctx")

    def each(self, on_remote, on_local, only=None):
        g, m = lax.div(self.c, self.M), lax.rem(self.c, self.M)
        for j in range(self.G) if only is None else (only,):
            target = m * self.G + j
            rows = self.src.at[pl.ds(j * self.P, self.P), :]
            far = remote(rows, self.dst.at[g], self.send.at[j], self.recv.at[g], ctx=target)
            near = pltpu.make_async_copy(rows, self.dst.at[g], self.local)

            @pl.when(target != self.c)
            def _():
                on_remote(far)

            @pl.when(target == self.c)
            def _():
                on_local(near)

    def start(self, only=None):
        self.each(lambda far: far.start(), lambda near: near.start(), only)

    def drain(self):
        self.each(lambda far: far.wait_send(), lambda near: None)

    def finish(self):
        rows = self.src.at[pl.ds(0, self.P), :]
        for g in range(self.G):
            source = g * self.M + lax.div(self.c, self.G)

            @pl.when(source != self.c)
            def _():
                remote(
                    rows, self.dst.at[g], self.send.at[0], self.recv.at[g], ctx=source
                ).wait_recv()

            @pl.when(source == self.c)
            def _():
                pltpu.make_async_copy(rows, self.dst.at[g], self.local).wait()


def mask_bias(seg_keys, seg_queries, bias, G, PP):
    rows = [seg_queries[i].astype(f32) for i in range(G)]
    for a in range(G):
        column = jnp.broadcast_to(seg_keys[a].astype(f32), (PP, PP)).T
        for b in range(G):
            bias[a * PP : (a + 1) * PP, b * PP : (b + 1) * PP] = jnp.where(
                column == rows[b], jnp.zeros((PP, PP), f32), jnp.full((PP, PP), NEG, f32)
            ).astype(bias.dtype)


def norm_rows(x):
    centred = x - jnp.mean(x, axis=-1, keepdims=True)
    factor = lax.rsqrt(jnp.mean(centred * centred, axis=-1, keepdims=True) + EPS)
    return centred * factor, factor


def norm_back(g, gain, normed, factor):
    h = g * gain
    return factor * (
        h
        - jnp.mean(h, axis=-1, keepdims=True)
        - normed * jnp.mean(h * normed, axis=-1, keepdims=True)
    )


def loop(n, body):
    def step(i, carry):
        body(i)
        return carry

    lax.fori_loop(0, n, step, 0)


def colsum(x):
    return jnp.sum(x, axis=0, keepdims=True)


def forward_kernel(
    dims,
    hid, cot, seg, wq_s, wo_s, wi_s, wu_s, qb, vb, ob, fg, fs, ub, sg, ss, ib,
    xs_o, wq_o, wo_o, wi_o, wu_o, k_o, v_o, q_o, seg_o, p_o, fac_o, ctxt_o, ctx_o,
    n1_o, f1_o, flow_o, act_o, dgel_o, gsec_o, gb_o, out_o, smg_o, sm_o,
    xs, ct, wq, wo, wi, wu, small_all, segc, segk, q, qt, kown, vown, kc, vc, bias, pst, m_s, l_s, ctxt, ctx,
    first, n1, f1, flow, h, h2, act, dgel, n2, gsec, gb, outv,
    ag_send, ag_recv, sw_send, sw_recv, pair_sem, ag_local, rg_send, rg_recv, rg_local, sm_send, sm_recv,
    kv_send, kv_recv, kv_local, kc_sem, p_sem, out_sem,
):
    S, C, G, PP = dims
    M, L, D = C // G, G * PP, hid.shape[2]
    FF = wi.shape[1]
    NP = D // 128
    T = 256
    s, c = lax.axis_index("seq"), lax.axis_index("ctx")
    m = lax.rem(c, M)

    def gather(kind, w, shard, full, *more):
        sems = [a.at[w] for a in (ag_send, ag_recv, sw_send, sw_recv, ag_local)]
        return kind(S, shard, full, *sems, *more)

    gathers = [
        gather(Gather, 0, wq_s, wq),
        gather(Gather, 1, wo_s, wo),
        gather(PairGather, 2, wi_s, wi, [pair_sem.at[i] for i in range(4)]),
        gather(Gather, 3, wu_s, wu),
    ]
    gq, go, gi, gu = gathers
    pending = []

    def put(src, dst):
        copy = pltpu.make_async_copy(src, dst, out_sem.at[len(pending)])
        copy.start()
        pending.append(copy)

    enter(S, C)()
    hid_move = Regroup(hid, xs, rg_send.at[0], rg_recv.at[0], rg_local.at[0], C, G)
    cot_move = Regroup(cot, ct, rg_send.at[1], rg_recv.at[1], rg_local.at[1], C, G)
    seg_move = Regroup(seg, segc, rg_send.at[2], rg_recv.at[2], rg_local.at[2], C, G)
    seg_move.start()
    hid_move.start()
    gq.start()
    width, share = D // S, FF // S
    small = small_all.at[s]
    small[...] = jnp.zeros(small.shape, bf16)
    for r, vector in enumerate((qb, vb, ob, fg, fs, ub, sg, ss)):
        small[r : r + 1, 0:width] = vector[...].reshape(1, width)
    for r in range(share // width):
        small[IB + r : IB + r + 1, 0:width] = ib[r * width : (r + 1) * width].reshape(1, width)
    small_copies = [
        remote(small, small, sm_send.at[d - 1], sm_recv.at[s], seq=jnp.bitwise_xor(s, d))
        for d in range(1, S)
    ]
    for copy in small_copies:
        copy.start()
    seg_move.finish()

    group = lax.div(c, M) * M
    seg_own = pltpu.make_async_copy(segc, seg_o.at[m], kv_local.at[2])
    seg_own.start()

    def peer(d):
        return group + lax.rem(m + d, M)

    def kv_copies(d):
        return [
            remote(src, dst.at[m], kv_send.at[i, d], kv_recv.at[i, m], ctx=peer(d))
            for i, (src, dst) in enumerate(((kown, k_o), (vown, v_o), (segc, seg_o)))
        ]

    def kv_arrivals(d):
        j = lax.rem(m + d, M)
        return [
            remote(src, dst.at[j], kv_send.at[i, d], kv_recv.at[i, j], ctx=peer(d))
            for i, (src, dst) in enumerate(((kown, k_o), (vown, v_o), (segc, seg_o)))
        ]

    for d in range(1, M):
        kv_copies(d)[2].start()

    for d in range(1, S):
        far = jnp.bitwise_xor(s, d)
        remote(small, small_all.at[far], sm_send.at[d - 1], sm_recv.at[far], seq=far).wait_recv()
    sm_o[...] = jnp.zeros(sm_o.shape, f32)
    for owner in range(S):
        block = small_all[owner].astype(f32)
        sm_o[0:IB, owner * width : (owner + 1) * width] = block[0:IB, 0:width]
        for r in range(share // width):
            start = owner * share + r * width
            a, b = start // D, start % D
            sm_o[IB + a : IB + a + 1, b : b + width] = block[IB + r : IB + r + 1, 0:width]
    mask_bias(segc, segc, bias, G, PP)
    gq.first()
    go.start()
    gi.start()
    gq.middle()
    gq.last()
    hid_move.finish()
    put(xs, xs_o)
    gq.ready(True, True)
    put(wq, wq_o)

    def project(i):
        cols = tile(i, T)
        qv = dotf(xs[...], wq[:, cols]) + sm_o[QB : QB + 1, cols]
        kv = dotf(xs[...], wq[:, span(D + i * T, T)])
        vv = dotf(xs[...], wq[:, span(2 * D + i * T, T)]) + sm_o[VB : VB + 1, cols]
        qs = (qv.astype(bf16).astype(f32) * HEAD_DIM**-0.5).astype(bf16)
        kv, vv = kv.astype(bf16), vv.astype(bf16)
        for u in range(T // 128):
            lanes = slice(u * 128, (u + 1) * 128)
            hp = i * (T // 128) + u
            q[hp] = qs[:, lanes]
            qt[hp] = qs[:, lanes].T
            kown[hp] = kv[:, lanes]
            vown[hp] = vv[:, lanes]

    loop(D // T, project)
    for d in range(1, M):
        for copy in kv_copies(d)[:2]:
            copy.start()
    own_kv = [
        pltpu.make_async_copy(kown, k_o.at[m], kv_local.at[0]),
        pltpu.make_async_copy(vown, v_o.at[m], kv_local.at[1]),
    ]
    for copy in own_kv:
        copy.start()
    put(q, q_o)
    go.first()
    gi.first()
    gu.start()

    row_of = lax.broadcasted_iota(jnp.int32, (128, L), 0)

    def keep_probs(hp, d):
        slot = lax.rem(hp, 2)
        return pltpu.make_async_copy(pst.at[slot], p_o.at[hp, d], p_sem.at[slot])

    def attend(keys, values, d, extra):
        fresh = isinstance(d, int)

        def pair(hp):
            extra(hp)
            slot = lax.rem(hp, 2)
            if fresh:

                @pl.when(hp >= 2)
                def _():
                    keep_probs(hp, d).wait()

            else:
                keep_probs(hp, d).wait()
            qv, kv, vt, b = qt[hp], keys[hp], values[hp].T, bias[...]
            for e in range(2):
                head = slice(e * HEAD_DIM, (e + 1) * HEAD_DIM)
                mine = (row_of < HEAD_DIM) if e == 0 else (row_of >= HEAD_DIM)
                scores = dotf(kv, jnp.where(mine, qv, jnp.zeros_like(qv))) + b
                top = jnp.max(scores, axis=0, keepdims=True)
                if fresh:
                    weights = jnp.exp(scores - top)
                    low = weights.astype(bf16)
                    m_s[d, hp, e : e + 1, :] = top
                    l_s[hp, e : e + 1, :] = colsum(weights)
                    ctxt[hp, head, :] = dotf(vt[head], low)
                else:
                    old = m_s[d - 1, hp, e : e + 1, :]
                    top = jnp.maximum(old, top)
                    keep = jnp.exp(old - top)
                    weights = jnp.exp(scores - top)
                    low = weights.astype(bf16)
                    m_s[d, hp, e : e + 1, :] = top
                    l_s[hp, e : e + 1, :] = l_s[hp, e : e + 1, :] * keep + colsum(weights)
                    ctxt[hp, head, :] = ctxt[hp, head, :] * keep + dotf(vt[head], low)
                pst[slot, e] = low
            keep_probs(hp, d).start()

        loop(NP, pair)

    def in_own(hp):
        @pl.when(hp == NP - 2)
        def _():
            go.middle()
            go.last()
            gi.middle()

        @pl.when(hp == NP - 1)
        def _():
            gi.last()
            cot_move.start()

    attend(kown, vown, 0, in_own)

    def far_chunk(d, carry):
        j = lax.rem(m + d, M)
        for copy in kv_arrivals(d):
            copy.wait_recv()
        loads = [
            pltpu.make_async_copy(k_o.at[j], kc, kc_sem.at[0]),
            pltpu.make_async_copy(v_o.at[j], vc, kc_sem.at[1]),
            pltpu.make_async_copy(seg_o.at[j], segk, kc_sem.at[2]),
        ]
        for copy in loads:
            copy.start()
        for copy in loads:
            copy.wait()
        mask_bias(segk, segc, bias, G, PP)

        def in_far(hp):
            @pl.when(jnp.logical_and(d == M - 1, hp == NP - 2))
            def _():
                gu.first()

        attend(kc, vc, d, in_far)
        return carry

    lax.fori_loop(1, M, far_chunk, 0)

    def close(hp):
        for e in range(2):
            head = slice(e * HEAD_DIM, (e + 1) * HEAD_DIM)
            share = 1.0 / l_s[hp, e : e + 1, :]
            ctxt[hp, head, :] = ctxt[hp, head, :] * share
            for d in range(M):
                fac_o[d, hp, e : e + 1, :] = jnp.exp(m_s[d, hp, e : e + 1, :] - m_s[M - 1, hp, e : e + 1, :]) * share
        ctx[:, tile(hp, 128)] = ctxt[hp].T.astype(bf16)

    loop(NP, close)

    put(ctxt, ctxt_o)
    put(ctx, ctx_o)
    go.ready(True, True)
    put(wo, wo_o)

    def project_out(i):
        cols = tile(i, T)
        first[:, cols] = dotf(ctx[...], wo[:, cols]) + sm_o[OB : OB + 1, cols]

    loop(D // T, project_out)

    def first_norm(r):
        rows = tile(r, RB)
        normed, factor = norm_rows(first[rows, :] + xs[rows, :].astype(f32))
        y = normed * sm_o[FG : FG + 1, :] + sm_o[FS : FS + 1, :]
        n1[rows, :] = normed
        f1[rows, :] = factor
        first[rows, :] = y
        flow[rows, :] = y.astype(bf16)

    loop(L // RB, first_norm)
    put(n1, n1_o)
    put(f1, f1_o)
    put(flow, flow_o)
    if M == 1:
        gu.first()
    gi.ready(True, True)

    def feed_quarter(now, before):
        def step(k):
            cols = tile(k, T)
            if now is not None:
                number, place = now
                where = gi.quarters[number] * (FF // 4)
                row = lax.div(where, D)
                place[:, cols] = dotf(flow[...], wi[:, span(where + k * T, T)]) + sm_o[pl.ds(IB + row, 1), cols]
            if before is not None:
                number, place = before
                where = gi.quarters[number] * (FF // 4) + k * T
                for r in range(L // RB):
                    rows = pl.ds(r * RB, RB)
                    x = place[rows, cols]
                    share = 0.5 * (1.0 + lax.erf(x * ROOT_HALF))
                    act[rows, span(where, T)] = (x * share).astype(bf16)
                    dgel[rows, span(where, T)] = (
                        share + x * (PDF_SCALE * jnp.exp(-0.5 * x * x))
                    ).astype(bf16)

        loop(FF // 4 // T, step)

    feed_quarter((0, h), None)
    feed_quarter((1, h2), (0, h))
    gi.late()
    feed_quarter((2, h), (1, h2))
    gi.late_ready()
    put(wi, wi_o)
    feed_quarter((3, h2), (2, h))
    feed_quarter(None, (3, h2))
    put(act, act_o)
    put(dgel, dgel_o)
    RU = FF // S

    def feed_out(masks, fresh):
        owners = [jnp.bitwise_xor(s, k) for k in masks]

        def step(i):
            cols = tile(i, T)
            total = sm_o[UB : UB + 1, cols] if fresh else n2[:, cols]
            for owner in owners:
                total = total + dotf(act[:, span(owner * RU, RU)], wu[span(owner * RU, RU), cols])
            n2[:, cols] = total

        loop(D // T, step)

    gu.middle()
    gu.ready(True, False)
    feed_out([k for k in range(S) if k & (k - 1) == 0], True)
    gu.last()
    gu.ready(False, True)
    put(wu, wu_o)
    feed_out([k for k in range(S) if k & (k - 1)], False)
    cot_move.finish()
    smg_o[...] = jnp.zeros(smg_o.shape, f32)

    def second_norm(r):
        rows = tile(r, RB)
        normed, factor = norm_rows(first[rows, :] + n2[rows, :])
        gain = sm_o[SG : SG + 1, :]
        outv[rows, :] = (normed * gain + sm_o[SS : SS + 1, :]).astype(bf16)
        g = ct[rows, :].astype(f32)
        smg_o[SG : SG + 1, :] += colsum(g * normed)
        smg_o[SS : SS + 1, :] += colsum(g)
        back = norm_back(g, gain, normed, factor)
        gsec[rows, :] = back
        low = back.astype(bf16)
        gb[rows, :] = low
        smg_o[UB : UB + 1, :] += colsum(low.astype(f32))

    loop(L // RB, second_norm)
    put(outv, out_o)
    put(gsec, gsec_o)
    put(gb, gb_o)

    for u in range(2):
        keep_probs(NP - 2 + u, 0).wait()
    for gather in gathers:
        gather.drain()
    for move in (hid_move, cot_move, seg_move):
        move.drain()
    for copy in small_copies:
        copy.wait_send()
    for d in range(1, M):
        for copy in kv_copies(d):
            copy.wait_send()
    for copy in own_kv + [seg_own] + pending:
        copy.wait()


def forward_call(S, C, hid, cot, seg, wq_s, wo_s, wi_s, wu_s, vectors):
    G, PP, D = hid.shape
    L, M, NP, FF = G * PP, C // G, D // 128, wi_s.shape[1]
    sds = jax.ShapeDtypeStruct
    outs = [
        ((L, D), bf16), ((D, 3 * D), bf16), ((D, D), bf16), ((D, FF), bf16), ((FF, D), bf16),
        ((M, NP, L, 128), bf16), ((M, NP, L, 128), bf16), ((NP, L, 128), bf16),
        ((M, G, 1, PP), jnp.int32), ((NP, M, 2, L, L), bf16), None, ((NP, 128, L), f32), ((L, D), bf16),
        ((L, D), f32), ((L, 1), f32), ((L, D), bf16), ((L, FF), bf16), ((L, FF), bf16),
        ((L, D), f32), ((L, D), bf16), ((L, D), bf16),
    ]
    scratch = [
        ((L, D), bf16), ((L, D), bf16), ((D, 3 * D), bf16), ((D, D), bf16), ((D, FF), bf16), ((FF, D), bf16),
        ((S, 16, D // S + -(D // S) % 128), bf16), ((G, 1, PP), jnp.int32), ((G, 1, PP), jnp.int32),
        ((NP, L, 128), bf16), ((NP, 128, L), bf16), ((NP, L, 128), bf16), ((NP, L, 128), bf16),
        ((NP, L, 128), bf16), ((NP, L, 128), bf16), ((L, L), f32), ((2, 2, L, L), bf16), ((M, NP, 2, L), f32), ((NP, 2, L), f32),
        ((NP, 128, L), f32), ((L, D), bf16),
        ((L, D), f32), ((L, D), f32), ((L, 1), f32), ((L, D), bf16), ((L, D), f32), ((L, D), f32), ((L, FF), bf16),
        ((L, FF), bf16), ((L, D), f32), ((L, D), f32), ((L, D), bf16), ((L, D), bf16),
    ]
    dma = pltpu.SemaphoreType.DMA
    sems = [
        dma((4, 2, S)), dma((4, 2, S)), dma((4, 2, S)), dma((4, 2, S)), dma((4, 2, S)), dma((4,)), dma((3, G)), dma((3, G)), dma((3,)),
        dma((S,)), dma((S,)), dma((3, M)), dma((3, M)), dma((3,)), dma((3,)), dma((2,)), dma((24,)),
    ]
    return pl.pallas_call(
        functools.partial(forward_kernel, (S, C, G, PP)),
        out_shape=[sds(*(o or ((M, NP, 2, L), f32))) for o in outs] + [sds((16, D), f32), sds((16, D), f32)],
        in_specs=[ANY] * 7 + [VMEM] * len(vectors),
        out_specs=[ANY if o else VMEM for o in outs] + [VMEM, VMEM],
        scratch_shapes=[pltpu.VMEM(*x) for x in scratch] + sems,
        compiler_params=pltpu.CompilerParams(
            collective_id=0, has_side_effects=True, vmem_limit_bytes=62 << 20
        ),
        name="forward",
    )(hid, cot, seg, wq_s, wo_s, wi_s, wu_s, *vectors)


def widen_kernel(count, *refs):
    srcs, dsts = refs[: count + 1], refs[count + 1 : 2 * count + 2]
    lows, highs = refs[2 * count + 2 : 3 * count + 2], refs[3 * count + 2 : 4 * count + 2]
    plain, in_sem, out_sem = refs[4 * count + 2 :]
    loads, stores = [], []
    for i in range(count):
        loads.append(pltpu.make_async_copy(srcs[i], lows[i], in_sem.at[i]))
        stores.append(pltpu.make_async_copy(highs[i], dsts[i], out_sem.at[i]))
    loads.append(pltpu.make_async_copy(srcs[count], plain, in_sem.at[count]))
    stores.append(pltpu.make_async_copy(plain, dsts[count], out_sem.at[count]))
    for copy in loads:
        copy.start()
    for i in range(count):
        loads[i].wait()
        rows = lows[i].shape[0]
        unit = next(u for u in (64, 48, 32, 16) if rows % u == 0)

        def step(r, low=lows[i], high=highs[i], unit=unit):
            at = tile(r, unit)
            high[at, :] = low[at, :].astype(f32)

        loop(rows // unit, step)
        stores[i].start()
    loads[count].wait()
    stores[count].start()
    for copy in stores:
        copy.wait()


def widen(arrays, plain):
    count = len(arrays)
    sds = jax.ShapeDtypeStruct
    return pl.pallas_call(
        functools.partial(widen_kernel, count),
        out_shape=[sds(a.shape, f32) for a in arrays] + [sds(plain.shape, plain.dtype)],
        in_specs=[ANY] * (count + 1),
        out_specs=[ANY] * (count + 1),
        scratch_shapes=[pltpu.VMEM(a.shape, bf16) for a in arrays]
        + [pltpu.VMEM(a.shape, f32) for a in arrays]
        + [pltpu.VMEM(plain.shape, plain.dtype), pltpu.SemaphoreType.DMA((count + 1,)), pltpu.SemaphoreType.DMA((count + 1,))],
        compiler_params=pltpu.CompilerParams(vmem_limit_bytes=62 << 20),
        name="widen",
    )(*arrays, plain)


def add_rows(dst, src):
    rows = dst.shape[0]
    unit = next(u for u in (96, 48, 16) if rows % u == 0)

    def step(r):
        at = tile(r, unit)
        dst[at, :] = dst[at, :] + src[at, :]

    loop(rows // unit, step)


class CoreSwap:
    def __init__(self, part, far, rows, send, recv):
        self.part, self.far, self.rows, self.send, self.recv = part, far, rows, send, recv
        self.c = lax.axis_index("ctx")
        self.core = lax.rem(self.c, 2)
        self.count = part.shape[1] // rows

    def copy(self, i):
        rows = tile(i, self.rows)
        return remote(
            self.part.at[1 - self.core, rows, :], self.far.at[rows, :], self.send.at[i], self.recv.at[i],
            ctx=jnp.bitwise_xor(self.c, 1),
        )

    def start(self, i):
        self.copy(i).start()

    def add(self):
        loop(self.count, lambda i: self.copy(i).wait_recv())
        add_rows(self.part.at[self.core], self.far)

    def drain(self):
        loop(self.count, lambda i: self.copy(i).wait_send())


class Reduce:
    def __init__(self, S, C, part, stride, offset, R, cols, rx, zl, zr, sems, places):
        self.S, self.K, self.part, self.rx, self.zl, self.zr = S, C // 2, part, rx, zl, zr
        self.c_send, self.c_recv, self.x_send, self.x_recv, self.z_send, self.z_recv, self.l_send = sems
        self.places, self.stride, self.offset, self.R, self.cols = places, stride, offset, R, cols
        self.half = R // 2
        self.s, self.c = lax.axis_index("seq"), lax.axis_index("ctx")
        self.core = lax.rem(self.c, 2)
        self.k = lax.div(self.c, 2)
        self.left, self.right = self.K // 2 - 1, self.K // 2
        self.orders = bit_orders(S)
        self.steps = len(self.orders[0])

    def rows(self, owner, start, count):
        return self.part.at[self.core, span(owner * self.stride + self.offset + start, count, 16), self.cols]

    def block(self, owner, p):
        return self.rows(owner, p * self.half, self.half)

    def result(self):
        return self.rows(self.s, 0, self.R)

    def copies(self, t):
        out, base = [], self.S - (1 << (self.steps - t))
        for p in range(2):
            order = self.orders[p]
            peer = jnp.bitwise_xor(self.s, order[t])
            for i, mask in reversed(list(enumerate(subsets(order[t + 1 :])))):
                copy = remote(
                    self.block(jnp.bitwise_xor(peer, mask), p),
                    self.rx.at[p, base + i],
                    self.x_send.at[p, base + i],
                    self.x_recv.at[p, base + i],
                    seq=peer,
                )
                out.append((copy, p, base + i, mask))
        return out

    def cross_start(self, t):
        if t > 0:
            self.cross_add(t - 1, False)
        for copy, _, _, _ in self.copies(t):
            copy.start()

    def cross_add(self, t, last):
        for copy, p, slot, mask in self.copies(t):
            if (mask == 0) == last:
                copy.wait_recv()
                add_rows(self.block(jnp.bitwise_xor(self.s, mask), p), self.rx.at[p, slot])

    def from_left(self):
        return remote(self.result(), self.zl, self.z_send.at[0], self.z_recv.at[0], ctx=self.c + 2)

    def from_right(self):
        return remote(self.result(), self.zr, self.z_send.at[0], self.z_recv.at[1], ctx=self.c - 2)

    def out_left(self):
        return remote(self.zr, self.zr, self.z_send.at[1], self.z_recv.at[1], ctx=self.c - 2)

    def out_right(self):
        return remote(self.zl, self.zl, self.z_send.at[1], self.z_recv.at[0], ctx=self.c + 2)

    def inward(self, level):
        if level == 0:
            for t in range(self.steps):
                self.cross_add(t, True)

        @pl.when(self.k == level)
        def _():
            if level > 0:
                self.from_left().wait_recv()
                add_rows(self.result(), self.zl)
            self.from_left().start()

        @pl.when(self.k == self.K - 1 - level)
        def _():
            if level > 0:
                self.from_right().wait_recv()
                add_rows(self.result(), self.zr)
            self.from_right().start()

    def outward(self, distance):
        @pl.when(self.k == self.left - distance)
        def _():
            self.from_right().wait_recv()
            if distance == 0:
                add_rows(self.zr, self.result())
            if distance < self.left:
                self.out_left().start()
            self.deliver(self.zr)

        @pl.when(self.k == self.right + distance)
        def _():
            self.from_left().wait_recv()
            if distance == 0:
                add_rows(self.zl, self.result())
            if distance < self.left:
                self.out_right().start()
            self.deliver(self.zl)

    def deliveries(self, src):
        out = []
        for i, (cols, place) in enumerate(self.places):
            dst = place(self.core)
            out.append(
                (
                    pltpu.make_async_copy(src.at[:, cols], dst, self.l_send.at[i]),
                    remote(
                        src.at[:, cols], dst, self.c_send.at[i], self.c_recv.at[i], ctx=jnp.bitwise_xor(self.c, 1)
                    ),
                )
            )
        return out

    def deliver(self, src):
        for near, far in self.deliveries(src):
            near.start()
            far.start()

    def finish(self):
        for near, far in self.deliveries(self.zl):
            near.wait()
            far.wait_recv()

    def stages(self):
        def each(step, *which):
            for w in which:
                step(w)

        run = functools.partial
        return [
            run(each, self.cross_start, 0),
            run(each, self.cross_start, *range(1, self.steps)),
            run(each, self.inward, 0),
            run(each, self.inward, *range(1, self.left + 1)),
            run(each, self.outward, 0),
            run(each, self.outward, *range(1, self.left + 1)),
        ]

    def drain(self):
        for t in range(self.steps):
            for copy, _, _, _ in self.copies(t):
                copy.wait_send()

        @pl.when(self.k <= self.left)
        def _():
            self.from_left().wait_send()

        @pl.when(self.k >= self.right)
        def _():
            self.from_right().wait_send()

        @pl.when(jnp.logical_and(self.k <= self.left, self.k > 0))
        def _():
            self.out_left().wait_send()

        @pl.when(jnp.logical_and(self.k >= self.right, self.k < self.K - 1))
        def _():
            self.out_right().wait_send()

        for _, far in self.deliveries(self.zl):
            far.wait_send()


class DirectReduce:
    def __init__(self, S, C, part, far, rx, zx, done, sems, places):
        self.S, self.K, self.part, self.far, self.rx, self.zx, self.done = S, C // 2, part, far, rx, zx, done
        self.h_send, self.h_recv, self.x_send, self.x_recv, self.z_send, self.z_recv, self.c_send, self.c_recv, self.l_send = sems
        self.places = places
        self.s, self.c = lax.axis_index("seq"), lax.axis_index("ctx")
        self.core = lax.rem(self.c, 2)
        self.k = lax.div(self.c, 2)

    def other(self):
        return jnp.bitwise_xor(self.c, 1)

    def halves(self):
        return remote(
            self.part.at[:, 1 - self.core], self.far, self.h_send.at[0], self.h_recv.at[0], ctx=self.other()
        )

    def start(self):
        self.halves().start()

    def crossing(self):
        out = []
        for d in range(self.S - 1, 0, -1):
            peer = jnp.bitwise_xor(self.s, d)
            out.append(
                remote(
                    self.part.at[peer, self.core], self.rx.at[d - 1], self.x_send.at[d - 1], self.x_recv.at[d - 1],
                    seq=peer,
                )
            )
        return out

    def cross_start(self):
        self.halves().wait_recv()
        for owner in range(self.S):
            add_rows(self.part.at[owner, self.core], self.far.at[owner])
        for copy in self.crossing():
            copy.start()

    def along(self, d):
        chip = lax.rem(self.k + d, self.K)
        return remote(
            self.part.at[self.s, self.core], self.zx.at[self.k], self.z_send.at[d - 1], self.z_recv.at[self.k],
            ctx=2 * chip + self.core,
        )

    def arrival(self, d):
        chip = lax.rem(self.k + d, self.K)
        return remote(
            self.part.at[self.s, self.core], self.zx.at[chip], self.z_send.at[d - 1], self.z_recv.at[chip],
            ctx=2 * chip + self.core,
        )

    def along_start(self):
        mine = self.part.at[self.s, self.core]
        for copy in self.crossing():
            copy.wait_recv()
        total = mine[...].astype(f32)
        for d in range(1, self.S):
            total = total + self.rx[d - 1].astype(f32)
        total = total.astype(bf16)
        mine[...] = total
        self.zx[self.k] = total
        for d in range(self.K - 1, 0, -1):
            self.along(d).start()

    def outputs(self):
        out = []
        for i, (cols, place) in enumerate(self.places):
            dst = place(self.core)
            src = self.done.at[:, cols]
            out.append(
                (
                    pltpu.make_async_copy(src, dst, self.l_send.at[i]),
                    remote(src, dst, self.c_send.at[i], self.c_recv.at[i], ctx=self.other()),
                )
            )
        return out

    def deliver(self):
        for d in range(1, self.K):
            self.arrival(d).wait_recv()
        total = self.zx[0].astype(f32)
        for j in range(1, self.K):
            total = total + self.zx[j].astype(f32)
        self.done[...] = total.astype(bf16)
        for near, far in self.outputs():
            near.start()
            far.start()

    def stages(self):
        return [self.cross_start, self.along_start, self.deliver]

    def finish(self):
        for near, far in self.outputs():
            near.wait()
            far.wait_recv()

    def drain(self):
        self.halves().wait_send()
        for copy in self.crossing():
            copy.wait_send()
        for d in range(1, self.K):
            self.along(d).wait_send()
        for _, far in self.outputs():
            far.wait_send()


SCHEDULE = {
    "outer": (('u0', 1),),
    "ffn0": (('u1', 1),),
    "ffn1": (('u0', 2), ('u2', 1)),
    "ffn2": (('u1', 2),),
    "ffn3": (('i0', 1),),
    "first": (('u0', 3), ('u2', 2)),
    "context": (('u1', 3), ('i1', 1)),
    "far0": (('u0', 4), ('i0', 2)),
    "pair0": (('i2', 1),),
    "far1": (('u2', 3), ('i1', 2), ('i3', 1)),
    "pair1": (('u1', 4),),
    "project0": (('u0', 5), ('i0', 3)),
    "input0": (('i2', 2),),
    "far2": (('o', 1),),
    "pair2": (('u2', 4), ('i1', 3)),
    "far3": (('u0', 6), ('u1', 5), ('i0', 4), ('i3', 2)),
    "pair3": (('i2', 3),),
    "project1": (('o', 2),),
    "input1": (('u2', 5), ('i1', 4), ('q0', 1)),
    "far4": (('i3', 3), ('u1', 6), ('q1', 1)),
    "pair4": (('i0', 5), ('i2', 4), ('o', 3)),
    "far5": (('q0', 2),),
    "pair5": (('u2', 6), ('i1', 5), ('i3', 4), ('q1', 2)),
    "input2": (('i0', 6), ('i2', 5), ('o', 4), ('q0', 3), ('q2', 1), ('q3', 1), ('q4', 1)),
    "end": (('q1', 3), ('s', 1), ('i1', 6), ('i3', 5), ('g0', 1), ('q2', 2), ('q3', 2), ('q4', 2), ('i2', 6), ('o', 5), ('q0', 4), ('s', 2), ('q2', 3), ('q3', 3), ('q4', 3), ('i3', 6), ('q1', 4), ('q0', 5), ('q2', 4), ('q3', 4), ('o', 6), ('s', 3), ('q4', 4), ('q1', 5), ('g1', 1), ('q2', 5), ('q3', 5), ('q0', 6), ('q4', 5), ('g2', 1), ('q1', 6), ('g3', 1), ('q2', 6), ('q3', 6), ('q4', 6)),
}


def backward_kernel(
    dims,
    outv, gsec_i, gb_i, act_i, dgel_i, wu_i, wi_i, wo_i, wq_i, flow_i, n1_i, f1_i, xs_i, ctx_i, ctxt_i,
    q_i, k_i, v_i, p_i, fac, smg_i, sm,
    out_o, gin_o, gq_o, go_o, gi_o, gu_o, land_o, small_o,
    pu, pi, po, pq, ps, fu, fi, fo, fq, fs, rxu, rxi, rxq, rxs, zlu, zli, zlq, zru, zri, zrq, zxs, dns,
    gsec, gb, grad_o, grad_ot, delta, smg,
    cs_send, cs_recv, h_send, h_recv, dx_send, dx_recv, dz_send, dz_recv, c_send, c_recv, x_send, x_recv, z_send, z_recv, rg_send, rg_recv, rg_local, in_sem, wq_sem, kv_sem, p_sem, dkv_send, dkv_recv,
    land_sem, l_send,
):
    S, C, G, PP = dims
    M, L, D = C // G, G * PP, gsec.shape[1]
    FF = act_i.shape[1]
    NP = D // 128
    T = 256
    s, c = lax.axis_index("seq"), lax.axis_index("ctx")
    m, core = lax.rem(c, M), lax.rem(c, 2)
    group = lax.div(c, M) * M

    H = D // 2
    R, RU = D // S, FF // S
    cut = RU // 3
    items = {}

    def piece(name, places, *refs):
        n = len(items)
        sems = [a.at[n] for a in (c_send, c_recv, x_send, x_recv, z_send, z_recv, l_send)]
        items[name] = Reduce(S, C, *refs, sems, places)

    for i in range(3):
        piece(
            f"u{i}", [(pl.ds(0, H), lambda e, i=i: gu_o.at[pl.ds(i * cut, cut), span(e * H, H)])],
            pu.at[i], cut, 0, cut, pl.ds(0, H), rxu.at[i], zlu.at[i], zru.at[i],
        )

    def narrow_piece(name, places, part, cols):
        n = len(items) - 3
        piece(name, places, part, R, 0, R, cols, rxi.at[n], zli.at[n], zri.at[n])

    for i in range(2):
        for j in range(2):
            narrow_piece(
                f"i{2 * i + j}",
                [(pl.ds(0, H), lambda e, i=i, j=j: gi_o.at[:, span(e * (FF // 2) + i * D + j * H, H)])],
                pi.at[i], pl.ds(j * H, H),
            )
    narrow_piece("o", [(pl.ds(0, H), lambda e: go_o.at[:, span(e * H, H)])], po, pl.ds(0, H))

    def qkv_place(i, a):
        return lambda e: gq_o.at[:, span(a * D + (2 * i + e) * 128, 128)]

    for i in range(2):
        narrow_piece(
            f"q{i}", [(pl.ds(a * 128, 128), qkv_place(i, a)) for a in range(3)], pq.at[i], pl.ds(0, H)
        )
    for a in range(3):
        piece(
            f"q{2 + a}", [(pl.ds(0, 128), qkv_place(2, a))],
            pq.at[2], R, 0, R, pl.ds(a * 128, 128), rxq.at[a], zlq.at[a], zrq.at[a],
        )
    def direct_piece(name, n, places, *refs):
        m_ = len(items)
        sems = [a.at[n] for a in (h_send, h_recv, dx_send, dx_recv, dz_send, dz_recv)]
        items[name] = DirectReduce(S, C, *refs, sems + [a.at[m_] for a in (c_send, c_recv, l_send)], places)

    SW = ps.shape[3]
    direct_piece("s", 0, [(pl.ds(0, SW), lambda e: small_o.at[e])], ps, fs, rxs, zxs, dns)
    swap_u = [CoreSwap(pu.at[i], fu.at[i], cut, cs_send.at[7 + i], cs_recv.at[7 + i]) for i in range(3)]
    swap_i = [CoreSwap(pi.at[i], fi.at[i], T, cs_send.at[1 + i], cs_recv.at[1 + i]) for i in range(2)]
    swap_o = CoreSwap(po, fo, T, cs_send.at[3], cs_recv.at[3])
    swap_q = [CoreSwap(pq.at[i], fq.at[i], T, cs_send.at[4 + i], cs_recv.at[4 + i]) for i in range(3)]

    ticks = {name: item.stages() for name, item in items.items()}
    ran = set()

    def point(name):
        for step in SCHEDULE.get(name, ()):
            ran.add(step)
            ticks[step[0]][step[1] - 1]()

    met = enter(S, C)
    out_move = Ungroup(outv, out_o, rg_send.at[0], rg_recv.at[0], rg_local.at[0], C, G)
    smg[...] = smg_i[...]

    def feed_forward(act, dgel, wu, wi, h, n1, f1, flow):
        loads = [
            pltpu.make_async_copy(src, dst, in_sem.at[i])
            for i, (src, dst) in enumerate(
                ((gb_i, gb), (act_i, act), (wu_i, wu), (dgel_i, dgel), (flow_i, flow), (wi_i, wi), (gsec_i, gsec),
                 (n1_i, n1), (f1_i, f1))
            )
        ]
        for copy in loads:
            copy.start()
        loads[0].wait()
        loads[1].wait()

        met()
        out_move.start()
        for i in range(3):

            def outer_grad(owner, i=i):
                block = dotg(act[:, span(owner * RU + i * cut, cut)], gb[...], 0, 0).astype(bf16)
                for e in range(2):
                    pu[i, e, tile(owner, cut), :] = block[:, e * H : (e + 1) * H]
                swap_u[i].start(owner)

            loop(S, outer_grad)
        swap_u[0].add()
        point("outer")
        for copy in loads[2:5]:
            copy.wait()

        def inner_grad(i, half, send):
            where = half * (FF // 2) + i * D
            cols = span(where, D)
            h[...] = dotg(gb[...], wu[span(where, D), :], 1, 1)

            def through(k, sums):
                rows = tile(k, RB)
                low = (h[rows, :] * dgel[rows, cols].astype(f32)).astype(bf16)
                act[rows, cols] = low
                return sums + colsum(low.astype(f32))

            sums = lax.fori_loop(0, L // RB, through, jnp.zeros((1, D), f32))
            smg[pl.ds(IB + half * (FF // 2 // D) + i, 1), :] = sums

            def grad(k):
                rows = tile(k, T)
                pi[i, half, rows, :] = dotg(flow[:, rows], act[:, cols], 0, 0).astype(bf16)
                if send:
                    swap_i[i].start(k)

            loop(D // T, grad)

        inner_grad(0, 1 - core, True)
        swap_u[1].add()
        swap_u[2].add()
        point("ffn0")
        inner_grad(0, core, False)
        point("ffn1")
        inner_grad(1, 1 - core, True)
        swap_i[0].add()
        point("ffn2")
        inner_grad(1, core, False)
        swap_i[1].add()
        point("ffn3")
        loads[5].wait()
        loads[6].wait()

        def first_grad(i):
            cols = tile(i, T)
            gsec[:, cols] += dotg(act[...], wi[cols, :], 1, 1)

        loop(D // T, first_grad)
        point("first")
        loads[7].wait()
        loads[8].wait()

        def first_back(k):
            rows = tile(k, RB)
            g, normed = gsec[rows, :], n1[rows, :]
            smg[FG : FG + 1, :] += colsum(g * normed)
            smg[FS : FS + 1, :] += colsum(g)
            back = norm_back(g, sm[FG : FG + 1, :], normed, f1[rows, :])
            gsec[rows, :] = back
            low = back.astype(bf16)
            gb[rows, :] = low
            smg[OB : OB + 1, :] += colsum(low.astype(f32))

        loop(L // RB, first_back)

    V = pltpu.VMEM
    pl.run_scoped(
        feed_forward, V((L, FF), bf16), V((L, FF), bf16), V((FF, D), bf16), V((D, FF), bf16), V((L, D), f32),
        V((L, D), f32), V((L, 1), f32), V((L, D), bf16),
    )
    point("norm")

    def context_back(wo, ctx, ctxt):
        loads = [
            pltpu.make_async_copy(src, dst, in_sem.at[i])
            for i, (src, dst) in enumerate(((ctx_i, ctx), (wo_i, wo), (ctxt_i, ctxt)))
        ]
        for copy in loads:
            copy.start()
        loads[0].wait()

        def out_grad(k):
            rows = tile(k, T)
            block = dotg(ctx[:, rows], gb[...], 0, 0).astype(bf16)
            for e in range(2):
                po[e, rows, :] = block[:, e * (D // 2) : (e + 1) * (D // 2)]
            swap_o.start(k)

        loop(D // T, out_grad)
        loads[1].wait()
        loads[2].wait()

        def back(k):
            grad = dotg(gb[...], wo[tile(k, T), :], 1, 1).astype(bf16)
            for u in range(T // 128):
                hp = k * (T // 128) + u
                mine = grad[:, u * 128 : (u + 1) * 128]
                turned = mine.T
                grad_o[hp] = mine
                grad_ot[hp] = turned
                both = turned.astype(f32) * ctxt[hp]
                for e in range(2):
                    delta[hp, e : e + 1, :] = colsum(both[e * HEAD_DIM : (e + 1) * HEAD_DIM])

        loop(D // T, back)

    pl.run_scoped(context_back, V((D, D), bf16), V((L, D), bf16), V((NP, 128, L), f32))
    swap_o.add()
    point("context")

    def attention(wq, xs, q, kb, vb, pb, own_k, own_v, stage, land, grads, dqt, turned_q):
        loads = [
            pltpu.make_async_copy(src, dst, in_sem.at[i])
            for i, (src, dst) in enumerate(
                ((q_i, q), (xs_i, xs))
            )
        ]
        groups = [(0, 2), (2, 2), (4, 2)]

        def weight_cols(first, count):
            return [
                pltpu.make_async_copy(
                    wq_i.at[:, pl.ds(a * D + first * 128, count * 128)],
                    wq.at[:, pl.ds(3 * first * 128 + a * count * 128, count * 128)],
                    wq_sem.at[first, a],
                )
                for a in range(3)
            ]

        def kv_load(hp):
            slot = lax.rem(hp, 2)
            return [
                pltpu.make_async_copy(src.at[:, hp], dst.at[slot], kv_sem.at[i, slot])
                for i, (src, dst) in enumerate(((k_i, kb), (v_i, vb)))
            ]

        def p_load(t):
            d = lax.rem(lax.rem(t, M) + 1, M)
            return pltpu.make_async_copy(p_i.at[lax.div(t, M), d], pb.at[lax.rem(t, 2)], p_sem.at[lax.rem(t, 2)])

        for copy in kv_load(0) + [p_load(0)] + loads:
            copy.start()
        for first, count in groups:
            for copy in weight_cols(first, count):
                copy.start()
        loads[0].wait()
        row_of = lax.broadcasted_iota(jnp.int32, (128, L), 0)
        lane_of = lax.broadcasted_iota(jnp.int32, (L, 128), 1)

        def send_back(hp, d):
            slot = lax.rem(hp, 2)
            return remote(
                stage.at[slot, d - 1], land_o.at[hp, d - 1], dkv_send.at[slot, d - 1], dkv_recv.at[hp, d - 1],
                ctx=group + lax.rem(m + d, M),
            )

        def chunk(hp, slot, d, put):
            j = lax.rem(m + d, M)
            t = hp * M + lax.rem(d - 1 + M, M)
            p_load(t).wait()

            @pl.when(t + 1 < NP * M)
            def _():
                p_load(t + 1).start()

            def block(ks, qs, kn, qn):
                key, value = kb[slot, j, ks, :], vb[slot, j, ks, :]
                turned = key.T
                query, up, up_t = q[hp, qs, :], grad_o[hp, qs, :], grad_ot[hp, :, qs]
                row_of = lax.broadcasted_iota(jnp.int32, (128, qn), 0)
                lane_of = lax.broadcasted_iota(jnp.int32, (qn, 128), 1)
                sums = []
                for e in range(2):
                    rows = (row_of < HEAD_DIM) if e == 0 else (row_of >= HEAD_DIM)
                    lanes = (lane_of < HEAD_DIM) if e == 0 else (lane_of >= HEAD_DIM)
                    zero, zero_t = jnp.zeros_like(query), jnp.zeros_like(up_t)
                    probs = pb[lax.rem(t, 2), e, ks, qs].astype(f32) * fac[d, hp, e : e + 1, qs]
                    dprobs = dotf(value, jnp.where(rows, up_t, zero_t))
                    dscores = (probs * (dprobs - delta[hp, e : e + 1, qs])).astype(bf16)
                    sums.append(
                        (
                            dotf(dscores, jnp.where(lanes, query, zero)),
                            dotf(probs.astype(bf16), jnp.where(lanes, up, zero)),
                        )
                    )
                    head = slice(e * HEAD_DIM, (e + 1) * HEAD_DIM)
                    dqt[head, qs] += dotf(turned[head], dscores)
                put(ks, sums[0][0] + sums[1][0], sums[0][1] + sums[1][1])

            if M == 2 and not isinstance(d, int):
                near, far = span(m * (L // 2), L // 2), span((1 - m) * (L // 2), L // 2)
                block(near, pl.ds(0, L), L // 2, L)
                block(far, far, L // 2, L // 2)
            else:
                block(pl.ds(0, L), pl.ds(0, L), L, L)

        def pair(hp, between):
            slot = lax.rem(hp, 2)
            for copy in kv_load(hp):
                copy.wait()

            @pl.when(hp + 1 < NP)
            def _():
                for copy in kv_load(hp + 1):
                    copy.start()

            dqt[...] = jnp.zeros(dqt.shape, f32)

            def far(d, carry):
                @pl.when(hp >= 2)
                def _():
                    send_back(hp - 2, d).wait_send()

                def put(ks, dk, dv):
                    stage[slot, d - 1, 0, ks, :] = dk.astype(bf16)
                    stage[slot, d - 1, 1, ks, :] = dv.astype(bf16)

                chunk(hp, slot, d, put)
                send_back(hp, d).start()
                return carry

            lax.fori_loop(1, M, far, 0)
            between()

            def put_own(ks, dk, dv):
                own_k[slot, ks, :] = dk
                own_v[slot, ks, :] = dv

            chunk(hp, slot, 0, put_own)
            turned_q[slot] = (dqt[...] * HEAD_DIM**-0.5).T.astype(bf16)

        def fetched(first, count):
            return pltpu.make_async_copy(land_o.at[pl.ds(first, count)], land.at[pl.ds(0, count)], land_sem.at[0])

        def fetch(first, count):
            for u in range(count):
                for d in range(1, M):
                    send_back(first + u, d).wait_recv()
            if M > 1:
                fetched(first, count).start()

        def project_back(first, count):
            if M > 1:
                fetched(first, count).wait()
            W = count * 128
            for u in range(count):
                slot = (first + u) % 2
                dk, dv = own_k[slot], own_v[slot]
                for d in range(1, M):
                    dk = dk + land[u, d - 1, 0].astype(f32)
                    dv = dv + land[u, d - 1, 1].astype(f32)
                grads[:, u * 128 : (u + 1) * 128] = turned_q[slot]
                grads[:, W + u * 128 : W + (u + 1) * 128] = dk.astype(bf16)
                grads[:, 2 * W + u * 128 : 2 * W + (u + 1) * 128] = dv.astype(bf16)
            cols = slice(first * 128, first * 128 + W)
            smg[QB : QB + 1, cols] = colsum(grads[:, 0:W].astype(f32))
            smg[VB : VB + 1, cols] = colsum(grads[:, 2 * W : 3 * W].astype(f32))

            def weight(k):
                rows = tile(k, T)
                block = dotg(xs[:, rows], grads[...], 0, 0).astype(bf16)
                for a in range(3):
                    for e in range(2):
                        pq[first // 2, e, rows, a * 128 : (a + 1) * 128] = block[
                            :, a * W + e * 128 : a * W + (e + 1) * 128
                        ]
                swap_q[first // 2].start(k)

            loop(D // T, weight)

        def input_back(first, count):
            for copy in weight_cols(first, count):
                copy.wait()
            W = 3 * count * 128
            base = 3 * first * 128

            def back(k):
                rows = tile(k, T)
                gsec[:, rows] += dotg(grads[:, 0:W], wq[rows, base : base + W], 1, 1)

            loop(D // T, back)

        def drain_stage():
            for hp in (NP - 2, NP - 1):
                for d in range(1, M):
                    send_back(hp, d).wait_send()

        def pair_group(first, count):
            def body(u):
                def here(name):
                    for k in range(count):

                        @pl.when(u == k)
                        def _():
                            point(f"{name}{first + k}")

                pair(first + u, lambda: here("far"))
                here("pair")

            loop(count, body)

        for g, (first, count) in enumerate(groups[:2]):
            pair_group(first, count)
            fetch(first, count)
            if g == 0:
                loads[1].wait()
            project_back(first, count)
            point(f"project{g}")
            input_back(first, count)
            swap_q[g].add()
            point(f"input{g}")
        pair_group(*groups[2])
        fetch(*groups[2])
        project_back(*groups[2])

        width = D // S
        ps[...] = jnp.zeros(ps.shape, bf16)
        share = FF // S
        for owner in range(S):
            ps[owner, 0, 0:8, 0:width] = smg[0:8, owner * width : (owner + 1) * width].astype(bf16)
            for r in range(share // width):
                start = owner * share + r * width
                a, b = start // D, start % D
                ps[owner, 1, r : r + 1, 0:width] = smg[IB + a : IB + a + 1, b : b + width].astype(bf16)
        items["s"].start()
        point("project2")
        input_back(*groups[2])
        for r in range(L // PP):
            rows = pl.ds(r * PP, PP)
            grads[rows, :] = gsec[rows, :].astype(bf16)
        swap_q[2].add()
        gin_move = Ungroup(grads, gin_o, rg_send.at[1], rg_recv.at[1], rg_local.at[1], C, G)
        for j in range(G):
            ticks[f"g{j}"] = [functools.partial(gin_move.start, j)]
        point("input2")
        point("end")
        assert ran == {(name, i + 1) for name in ticks for i in range(len(ticks[name]))}
        gin_move.finish()
        gin_move.drain()
        drain_stage()

    pl.run_scoped(
        attention, V((D, 3 * D), bf16), V((L, D), bf16), V((NP, L, 128), bf16),
        V((2, M, L, 128), bf16), V((2, M, L, 128), bf16), V((2, 2, L, L), bf16),
        V((2, L, 128), f32), V((2, L, 128), f32), V((2, max(M - 1, 1), 2, L, 128), bf16),
        V((2, max(M - 1, 1), 2, L, 128), bf16), V((L, 3 * T), bf16), V((128, L), f32),
        V((2, L, 128), bf16),
    )
    out_move.finish()
    out_move.drain()
    for item in items.values():
        item.finish()
        item.drain()
    for swap in swap_u + swap_i + [swap_o] + swap_q:
        swap.drain()


def backward_call(S, C, G, PP, saved):
    (xs, wq, wo, wi, wu, k, v, q, _, p, fac, ctxt, ctx, n1, f1, flow, act, dgel, gsec, gb, outv, smg, sm) = saved
    L, D = xs.shape
    M, NP, FF = C // G, D // 128, wi.shape[1]
    R, RU = D // S, FF // S
    sds = jax.ShapeDtypeStruct
    land = max(M - 1, 1)
    H, SR, SW = D // 2, 32, 256
    outs = [
        ((G, PP, D), bf16), ((G, PP, D), bf16), ((R, 3 * D), bf16), ((R, D), bf16), ((R, FF), bf16), ((RU, D), bf16),
        ((NP, land, 2, L, 128), bf16), ((2, SR // 2, SW), bf16),
    ]
    cut = RU // 3
    scratch = [
        (3, 2, S * cut, H), (2, 2, D, D), (2, D, H), (3, 2, D, H), (S, 2, SR // 2, SW),
        (3, S * cut, H), (2, D, D), (D, H), (3, D, H), (S, SR // 2, SW),
        (3, 2, S - 1, cut // 2, H), (7, 2, S - 1, R // 2, H), (3, 2, S - 1, R // 2, 128), (S - 1, SR // 2, SW),
        (3, cut, H), (7, R, H), (3, R, 128), (3, cut, H), (7, R, H), (3, R, 128),
        (C // 2, SR // 2, SW), (SR // 2, SW),
    ]
    scratch = [(x, bf16) for x in scratch] + [
        ((L, D), f32), ((L, D), bf16), ((NP, L, 128), bf16), ((NP, 128, L), bf16), ((NP, 2, L), f32), ((16, D), f32),
    ]
    dma = pltpu.SemaphoreType.DMA
    sems = [
        dma((10, 8)), dma((10, 8)), dma((1, 1)), dma((1, 1)), dma((1, S - 1)), dma((1, S - 1)), dma((1, C // 2)), dma((1, C // 2)),
        dma((16, 3)), dma((16, 3)), dma((16, 2, S - 1)), dma((16, 2, S - 1)), dma((16, 2)),
        dma((16, 2)),
        dma((2, G)), dma((2, G)), dma((2,)), dma((10,)), dma((NP, 3)), dma((2, 2)), dma((2,)), dma((2, land)), dma((NP, land)), dma((1,)),
        dma((16, 3)),
    ]
    results = pl.pallas_call(
        functools.partial(backward_kernel, (S, C, G, PP)),
        out_shape=[sds(*o) for o in outs],
        in_specs=[ANY] * 19 + [VMEM] * 3,
        out_specs=[ANY] * len(outs),
        scratch_shapes=[pltpu.VMEM(*x) for x in scratch] + sems,
        compiler_params=pltpu.CompilerParams(
            collective_id=1, has_side_effects=True, vmem_limit_bytes=62 << 20
        ),
        name="backward",
    )(outv, gsec, gb, act, dgel, wu, wi, wo, wq, flow, n1, f1, xs, ctx, ctxt, q, k, v, p, fac, smg, sm)
    return results


def solution(mesh):
    S, C = mesh.shape["seq"], mesh.shape["ctx"]

    def on_device(
        hid, cot, seg, wq, qb, vb, wo, ob, fg, fs, wi, ib, wu, ub, sg, ss
    ):
        G, PP, D = hid.shape
        saved = forward_call(S, C, hid, cot, seg.reshape(G, 1, PP), wq, wo, wi, wu, [qb, vb, ob, fg, fs, ub, sg, ss, ib])
        out, gin, gq, go, gi, gu, _, gs = backward_call(S, C, G, PP, saved)
        gu, gi, gq, go, gin, out = widen([gu, gi, gq, go, gin.reshape(G * PP, D)], out.reshape(G * PP, D))
        gs = gs.reshape(-1, gs.shape[-1]).astype(f32)
        width = D // S
        row = lambda r: gs[r, :width]
        grad_ib = gs[16 : 16 + ib.shape[0] // width, :width].reshape(-1)
        return (
            out.reshape(G, PP, D), gin.reshape(G, PP, D), gq, row(QB), row(VB), go, row(OB), row(FG), row(FS), gi,
            grad_ib, gu, row(UB), row(SG), row(SS),
        )

    rows, matrix, vector = P("seq", "ctx", None), P("seq", None), P("seq")
    return jax.shard_map(
        on_device,
        mesh=mesh,
        in_specs=(
            rows, rows, P("seq", "ctx"), matrix, vector, vector, matrix, vector, vector, vector, matrix, vector,
            matrix, vector, vector, vector,
        ),
        out_specs=(
            rows, rows, matrix, vector, vector, matrix, vector, vector, vector, matrix, vector, matrix, vector,
            vector, vector,
        ),
        check_vma=False,
    )
```

```python
import functools

import jax
import jax.numpy as jnp
from jax import lax
from jax.experimental import pallas as pl
from jax.experimental.pallas import tpu as pltpu
from jax.sharding import PartitionSpec as P

HEAD_DIM = 64
EPS = 1e-12
NEG = -1e30
RB = 64
ROOT_HALF = 0.7071067811865476
PDF_SCALE = 0.3989422804014327
f32 = jnp.float32
bf16 = jnp.bfloat16
MESH = pl.DeviceIdType.MESH
ANY = pl.BlockSpec(memory_space=pl.ANY)
VMEM = pl.BlockSpec(memory_space=pltpu.VMEM)

QB, VB, OB, FG, FS, UB, SG, SS, IB = 0, 1, 2, 3, 4, 5, 6, 7, 8


def tile(i, width):
    return pl.ds(pl.multiple_of(i * width, width), width)


def span(start, width, unit=128):
    return pl.ds(pl.multiple_of(start, unit), width)


def dotf(a, b):
    return jnp.dot(a, b, preferred_element_type=f32)


def dotg(a, b, ca, cb):
    return lax.dot_general(a, b, (((ca,), (cb,)), ((), ())), preferred_element_type=f32)


def remote(src, dst, send_sem, recv_sem, **where):
    return pltpu.make_async_remote_copy(
        src_ref=src,
        dst_ref=dst,
        send_sem=send_sem,
        recv_sem=recv_sem,
        device_id=where,
        device_id_type=MESH,
    )


def enter(S, C):
    s, c = lax.axis_index("seq"), lax.axis_index("ctx")
    barrier = pltpu.get_barrier_semaphore()
    for d in range(1, S):
        pl.semaphore_signal(
            barrier, inc=1, device_id={"seq": lax.rem(s + d, S)}, device_id_type=MESH
        )

    def greet(d, carry):
        pl.semaphore_signal(
            barrier, inc=1, device_id={"ctx": lax.rem(c + d, C)}, device_id_type=MESH
        )
        return carry

    lax.fori_loop(1, C, greet, 0)

    def wait():
        pl.semaphore_wait(barrier, S - 1 + C - 1)

    return wait


def bit_orders(S):
    bits = [1 << k for k in range(S.bit_length() - 1)]
    return (bits, bits[1:] + bits[:1])


def subsets(bits):
    out = [0]
    for b in bits:
        out = out + [o | b for o in out]
    return out


class Gather:
    def __init__(self, S, shard, full, send, recv, swap_send, swap_recv, local):
        self.S, self.shard, self.full = S, shard, full
        self.send, self.recv, self.local = send, recv, local
        self.swap_send, self.swap_recv = swap_send, swap_recv
        self.R, self.N = shard.shape
        self.s, self.c = lax.axis_index("seq"), lax.axis_index("ctx")
        self.cols = span(lax.rem(self.c, 2) * (self.N // 2), self.N // 2)
        self.orders = bit_orders(S)
        self.steps = len(self.orders[0])
        self.half = self.R // 2

    def block(self, owner, p):
        return self.full.at[span(owner * self.R + p * self.half, self.half, 16), self.cols]

    def copy_own(self):
        return pltpu.make_async_copy(
            self.shard, self.full.at[span(self.s * self.R, self.R, 16), :], self.local
        )

    def copies(self, t, direct):
        out = []
        for p in range(2):
            order = self.orders[p]
            for i, mask in enumerate(subsets(order[:t])):
                if (mask == 0) == direct:
                    owner = jnp.bitwise_xor(self.s, mask)
                    src = self.block(owner, p)
                    if mask == 0:
                        src = self.shard.at[pl.ds(p * self.half, self.half), self.cols]
                    k = (1 << t) - 1 + i
                    peer = jnp.bitwise_xor(self.s, order[t])
                    out.append(remote(src, self.block(owner, p), self.send.at[p, k], self.recv.at[p, k], seq=peer))
        return out

    def swaps(self, t, direct):
        out = []
        for p in range(2):
            order = self.orders[p]
            for i, mask in enumerate(subsets(order[:t])):
                if (mask == 0) == direct:
                    got = self.block(jnp.bitwise_xor(self.s, order[t] ^ mask), p)
                    k = (1 << t) - 1 + i
                    out.append(
                        remote(
                            got, got, self.swap_send.at[p, k], self.swap_recv.at[p, k], ctx=jnp.bitwise_xor(self.c, 1)
                        )
                    )
        return out

    def start(self):
        for t in range(self.steps):
            for copy in self.copies(t, True):
                copy.start()
        self.copy_own().start()

    def pass_on(self, t):
        for copy in self.copies(t, False):
            copy.start()

    def arrive(self, t, direct):
        for copy in self.copies(t, direct):
            copy.wait_recv()
        for copy in self.swaps(t, direct):
            copy.start()

    def first(self):
        self.arrive(0, True)
        self.pass_on(1)

    def middle(self):
        for t in range(1, self.steps):
            self.arrive(t, True)
            if t + 1 < self.steps:
                self.arrive(t, False)
                self.pass_on(t + 1)

    def last(self):
        self.arrive(self.steps - 1, False)

    def ready(self, early, late):
        if early:
            self.copy_own().wait()
        for t in range(self.steps):
            for direct in (True, False):
                final = t == self.steps - 1 and not direct
                if late if final else early:
                    for copy in self.swaps(t, direct):
                        copy.wait_recv()

    def drain(self):
        for t in range(self.steps):
            for direct in (True, False):
                for copy in self.copies(t, direct) + self.swaps(t, direct):
                    copy.wait_send()


class PairGather(Gather):
    def __init__(self, S, shard, full, send, recv, swap_send, swap_recv, local, pair_sems):
        super().__init__(S, shard, full, send, recv, swap_send, swap_recv, local)
        self.pair_send, self.pair_recv, self.late_send, self.late_recv = pair_sems
        core, odd, width = lax.rem(self.c, 2), lax.rem(lax.div(self.c, 2), 2), self.N // 4
        self.cols = span((2 * core + odd) * width, width)
        self.late_cols = span((2 * core + 1 - odd) * width, width)
        self.quarters = [2 * core + odd, 2 * (1 - core) + odd, 2 * core + 1 - odd, 2 * (1 - core) + 1 - odd]

    def late_block(self, owner, p):
        return self.full.at[span(owner * self.R + p * self.half, self.half, 16), self.late_cols]

    def arrived(self, t, direct):
        for p in range(2):
            order = self.orders[p]
            for i, mask in enumerate(subsets(order[:t])):
                if (mask == 0) == direct:
                    yield p, (1 << t) - 1 + i, jnp.bitwise_xor(self.s, order[t] ^ mask)

    def pair_copies(self, t, direct):
        return [
            remote(
                self.block(owner, p), self.block(owner, p), self.pair_send.at[p, k], self.pair_recv.at[p, k],
                ctx=jnp.bitwise_xor(self.c, 2),
            )
            for p, k, owner in self.arrived(t, direct)
        ]

    def late_swaps(self, t, direct):
        return [
            remote(
                self.late_block(owner, p), self.late_block(owner, p), self.late_send.at[p, k], self.late_recv.at[p, k],
                ctx=jnp.bitwise_xor(self.c, 1),
            )
            for p, k, owner in self.arrived(t, direct)
        ]

    def arrive(self, t, direct):
        super().arrive(t, direct)
        for copy in self.pair_copies(t, direct):
            copy.start()

    def every(self):
        return [(t, direct) for t in range(self.steps) for direct in (True, False)]

    def late(self):
        for which in self.every():
            for copy in self.pair_copies(*which):
                copy.wait_recv()
            for copy in self.late_swaps(*which):
                copy.start()

    def late_ready(self):
        for which in self.every():
            for copy in self.late_swaps(*which):
                copy.wait_recv()

    def drain(self):
        super().drain()
        for which in self.every():
            for copy in self.pair_copies(*which) + self.late_swaps(*which):
                copy.wait_send()


class Regroup:
    def __init__(self, src, dst, send, recv, local, C, G):
        self.src, self.dst, self.send, self.recv, self.local = src, dst, send, recv, local
        self.G, self.M = G, C // G
        self.c = lax.axis_index("ctx")

    def dst_at(self, j):
        if len(self.dst.shape) == 2:
            rows = self.src.shape[1]
            return self.dst.at[tile(j, rows), :]
        return self.dst.at[j]

    def each(self, on_remote, on_local):
        place = lax.rem(self.c, self.G)
        for g in range(self.G):
            target = g * self.M + lax.div(self.c, self.G)
            far = remote(
                self.src.at[g], self.dst_at(place), self.send.at[g], self.recv.at[place], ctx=target
            )
            near = pltpu.make_async_copy(self.src.at[g], self.dst_at(place), self.local)

            @pl.when(target != self.c)
            def _():
                on_remote(far)

            @pl.when(target == self.c)
            def _():
                on_local(near)

    def start(self):
        self.each(lambda far: far.start(), lambda near: near.start())

    def drain(self):
        self.each(lambda far: far.wait_send(), lambda near: None)

    def finish(self):
        m = lax.rem(self.c, self.M)
        for j in range(self.G):
            source = m * self.G + j

            @pl.when(source != self.c)
            def _():
                remote(
                    self.src.at[0], self.dst_at(j), self.send.at[0], self.recv.at[j], ctx=source
                ).wait_recv()

            @pl.when(source == self.c)
            def _():
                pltpu.make_async_copy(self.src.at[0], self.dst_at(j), self.local).wait()


class Ungroup:
    def __init__(self, src, dst, send, recv, local, C, G):
        self.src, self.dst, self.send, self.recv, self.local = src, dst, send, recv, local
        self.G, self.M, self.P = G, C // G, dst.shape[1]
        self.c = lax.axis_index("ctx")

    def each(self, on_remote, on_local, only=None):
        g, m = lax.div(self.c, self.M), lax.rem(self.c, self.M)
        for j in range(self.G) if only is None else (only,):
            target = m * self.G + j
            rows = self.src.at[pl.ds(j * self.P, self.P), :]
            far = remote(rows, self.dst.at[g], self.send.at[j], self.recv.at[g], ctx=target)
            near = pltpu.make_async_copy(rows, self.dst.at[g], self.local)

            @pl.when(target != self.c)
            def _():
                on_remote(far)

            @pl.when(target == self.c)
            def _():
                on_local(near)

    def start(self, only=None):
        self.each(lambda far: far.start(), lambda near: near.start(), only)

    def drain(self):
        self.each(lambda far: far.wait_send(), lambda near: None)

    def finish(self):
        rows = self.src.at[pl.ds(0, self.P), :]
        for g in range(self.G):
            source = g * self.M + lax.div(self.c, self.G)

            @pl.when(source != self.c)
            def _():
                remote(
                    rows, self.dst.at[g], self.send.at[0], self.recv.at[g], ctx=source
                ).wait_recv()

            @pl.when(source == self.c)
            def _():
                pltpu.make_async_copy(rows, self.dst.at[g], self.local).wait()


def mask_bias(seg_keys, seg_queries, bias, G, PP):
    rows = [seg_queries[i].astype(f32) for i in range(G)]
    for a in range(G):
        column = jnp.broadcast_to(seg_keys[a].astype(f32), (PP, PP)).T
        for b in range(G):
            bias[a * PP : (a + 1) * PP, b * PP : (b + 1) * PP] = jnp.where(
                column == rows[b], jnp.zeros((PP, PP), f32), jnp.full((PP, PP), NEG, f32)
            ).astype(bias.dtype)


def norm_rows(x):
    centred = x - jnp.mean(x, axis=-1, keepdims=True)
    factor = lax.rsqrt(jnp.mean(centred * centred, axis=-1, keepdims=True) + EPS)
    return centred * factor, factor


def norm_back(g, gain, normed, factor):
    h = g * gain
    return factor * (
        h
        - jnp.mean(h, axis=-1, keepdims=True)
        - normed * jnp.mean(h * normed, axis=-1, keepdims=True)
    )


def loop(n, body):
    def step(i, carry):
        body(i)
        return carry

    lax.fori_loop(0, n, step, 0)


def colsum(x):
    return jnp.sum(x, axis=0, keepdims=True)


def forward_kernel(
    dims,
    hid, cot, seg, wq_s, wo_s, wi_s, wu_s, qb, vb, ob, fg, fs, ub, sg, ss, ib,
    xs_o, wq_o, wo_o, wi_o, wu_o, k_o, v_o, q_o, seg_o, p_o, fac_o, ctxt_o, ctx_o,
    n1_o, f1_o, flow_o, act_o, dgel_o, gsec_o, gb_o, out_o, smg_o, sm_o,
    xs, ct, wq, wo, wi, wu, small_all, segc, segk, q, qt, kown, vown, kc, vc, bias, pst, m_s, l_s, ctxt, ctx,
    first, n1, f1, flow, h, h2, act, dgel, n2, gsec, gb, outv,
    ag_send, ag_recv, sw_send, sw_recv, pair_sem, ag_local, rg_send, rg_recv, rg_local, sm_send, sm_recv,
    kv_send, kv_recv, kv_local, kc_sem, p_sem, out_sem,
):
    S, C, G, PP = dims
    M, L, D = C // G, G * PP, hid.shape[2]
    FF = wi.shape[1]
    NP = D // 128
    T = 256
    s, c = lax.axis_index("seq"), lax.axis_index("ctx")
    m = lax.rem(c, M)

    def gather(kind, w, shard, full, *more):
        sems = [a.at[w] for a in (ag_send, ag_recv, sw_send, sw_recv, ag_local)]
        return kind(S, shard, full, *sems, *more)

    gathers = [
        gather(Gather, 0, wq_s, wq),
        gather(Gather, 1, wo_s, wo),
        gather(PairGather, 2, wi_s, wi, [pair_sem.at[i] for i in range(4)]),
        gather(Gather, 3, wu_s, wu),
    ]
    gq, go, gi, gu = gathers
    pending = []

    def put(src, dst):
        copy = pltpu.make_async_copy(src, dst, out_sem.at[len(pending)])
        copy.start()
        pending.append(copy)

    enter(S, C)()
    hid_move = Regroup(hid, xs, rg_send.at[0], rg_recv.at[0], rg_local.at[0], C, G)
    cot_move = Regroup(cot, ct, rg_send.at[1], rg_recv.at[1], rg_local.at[1], C, G)
    seg_move = Regroup(seg, segc, rg_send.at[2], rg_recv.at[2], rg_local.at[2], C, G)
    seg_move.start()
    hid_move.start()
    gq.start()
    width, share = D // S, FF // S
    small = small_all.at[s]
    small[...] = jnp.zeros(small.shape, bf16)
    for r, vector in enumerate((qb, vb, ob, fg, fs, ub, sg, ss)):
        small[r : r + 1, 0:width] = vector[...].reshape(1, width)
    for r in range(share // width):
        small[IB + r : IB + r + 1, 0:width] = ib[r * width : (r + 1) * width].reshape(1, width)
    small_copies = [
        remote(small, small, sm_send.at[d - 1], sm_recv.at[s], seq=jnp.bitwise_xor(s, d))
        for d in range(1, S)
    ]
    for copy in small_copies:
        copy.start()
    seg_move.finish()

    group = lax.div(c, M) * M
    seg_own = pltpu.make_async_copy(segc, seg_o.at[m], kv_local.at[2])
    seg_own.start()

    def peer(d):
        return group + lax.rem(m + d, M)

    def kv_copies(d):
        return [
            remote(src, dst.at[m], kv_send.at[i, d], kv_recv.at[i, m], ctx=peer(d))
            for i, (src, dst) in enumerate(((kown, k_o), (vown, v_o), (segc, seg_o)))
        ]

    def kv_arrivals(d):
        j = lax.rem(m + d, M)
        return [
            remote(src, dst.at[j], kv_send.at[i, d], kv_recv.at[i, j], ctx=peer(d))
            for i, (src, dst) in enumerate(((kown, k_o), (vown, v_o), (segc, seg_o)))
        ]

    for d in range(1, M):
        kv_copies(d)[2].start()

    for d in range(1, S):
        far = jnp.bitwise_xor(s, d)
        remote(small, small_all.at[far], sm_send.at[d - 1], sm_recv.at[far], seq=far).wait_recv()
    sm_o[...] = jnp.zeros(sm_o.shape, f32)
    for owner in range(S):
        block = small_all[owner].astype(f32)
        sm_o[0:IB, owner * width : (owner + 1) * width] = block[0:IB, 0:width]
        for r in range(share // width):
            start = owner * share + r * width
            a, b = start // D, start % D
            sm_o[IB + a : IB + a + 1, b : b + width] = block[IB + r : IB + r + 1, 0:width]
    mask_bias(segc, segc, bias, G, PP)
    gq.first()
    go.start()
    gi.start()
    gq.middle()
    gq.last()
    hid_move.finish()
    put(xs, xs_o)
    gq.ready(True, True)
    put(wq, wq_o)

    def project(i):
        cols = tile(i, T)
        qv = dotf(xs[...], wq[:, cols]) + sm_o[QB : QB + 1, cols]
        kv = dotf(xs[...], wq[:, span(D + i * T, T)])
        vv = dotf(xs[...], wq[:, span(2 * D + i * T, T)]) + sm_o[VB : VB + 1, cols]
        qs = (qv.astype(bf16).astype(f32) * HEAD_DIM**-0.5).astype(bf16)
        kv, vv = kv.astype(bf16), vv.astype(bf16)
        for u in range(T // 128):
            lanes = slice(u * 128, (u + 1) * 128)
            hp = i * (T // 128) + u
            q[hp] = qs[:, lanes]
            qt[hp] = qs[:, lanes].T
            kown[hp] = kv[:, lanes]
            vown[hp] = vv[:, lanes]

    loop(D // T, project)
    for d in range(1, M):
        for copy in kv_copies(d)[:2]:
            copy.start()
    own_kv = [
        pltpu.make_async_copy(kown, k_o.at[m], kv_local.at[0]),
        pltpu.make_async_copy(vown, v_o.at[m], kv_local.at[1]),
    ]
    for copy in own_kv:
        copy.start()
    put(q, q_o)
    go.first()
    gi.first()
    gu.start()

    row_of = lax.broadcasted_iota(jnp.int32, (128, L), 0)

    def keep_probs(hp, d):
        slot = lax.rem(hp, 2)
        return pltpu.make_async_copy(pst.at[slot], p_o.at[hp, d], p_sem.at[slot])

    def reachable(keys, values, hp, d, slot):
        near, far = span(m * (L // 2), L // 2), span((1 - m) * (L // 2), L // 2)
        qv, qf = qt[hp], qt[hp, :, far]
        vn, vf = values[hp, near, :].T, values[hp, far, :].T
        low_rows = lax.broadcasted_iota(jnp.int32, (128, L // 2), 0) < HEAD_DIM
        for e in range(2):
            head, one = slice(e * HEAD_DIM, (e + 1) * HEAD_DIM), slice(e, e + 1)
            mine = (row_of < HEAD_DIM) if e == 0 else (row_of >= HEAD_DIM)
            mine_far = low_rows if e == 0 else jnp.logical_not(low_rows)
            s_near = dotf(keys[hp, near, :], jnp.where(mine, qv, jnp.zeros_like(qv))) + bias[near, :]
            s_far = dotf(keys[hp, far, :], jnp.where(mine_far, qf, jnp.zeros_like(qf))) + bias[far, far]
            old = m_s[d - 1, hp, one, :]
            m_s[d, hp, one, :] = jnp.maximum(old, jnp.max(s_near, axis=0, keepdims=True))
            m_s[d, hp, one, far] = jnp.maximum(m_s[d, hp, one, far], jnp.max(s_far, axis=0, keepdims=True))
            top = m_s[d, hp, one, :]
            keep = jnp.exp(old - top)
            w_near, w_far = jnp.exp(s_near - top), jnp.exp(s_far - m_s[d, hp, one, far])
            low_near, low_far = w_near.astype(bf16), w_far.astype(bf16)
            l_s[hp, one, :] = l_s[hp, one, :] * keep + colsum(w_near)
            l_s[hp, one, far] += colsum(w_far)
            ctxt[hp, head, :] = ctxt[hp, head, :] * keep + dotf(vn[head], low_near)
            ctxt[hp, head, far] += dotf(vf[head], low_far)
            pst[slot, e, near, :] = low_near
            pst[slot, e, far, far] = low_far

    def attend(keys, values, d, extra):
        fresh = isinstance(d, int)

        def pair(hp):
            extra(hp)
            slot = lax.rem(hp, 2)
            if fresh:

                @pl.when(hp >= 2)
                def _():
                    keep_probs(hp, d).wait()

            else:
                keep_probs(hp, d).wait()
            if M == 2 and not fresh:
                reachable(keys, values, hp, d, slot)
                keep_probs(hp, d).start()
                return
            qv, kv, vt, b = qt[hp], keys[hp], values[hp].T, bias[...]
            for e in range(2):
                head = slice(e * HEAD_DIM, (e + 1) * HEAD_DIM)
                mine = (row_of < HEAD_DIM) if e == 0 else (row_of >= HEAD_DIM)
                scores = dotf(kv, jnp.where(mine, qv, jnp.zeros_like(qv))) + b
                top = jnp.max(scores, axis=0, keepdims=True)
                if fresh:
                    weights = jnp.exp(scores - top)
                    low = weights.astype(bf16)
                    m_s[d, hp, e : e + 1, :] = top
                    l_s[hp, e : e + 1, :] = colsum(weights)
                    ctxt[hp, head, :] = dotf(vt[head], low)
                else:
                    old = m_s[d - 1, hp, e : e + 1, :]
                    top = jnp.maximum(old, top)
                    keep = jnp.exp(old - top)
                    weights = jnp.exp(scores - top)
                    low = weights.astype(bf16)
                    m_s[d, hp, e : e + 1, :] = top
                    l_s[hp, e : e + 1, :] = l_s[hp, e : e + 1, :] * keep + colsum(weights)
                    ctxt[hp, head, :] = ctxt[hp, head, :] * keep + dotf(vt[head], low)
                pst[slot, e] = low
            keep_probs(hp, d).start()

        loop(NP, pair)

    def in_own(hp):
        @pl.when(hp == NP - 2)
        def _():
            go.middle()
            go.last()
            gi.middle()

        @pl.when(hp == NP - 1)
        def _():
            gi.last()
            cot_move.start()

    attend(kown, vown, 0, in_own)

    def far_chunk(d, carry):
        j = lax.rem(m + d, M)
        for copy in kv_arrivals(d):
            copy.wait_recv()
        loads = [
            pltpu.make_async_copy(k_o.at[j], kc, kc_sem.at[0]),
            pltpu.make_async_copy(v_o.at[j], vc, kc_sem.at[1]),
            pltpu.make_async_copy(seg_o.at[j], segk, kc_sem.at[2]),
        ]
        for copy in loads:
            copy.start()
        for copy in loads:
            copy.wait()
        mask_bias(segk, segc, bias, G, PP)

        def in_far(hp):
            @pl.when(jnp.logical_and(d == M - 1, hp == NP - 2))
            def _():
                gu.first()

        attend(kc, vc, d, in_far)
        return carry

    lax.fori_loop(1, M, far_chunk, 0)

    def close(hp):
        for e in range(2):
            head = slice(e * HEAD_DIM, (e + 1) * HEAD_DIM)
            share = 1.0 / l_s[hp, e : e + 1, :]
            ctxt[hp, head, :] = ctxt[hp, head, :] * share
            for d in range(M):
                fac_o[d, hp, e : e + 1, :] = jnp.exp(m_s[d, hp, e : e + 1, :] - m_s[M - 1, hp, e : e + 1, :]) * share
        ctx[:, tile(hp, 128)] = ctxt[hp].T.astype(bf16)

    loop(NP, close)

    put(ctxt, ctxt_o)
    put(ctx, ctx_o)
    go.ready(True, True)
    put(wo, wo_o)

    def project_out(i):
        cols = tile(i, T)
        first[:, cols] = dotf(ctx[...], wo[:, cols]) + sm_o[OB : OB + 1, cols]

    loop(D // T, project_out)

    def first_norm(r):
        rows = tile(r, RB)
        normed, factor = norm_rows(first[rows, :] + xs[rows, :].astype(f32))
        y = normed * sm_o[FG : FG + 1, :] + sm_o[FS : FS + 1, :]
        n1[rows, :] = normed
        f1[rows, :] = factor
        first[rows, :] = y
        flow[rows, :] = y.astype(bf16)

    loop(L // RB, first_norm)
    put(n1, n1_o)
    put(f1, f1_o)
    put(flow, flow_o)
    if M == 1:
        gu.first()
    gi.ready(True, True)

    def feed_quarter(now, before):
        def step(k):
            cols = tile(k, T)
            if now is not None:
                number, place = now
                where = gi.quarters[number] * (FF // 4)
                row = lax.div(where, D)
                place[:, cols] = dotf(flow[...], wi[:, span(where + k * T, T)]) + sm_o[pl.ds(IB + row, 1), cols]
            if before is not None:
                number, place = before
                where = gi.quarters[number] * (FF // 4) + k * T
                for r in range(L // RB):
                    rows = pl.ds(r * RB, RB)
                    x = place[rows, cols]
                    share = 0.5 * (1.0 + lax.erf(x * ROOT_HALF))
                    act[rows, span(where, T)] = (x * share).astype(bf16)
                    dgel[rows, span(where, T)] = (
                        share + x * (PDF_SCALE * jnp.exp(-0.5 * x * x))
                    ).astype(bf16)

        loop(FF // 4 // T, step)

    feed_quarter((0, h), None)
    feed_quarter((1, h2), (0, h))
    gi.late()
    feed_quarter((2, h), (1, h2))
    gi.late_ready()
    put(wi, wi_o)
    feed_quarter((3, h2), (2, h))
    feed_quarter(None, (3, h2))
    put(act, act_o)
    put(dgel, dgel_o)
    RU = FF // S

    def feed_out(masks, fresh):
        owners = [jnp.bitwise_xor(s, k) for k in masks]

        def step(i):
            cols = tile(i, T)
            total = sm_o[UB : UB + 1, cols] if fresh else n2[:, cols]
            for owner in owners:
                total = total + dotf(act[:, span(owner * RU, RU)], wu[span(owner * RU, RU), cols])
            n2[:, cols] = total

        loop(D // T, step)

    gu.middle()
    gu.ready(True, False)
    feed_out([k for k in range(S) if k & (k - 1) == 0], True)
    gu.last()
    gu.ready(False, True)
    put(wu, wu_o)
    feed_out([k for k in range(S) if k & (k - 1)], False)
    cot_move.finish()
    smg_o[...] = jnp.zeros(smg_o.shape, f32)

    def second_norm(r):
        rows = tile(r, RB)
        normed, factor = norm_rows(first[rows, :] + n2[rows, :])
        gain = sm_o[SG : SG + 1, :]
        outv[rows, :] = (normed * gain + sm_o[SS : SS + 1, :]).astype(bf16)
        g = ct[rows, :].astype(f32)
        smg_o[SG : SG + 1, :] += colsum(g * normed)
        smg_o[SS : SS + 1, :] += colsum(g)
        back = norm_back(g, gain, normed, factor)
        gsec[rows, :] = back
        low = back.astype(bf16)
        gb[rows, :] = low
        smg_o[UB : UB + 1, :] += colsum(low.astype(f32))

    loop(L // RB, second_norm)
    put(outv, out_o)
    put(gsec, gsec_o)
    put(gb, gb_o)

    for u in range(2):
        keep_probs(NP - 2 + u, 0).wait()
    for gather in gathers:
        gather.drain()
    for move in (hid_move, cot_move, seg_move):
        move.drain()
    for copy in small_copies:
        copy.wait_send()
    for d in range(1, M):
        for copy in kv_copies(d):
            copy.wait_send()
    for copy in own_kv + [seg_own] + pending:
        copy.wait()


def forward_call(S, C, hid, cot, seg, wq_s, wo_s, wi_s, wu_s, vectors):
    G, PP, D = hid.shape
    L, M, NP, FF = G * PP, C // G, D // 128, wi_s.shape[1]
    sds = jax.ShapeDtypeStruct
    outs = [
        ((L, D), bf16), ((D, 3 * D), bf16), ((D, D), bf16), ((D, FF), bf16), ((FF, D), bf16),
        ((M, NP, L, 128), bf16), ((M, NP, L, 128), bf16), ((NP, L, 128), bf16),
        ((M, G, 1, PP), jnp.int32), ((NP, M, 2, L, L), bf16), None, ((NP, 128, L), f32), ((L, D), bf16),
        ((L, D), f32), ((L, 1), f32), ((L, D), bf16), ((L, FF), bf16), ((L, FF), bf16),
        ((L, D), f32), ((L, D), bf16), ((L, D), bf16),
    ]
    scratch = [
        ((L, D), bf16), ((L, D), bf16), ((D, 3 * D), bf16), ((D, D), bf16), ((D, FF), bf16), ((FF, D), bf16),
        ((S, 16, D // S + -(D // S) % 128), bf16), ((G, 1, PP), jnp.int32), ((G, 1, PP), jnp.int32),
        ((NP, L, 128), bf16), ((NP, 128, L), bf16), ((NP, L, 128), bf16), ((NP, L, 128), bf16),
        ((NP, L, 128), bf16), ((NP, L, 128), bf16), ((L, L), f32), ((2, 2, L, L), bf16), ((M, NP, 2, L), f32), ((NP, 2, L), f32),
        ((NP, 128, L), f32), ((L, D), bf16),
        ((L, D), f32), ((L, D), f32), ((L, 1), f32), ((L, D), bf16), ((L, D), f32), ((L, D), f32), ((L, FF), bf16),
        ((L, FF), bf16), ((L, D), f32), ((L, D), f32), ((L, D), bf16), ((L, D), bf16),
    ]
    dma = pltpu.SemaphoreType.DMA
    sems = [
        dma((4, 2, S)), dma((4, 2, S)), dma((4, 2, S)), dma((4, 2, S)), dma((4, 2, S)), dma((4,)), dma((3, G)), dma((3, G)), dma((3,)),
        dma((S,)), dma((S,)), dma((3, M)), dma((3, M)), dma((3,)), dma((3,)), dma((2,)), dma((24,)),
    ]
    return pl.pallas_call(
        functools.partial(forward_kernel, (S, C, G, PP)),
        out_shape=[sds(*(o or ((M, NP, 2, L), f32))) for o in outs] + [sds((16, D), f32), sds((16, D), f32)],
        in_specs=[ANY] * 7 + [VMEM] * len(vectors),
        out_specs=[ANY if o else VMEM for o in outs] + [VMEM, VMEM],
        scratch_shapes=[pltpu.VMEM(*x) for x in scratch] + sems,
        compiler_params=pltpu.CompilerParams(
            collective_id=0, has_side_effects=True, vmem_limit_bytes=62 << 20
        ),
        name="forward",
    )(hid, cot, seg, wq_s, wo_s, wi_s, wu_s, *vectors)


def widen_kernel(count, *refs):
    srcs, dsts = refs[: count + 1], refs[count + 1 : 2 * count + 2]
    lows, highs = refs[2 * count + 2 : 3 * count + 2], refs[3 * count + 2 : 4 * count + 2]
    plain, in_sem, out_sem = refs[4 * count + 2 :]
    loads, stores = [], []
    for i in range(count):
        loads.append(pltpu.make_async_copy(srcs[i], lows[i], in_sem.at[i]))
        stores.append(pltpu.make_async_copy(highs[i], dsts[i], out_sem.at[i]))
    loads.append(pltpu.make_async_copy(srcs[count], plain, in_sem.at[count]))
    stores.append(pltpu.make_async_copy(plain, dsts[count], out_sem.at[count]))
    for copy in loads:
        copy.start()
    for i in range(count):
        loads[i].wait()
        rows = lows[i].shape[0]
        unit = next(u for u in (64, 48, 32, 16) if rows % u == 0)

        def step(r, low=lows[i], high=highs[i], unit=unit):
            at = tile(r, unit)
            high[at, :] = low[at, :].astype(f32)

        loop(rows // unit, step)
        stores[i].start()
    loads[count].wait()
    stores[count].start()
    for copy in stores:
        copy.wait()


def widen(arrays, plain):
    count = len(arrays)
    sds = jax.ShapeDtypeStruct
    return pl.pallas_call(
        functools.partial(widen_kernel, count),
        out_shape=[sds(a.shape, f32) for a in arrays] + [sds(plain.shape, plain.dtype)],
        in_specs=[ANY] * (count + 1),
        out_specs=[ANY] * (count + 1),
        scratch_shapes=[pltpu.VMEM(a.shape, bf16) for a in arrays]
        + [pltpu.VMEM(a.shape, f32) for a in arrays]
        + [pltpu.VMEM(plain.shape, plain.dtype), pltpu.SemaphoreType.DMA((count + 1,)), pltpu.SemaphoreType.DMA((count + 1,))],
        compiler_params=pltpu.CompilerParams(vmem_limit_bytes=62 << 20),
        name="widen",
    )(*arrays, plain)


def add_rows(dst, src):
    rows = dst.shape[0]
    unit = next(u for u in (96, 48, 16) if rows % u == 0)

    def step(r):
        at = tile(r, unit)
        dst[at, :] = dst[at, :] + src[at, :]

    loop(rows // unit, step)


class CoreSwap:
    def __init__(self, part, far, rows, send, recv):
        self.part, self.far, self.rows, self.send, self.recv = part, far, rows, send, recv
        self.c = lax.axis_index("ctx")
        self.core = lax.rem(self.c, 2)
        self.count = part.shape[1] // rows

    def copy(self, i):
        rows = tile(i, self.rows)
        return remote(
            self.part.at[1 - self.core, rows, :], self.far.at[rows, :], self.send.at[i], self.recv.at[i],
            ctx=jnp.bitwise_xor(self.c, 1),
        )

    def start(self, i):
        self.copy(i).start()

    def add(self):
        loop(self.count, lambda i: self.copy(i).wait_recv())
        add_rows(self.part.at[self.core], self.far)

    def drain(self):
        loop(self.count, lambda i: self.copy(i).wait_send())


class Reduce:
    def __init__(self, S, C, part, stride, offset, R, cols, rx, zl, zr, sems, places):
        self.S, self.K, self.part, self.rx, self.zl, self.zr = S, C // 2, part, rx, zl, zr
        self.c_send, self.c_recv, self.x_send, self.x_recv, self.z_send, self.z_recv, self.l_send = sems
        self.places, self.stride, self.offset, self.R, self.cols = places, stride, offset, R, cols
        self.half = R // 2
        self.s, self.c = lax.axis_index("seq"), lax.axis_index("ctx")
        self.core = lax.rem(self.c, 2)
        self.k = lax.div(self.c, 2)
        self.left, self.right = self.K // 2 - 1, self.K // 2
        self.orders = bit_orders(S)
        self.steps = len(self.orders[0])

    def rows(self, owner, start, count):
        return self.part.at[self.core, span(owner * self.stride + self.offset + start, count, 16), self.cols]

    def block(self, owner, p):
        return self.rows(owner, p * self.half, self.half)

    def result(self):
        return self.rows(self.s, 0, self.R)

    def copies(self, t):
        out, base = [], self.S - (1 << (self.steps - t))
        for p in range(2):
            order = self.orders[p]
            peer = jnp.bitwise_xor(self.s, order[t])
            for i, mask in reversed(list(enumerate(subsets(order[t + 1 :])))):
                copy = remote(
                    self.block(jnp.bitwise_xor(peer, mask), p),
                    self.rx.at[p, base + i],
                    self.x_send.at[p, base + i],
                    self.x_recv.at[p, base + i],
                    seq=peer,
                )
                out.append((copy, p, base + i, mask))
        return out

    def cross_start(self, t):
        if t > 0:
            self.cross_add(t - 1, False)
        for copy, _, _, _ in self.copies(t):
            copy.start()

    def cross_add(self, t, last):
        for copy, p, slot, mask in self.copies(t):
            if (mask == 0) == last:
                copy.wait_recv()
                add_rows(self.block(jnp.bitwise_xor(self.s, mask), p), self.rx.at[p, slot])

    def from_left(self):
        return remote(self.result(), self.zl, self.z_send.at[0], self.z_recv.at[0], ctx=self.c + 2)

    def from_right(self):
        return remote(self.result(), self.zr, self.z_send.at[0], self.z_recv.at[1], ctx=self.c - 2)

    def out_left(self):
        return remote(self.zr, self.zr, self.z_send.at[1], self.z_recv.at[1], ctx=self.c - 2)

    def out_right(self):
        return remote(self.zl, self.zl, self.z_send.at[1], self.z_recv.at[0], ctx=self.c + 2)

    def inward(self, level):
        if level == 0:
            for t in range(self.steps):
                self.cross_add(t, True)

        @pl.when(self.k == level)
        def _():
            if level > 0:
                self.from_left().wait_recv()
                add_rows(self.result(), self.zl)
            self.from_left().start()

        @pl.when(self.k == self.K - 1 - level)
        def _():
            if level > 0:
                self.from_right().wait_recv()
                add_rows(self.result(), self.zr)
            self.from_right().start()

    def outward(self, distance):
        @pl.when(self.k == self.left - distance)
        def _():
            self.from_right().wait_recv()
            if distance == 0:
                add_rows(self.zr, self.result())
            if distance < self.left:
                self.out_left().start()
            self.deliver(self.zr)

        @pl.when(self.k == self.right + distance)
        def _():
            self.from_left().wait_recv()
            if distance == 0:
                add_rows(self.zl, self.result())
            if distance < self.left:
                self.out_right().start()
            self.deliver(self.zl)

    def deliveries(self, src):
        out = []
        for i, (cols, place) in enumerate(self.places):
            dst = place(self.core)
            out.append(
                (
                    pltpu.make_async_copy(src.at[:, cols], dst, self.l_send.at[i]),
                    remote(
                        src.at[:, cols], dst, self.c_send.at[i], self.c_recv.at[i], ctx=jnp.bitwise_xor(self.c, 1)
                    ),
                )
            )
        return out

    def deliver(self, src):
        for near, far in self.deliveries(src):
            near.start()
            far.start()

    def finish(self):
        for near, far in self.deliveries(self.zl):
            near.wait()
            far.wait_recv()

    def stages(self):
        def each(step, *which):
            for w in which:
                step(w)

        run = functools.partial
        return [
            run(each, self.cross_start, 0),
            run(each, self.cross_start, *range(1, self.steps)),
            run(each, self.inward, 0),
            run(each, self.inward, *range(1, self.left + 1)),
            run(each, self.outward, 0),
            run(each, self.outward, *range(1, self.left + 1)),
        ]

    def drain(self):
        for t in range(self.steps):
            for copy, _, _, _ in self.copies(t):
                copy.wait_send()

        @pl.when(self.k <= self.left)
        def _():
            self.from_left().wait_send()

        @pl.when(self.k >= self.right)
        def _():
            self.from_right().wait_send()

        @pl.when(jnp.logical_and(self.k <= self.left, self.k > 0))
        def _():
            self.out_left().wait_send()

        @pl.when(jnp.logical_and(self.k >= self.right, self.k < self.K - 1))
        def _():
            self.out_right().wait_send()

        for _, far in self.deliveries(self.zl):
            far.wait_send()


class DirectReduce:
    def __init__(self, S, C, part, far, rx, zx, done, sems, places):
        self.S, self.K, self.part, self.far, self.rx, self.zx, self.done = S, C // 2, part, far, rx, zx, done
        self.h_send, self.h_recv, self.x_send, self.x_recv, self.z_send, self.z_recv, self.c_send, self.c_recv, self.l_send = sems
        self.places = places
        self.s, self.c = lax.axis_index("seq"), lax.axis_index("ctx")
        self.core = lax.rem(self.c, 2)
        self.k = lax.div(self.c, 2)

    def other(self):
        return jnp.bitwise_xor(self.c, 1)

    def halves(self):
        return remote(
            self.part.at[:, 1 - self.core], self.far, self.h_send.at[0], self.h_recv.at[0], ctx=self.other()
        )

    def start(self):
        self.halves().start()

    def crossing(self):
        out = []
        for d in range(self.S - 1, 0, -1):
            peer = jnp.bitwise_xor(self.s, d)
            out.append(
                remote(
                    self.part.at[peer, self.core], self.rx.at[d - 1], self.x_send.at[d - 1], self.x_recv.at[d - 1],
                    seq=peer,
                )
            )
        return out

    def cross_start(self):
        self.halves().wait_recv()
        for owner in range(self.S):
            add_rows(self.part.at[owner, self.core], self.far.at[owner])
        for copy in self.crossing():
            copy.start()

    def along(self, d):
        chip = lax.rem(self.k + d, self.K)
        return remote(
            self.part.at[self.s, self.core], self.zx.at[self.k], self.z_send.at[d - 1], self.z_recv.at[self.k],
            ctx=2 * chip + self.core,
        )

    def arrival(self, d):
        chip = lax.rem(self.k + d, self.K)
        return remote(
            self.part.at[self.s, self.core], self.zx.at[chip], self.z_send.at[d - 1], self.z_recv.at[chip],
            ctx=2 * chip + self.core,
        )

    def along_start(self):
        mine = self.part.at[self.s, self.core]
        for copy in self.crossing():
            copy.wait_recv()
        total = mine[...].astype(f32)
        for d in range(1, self.S):
            total = total + self.rx[d - 1].astype(f32)
        total = total.astype(bf16)
        mine[...] = total
        self.zx[self.k] = total
        for d in range(self.K - 1, 0, -1):
            self.along(d).start()

    def outputs(self):
        out = []
        for i, (cols, place) in enumerate(self.places):
            dst = place(self.core)
            src = self.done.at[:, cols]
            out.append(
                (
                    pltpu.make_async_copy(src, dst, self.l_send.at[i]),
                    remote(src, dst, self.c_send.at[i], self.c_recv.at[i], ctx=self.other()),
                )
            )
        return out

    def deliver(self):
        for d in range(1, self.K):
            self.arrival(d).wait_recv()
        total = self.zx[0].astype(f32)
        for j in range(1, self.K):
            total = total + self.zx[j].astype(f32)
        self.done[...] = total.astype(bf16)
        for near, far in self.outputs():
            near.start()
            far.start()

    def stages(self):
        return [self.cross_start, self.along_start, self.deliver]

    def finish(self):
        for near, far in self.outputs():
            near.wait()
            far.wait_recv()

    def drain(self):
        self.halves().wait_send()
        for copy in self.crossing():
            copy.wait_send()
        for d in range(1, self.K):
            self.along(d).wait_send()
        for _, far in self.outputs():
            far.wait_send()


SCHEDULE = {
    "outer": (('u0', 1),),
    "ffn0": (('u1', 1),),
    "ffn1": (('u0', 2), ('u2', 1)),
    "ffn2": (('u1', 2),),
    "ffn3": (('i0', 1),),
    "first": (('u0', 3), ('u2', 2)),
    "context": (('u1', 3), ('i1', 1)),
    "far0": (('u0', 4), ('i0', 2)),
    "pair0": (('i2', 1),),
    "far1": (('u2', 3), ('i1', 2), ('i3', 1)),
    "pair1": (('u1', 4),),
    "project0": (('u0', 5), ('i0', 3)),
    "input0": (('i2', 2),),
    "far2": (('o', 1),),
    "pair2": (('u2', 4), ('i1', 3)),
    "far3": (('u0', 6), ('u1', 5), ('i0', 4), ('i3', 2)),
    "pair3": (('i2', 3),),
    "project1": (('o', 2),),
    "input1": (('u2', 5), ('i1', 4), ('q0', 1)),
    "far4": (('i3', 3), ('u1', 6), ('q1', 1)),
    "pair4": (('i0', 5), ('i2', 4), ('o', 3)),
    "far5": (('q0', 2),),
    "pair5": (('u2', 6), ('i1', 5), ('i3', 4), ('q1', 2)),
    "input2": (('i0', 6), ('i2', 5), ('o', 4), ('q0', 3), ('q2', 1), ('q3', 1), ('q4', 1)),
    "end": (('q1', 3), ('s', 1), ('i1', 6), ('i3', 5), ('g0', 1), ('q2', 2), ('q3', 2), ('q4', 2), ('i2', 6), ('o', 5), ('q0', 4), ('s', 2), ('q2', 3), ('q3', 3), ('q4', 3), ('i3', 6), ('q1', 4), ('q0', 5), ('q2', 4), ('q3', 4), ('o', 6), ('s', 3), ('q4', 4), ('q1', 5), ('g1', 1), ('q2', 5), ('q3', 5), ('q0', 6), ('q4', 5), ('g2', 1), ('q1', 6), ('g3', 1), ('q2', 6), ('q3', 6), ('q4', 6)),
}


def backward_kernel(
    dims,
    outv, gsec_i, gb_i, act_i, dgel_i, wu_i, wi_i, wo_i, wq_i, flow_i, n1_i, f1_i, xs_i, ctx_i, ctxt_i,
    q_i, k_i, v_i, p_i, fac, smg_i, sm,
    out_o, gin_o, gq_o, go_o, gi_o, gu_o, land_o, small_o,
    pu, pi, po, pq, ps, fu, fi, fo, fq, fs, rxu, rxi, rxq, rxs, zlu, zli, zlq, zru, zri, zrq, zxs, dns,
    gsec, gb, grad_o, grad_ot, delta, smg,
    cs_send, cs_recv, h_send, h_recv, dx_send, dx_recv, dz_send, dz_recv, c_send, c_recv, x_send, x_recv, z_send, z_recv, rg_send, rg_recv, rg_local, in_sem, wq_sem, kv_sem, p_sem, dkv_send, dkv_recv,
    land_sem, l_send,
):
    S, C, G, PP = dims
    M, L, D = C // G, G * PP, gsec.shape[1]
    FF = act_i.shape[1]
    NP = D // 128
    T = 256
    s, c = lax.axis_index("seq"), lax.axis_index("ctx")
    m, core = lax.rem(c, M), lax.rem(c, 2)
    group = lax.div(c, M) * M

    H = D // 2
    R, RU = D // S, FF // S
    cut = RU // 3
    items = {}

    def piece(name, places, *refs):
        n = len(items)
        sems = [a.at[n] for a in (c_send, c_recv, x_send, x_recv, z_send, z_recv, l_send)]
        items[name] = Reduce(S, C, *refs, sems, places)

    for i in range(3):
        piece(
            f"u{i}", [(pl.ds(0, H), lambda e, i=i: gu_o.at[pl.ds(i * cut, cut), span(e * H, H)])],
            pu.at[i], cut, 0, cut, pl.ds(0, H), rxu.at[i], zlu.at[i], zru.at[i],
        )

    def narrow_piece(name, places, part, cols):
        n = len(items) - 3
        piece(name, places, part, R, 0, R, cols, rxi.at[n], zli.at[n], zri.at[n])

    for i in range(2):
        for j in range(2):
            narrow_piece(
                f"i{2 * i + j}",
                [(pl.ds(0, H), lambda e, i=i, j=j: gi_o.at[:, span(e * (FF // 2) + i * D + j * H, H)])],
                pi.at[i], pl.ds(j * H, H),
            )
    narrow_piece("o", [(pl.ds(0, H), lambda e: go_o.at[:, span(e * H, H)])], po, pl.ds(0, H))

    def qkv_place(i, a):
        return lambda e: gq_o.at[:, span(a * D + (2 * i + e) * 128, 128)]

    for i in range(2):
        narrow_piece(
            f"q{i}", [(pl.ds(a * 128, 128), qkv_place(i, a)) for a in range(3)], pq.at[i], pl.ds(0, H)
        )
    for a in range(3):
        piece(
            f"q{2 + a}", [(pl.ds(0, 128), qkv_place(2, a))],
            pq.at[2], R, 0, R, pl.ds(a * 128, 128), rxq.at[a], zlq.at[a], zrq.at[a],
        )
    def direct_piece(name, n, places, *refs):
        m_ = len(items)
        sems = [a.at[n] for a in (h_send, h_recv, dx_send, dx_recv, dz_send, dz_recv)]
        items[name] = DirectReduce(S, C, *refs, sems + [a.at[m_] for a in (c_send, c_recv, l_send)], places)

    SW = ps.shape[3]
    direct_piece("s", 0, [(pl.ds(0, SW), lambda e: small_o.at[e])], ps, fs, rxs, zxs, dns)
    swap_u = [CoreSwap(pu.at[i], fu.at[i], cut, cs_send.at[7 + i], cs_recv.at[7 + i]) for i in range(3)]
    swap_i = [CoreSwap(pi.at[i], fi.at[i], T, cs_send.at[1 + i], cs_recv.at[1 + i]) for i in range(2)]
    swap_o = CoreSwap(po, fo, T, cs_send.at[3], cs_recv.at[3])
    swap_q = [CoreSwap(pq.at[i], fq.at[i], T, cs_send.at[4 + i], cs_recv.at[4 + i]) for i in range(3)]

    ticks = {name: item.stages() for name, item in items.items()}
    ran = set()

    def point(name):
        for step in SCHEDULE.get(name, ()):
            ran.add(step)
            ticks[step[0]][step[1] - 1]()

    met = enter(S, C)
    out_move = Ungroup(outv, out_o, rg_send.at[0], rg_recv.at[0], rg_local.at[0], C, G)
    smg[...] = smg_i[...]

    def feed_forward(act, dgel, wu, wi, h, n1, f1, flow):
        loads = [
            pltpu.make_async_copy(src, dst, in_sem.at[i])
            for i, (src, dst) in enumerate(
                ((gb_i, gb), (act_i, act), (wu_i, wu), (dgel_i, dgel), (flow_i, flow), (wi_i, wi), (gsec_i, gsec),
                 (n1_i, n1), (f1_i, f1))
            )
        ]
        for copy in loads:
            copy.start()
        loads[0].wait()
        loads[1].wait()

        met()
        out_move.start()
        for i in range(3):

            def outer_grad(owner, i=i):
                block = dotg(act[:, span(owner * RU + i * cut, cut)], gb[...], 0, 0).astype(bf16)
                for e in range(2):
                    pu[i, e, tile(owner, cut), :] = block[:, e * H : (e + 1) * H]
                swap_u[i].start(owner)

            loop(S, outer_grad)
        swap_u[0].add()
        point("outer")
        for copy in loads[2:5]:
            copy.wait()

        def inner_grad(i, half, send):
            where = half * (FF // 2) + i * D
            cols = span(where, D)
            h[...] = dotg(gb[...], wu[span(where, D), :], 1, 1)

            def through(k, sums):
                rows = tile(k, RB)
                low = (h[rows, :] * dgel[rows, cols].astype(f32)).astype(bf16)
                act[rows, cols] = low
                return sums + colsum(low.astype(f32))

            sums = lax.fori_loop(0, L // RB, through, jnp.zeros((1, D), f32))
            smg[pl.ds(IB + half * (FF // 2 // D) + i, 1), :] = sums

            def grad(k):
                rows = tile(k, T)
                pi[i, half, rows, :] = dotg(flow[:, rows], act[:, cols], 0, 0).astype(bf16)
                if send:
                    swap_i[i].start(k)

            loop(D // T, grad)

        inner_grad(0, 1 - core, True)
        swap_u[1].add()
        swap_u[2].add()
        point("ffn0")
        inner_grad(0, core, False)
        point("ffn1")
        inner_grad(1, 1 - core, True)
        swap_i[0].add()
        point("ffn2")
        inner_grad(1, core, False)
        swap_i[1].add()
        point("ffn3")
        loads[5].wait()
        loads[6].wait()

        def first_grad(i):
            cols = tile(i, T)
            gsec[:, cols] += dotg(act[...], wi[cols, :], 1, 1)

        loop(D // T, first_grad)
        point("first")
        loads[7].wait()
        loads[8].wait()

        def first_back(k):
            rows = tile(k, RB)
            g, normed = gsec[rows, :], n1[rows, :]
            smg[FG : FG + 1, :] += colsum(g * normed)
            smg[FS : FS + 1, :] += colsum(g)
            back = norm_back(g, sm[FG : FG + 1, :], normed, f1[rows, :])
            gsec[rows, :] = back
            low = back.astype(bf16)
            gb[rows, :] = low
            smg[OB : OB + 1, :] += colsum(low.astype(f32))

        loop(L // RB, first_back)

    V = pltpu.VMEM
    pl.run_scoped(
        feed_forward, V((L, FF), bf16), V((L, FF), bf16), V((FF, D), bf16), V((D, FF), bf16), V((L, D), f32),
        V((L, D), f32), V((L, 1), f32), V((L, D), bf16),
    )
    point("norm")

    def context_back(wo, ctx, ctxt):
        loads = [
            pltpu.make_async_copy(src, dst, in_sem.at[i])
            for i, (src, dst) in enumerate(((ctx_i, ctx), (wo_i, wo), (ctxt_i, ctxt)))
        ]
        for copy in loads:
            copy.start()
        loads[0].wait()

        def out_grad(k):
            rows = tile(k, T)
            block = dotg(ctx[:, rows], gb[...], 0, 0).astype(bf16)
            for e in range(2):
                po[e, rows, :] = block[:, e * (D // 2) : (e + 1) * (D // 2)]
            swap_o.start(k)

        loop(D // T, out_grad)
        loads[1].wait()
        loads[2].wait()

        def back(k):
            grad = dotg(gb[...], wo[tile(k, T), :], 1, 1).astype(bf16)
            for u in range(T // 128):
                hp = k * (T // 128) + u
                mine = grad[:, u * 128 : (u + 1) * 128]
                turned = mine.T
                grad_o[hp] = mine
                grad_ot[hp] = turned
                both = turned.astype(f32) * ctxt[hp]
                for e in range(2):
                    delta[hp, e : e + 1, :] = colsum(both[e * HEAD_DIM : (e + 1) * HEAD_DIM])

        loop(D // T, back)

    pl.run_scoped(context_back, V((D, D), bf16), V((L, D), bf16), V((NP, 128, L), f32))
    swap_o.add()
    point("context")

    def attention(wq, xs, q, kb, vb, pb, own_k, own_v, stage, land, grads, dqt, turned_q):
        loads = [
            pltpu.make_async_copy(src, dst, in_sem.at[i])
            for i, (src, dst) in enumerate(
                ((q_i, q), (xs_i, xs))
            )
        ]
        groups = [(0, 2), (2, 2), (4, 2)]

        def weight_cols(first, count):
            return [
                pltpu.make_async_copy(
                    wq_i.at[:, pl.ds(a * D + first * 128, count * 128)],
                    wq.at[:, pl.ds(3 * first * 128 + a * count * 128, count * 128)],
                    wq_sem.at[first, a],
                )
                for a in range(3)
            ]

        def kv_load(hp):
            slot = lax.rem(hp, 2)
            return [
                pltpu.make_async_copy(src.at[:, hp], dst.at[slot], kv_sem.at[i, slot])
                for i, (src, dst) in enumerate(((k_i, kb), (v_i, vb)))
            ]

        def p_load(t):
            d = lax.rem(lax.rem(t, M) + 1, M)
            return pltpu.make_async_copy(p_i.at[lax.div(t, M), d], pb.at[lax.rem(t, 2)], p_sem.at[lax.rem(t, 2)])

        for copy in kv_load(0) + [p_load(0)] + loads:
            copy.start()
        for first, count in groups:
            for copy in weight_cols(first, count):
                copy.start()
        loads[0].wait()
        row_of = lax.broadcasted_iota(jnp.int32, (128, L), 0)
        lane_of = lax.broadcasted_iota(jnp.int32, (L, 128), 1)

        def send_back(hp, d):
            slot = lax.rem(hp, 2)
            return remote(
                stage.at[slot, d - 1], land_o.at[hp, d - 1], dkv_send.at[slot, d - 1], dkv_recv.at[hp, d - 1],
                ctx=group + lax.rem(m + d, M),
            )

        def chunk(hp, slot, d, put):
            j = lax.rem(m + d, M)
            t = hp * M + lax.rem(d - 1 + M, M)
            p_load(t).wait()

            @pl.when(t + 1 < NP * M)
            def _():
                p_load(t + 1).start()

            def block(ks, qs, kn, qn):
                key, value = kb[slot, j, ks, :], vb[slot, j, ks, :]
                turned = key.T
                query, up, up_t = q[hp, qs, :], grad_o[hp, qs, :], grad_ot[hp, :, qs]
                row_of = lax.broadcasted_iota(jnp.int32, (128, qn), 0)
                lane_of = lax.broadcasted_iota(jnp.int32, (qn, 128), 1)
                sums = []
                for e in range(2):
                    rows = (row_of < HEAD_DIM) if e == 0 else (row_of >= HEAD_DIM)
                    lanes = (lane_of < HEAD_DIM) if e == 0 else (lane_of >= HEAD_DIM)
                    zero, zero_t = jnp.zeros_like(query), jnp.zeros_like(up_t)
                    probs = pb[lax.rem(t, 2), e, ks, qs].astype(f32) * fac[d, hp, e : e + 1, qs]
                    dprobs = dotf(value, jnp.where(rows, up_t, zero_t))
                    dscores = (probs * (dprobs - delta[hp, e : e + 1, qs])).astype(bf16)
                    sums.append(
                        (
                            dotf(dscores, jnp.where(lanes, query, zero)),
                            dotf(probs.astype(bf16), jnp.where(lanes, up, zero)),
                        )
                    )
                    head = slice(e * HEAD_DIM, (e + 1) * HEAD_DIM)
                    dqt[head, qs] += dotf(turned[head], dscores)
                put(ks, sums[0][0] + sums[1][0], sums[0][1] + sums[1][1])

            if M == 2 and not isinstance(d, int):
                near, far = span(m * (L // 2), L // 2), span((1 - m) * (L // 2), L // 2)
                block(near, pl.ds(0, L), L // 2, L)
                block(far, far, L // 2, L // 2)
            else:
                block(pl.ds(0, L), pl.ds(0, L), L, L)

        def pair(hp, between):
            slot = lax.rem(hp, 2)
            for copy in kv_load(hp):
                copy.wait()

            @pl.when(hp + 1 < NP)
            def _():
                for copy in kv_load(hp + 1):
                    copy.start()

            dqt[...] = jnp.zeros(dqt.shape, f32)

            def far(d, carry):
                @pl.when(hp >= 2)
                def _():
                    send_back(hp - 2, d).wait_send()

                def put(ks, dk, dv):
                    stage[slot, d - 1, 0, ks, :] = dk.astype(bf16)
                    stage[slot, d - 1, 1, ks, :] = dv.astype(bf16)

                chunk(hp, slot, d, put)
                send_back(hp, d).start()
                return carry

            lax.fori_loop(1, M, far, 0)
            between()

            def put_own(ks, dk, dv):
                own_k[slot, ks, :] = dk
                own_v[slot, ks, :] = dv

            chunk(hp, slot, 0, put_own)
            turned_q[slot] = (dqt[...] * HEAD_DIM**-0.5).T.astype(bf16)

        def fetched(first, count):
            return pltpu.make_async_copy(land_o.at[pl.ds(first, count)], land.at[pl.ds(0, count)], land_sem.at[0])

        def fetch(first, count):
            for u in range(count):
                for d in range(1, M):
                    send_back(first + u, d).wait_recv()
            if M > 1:
                fetched(first, count).start()

        def project_back(first, count):
            if M > 1:
                fetched(first, count).wait()
            W = count * 128
            for u in range(count):
                slot = (first + u) % 2
                dk, dv = own_k[slot], own_v[slot]
                for d in range(1, M):
                    dk = dk + land[u, d - 1, 0].astype(f32)
                    dv = dv + land[u, d - 1, 1].astype(f32)
                grads[:, u * 128 : (u + 1) * 128] = turned_q[slot]
                grads[:, W + u * 128 : W + (u + 1) * 128] = dk.astype(bf16)
                grads[:, 2 * W + u * 128 : 2 * W + (u + 1) * 128] = dv.astype(bf16)
            cols = slice(first * 128, first * 128 + W)
            smg[QB : QB + 1, cols] = colsum(grads[:, 0:W].astype(f32))
            smg[VB : VB + 1, cols] = colsum(grads[:, 2 * W : 3 * W].astype(f32))

            def weight(k):
                rows = tile(k, T)
                block = dotg(xs[:, rows], grads[...], 0, 0).astype(bf16)
                for a in range(3):
                    for e in range(2):
                        pq[first // 2, e, rows, a * 128 : (a + 1) * 128] = block[
                            :, a * W + e * 128 : a * W + (e + 1) * 128
                        ]
                swap_q[first // 2].start(k)

            loop(D // T, weight)

        def input_back(first, count):
            for copy in weight_cols(first, count):
                copy.wait()
            W = 3 * count * 128
            base = 3 * first * 128

            def back(k):
                rows = tile(k, T)
                gsec[:, rows] += dotg(grads[:, 0:W], wq[rows, base : base + W], 1, 1)

            loop(D // T, back)

        def drain_stage():
            for hp in (NP - 2, NP - 1):
                for d in range(1, M):
                    send_back(hp, d).wait_send()

        def pair_group(first, count):
            def body(u):
                def here(name):
                    for k in range(count):

                        @pl.when(u == k)
                        def _():
                            point(f"{name}{first + k}")

                pair(first + u, lambda: here("far"))
                here("pair")

            loop(count, body)

        for g, (first, count) in enumerate(groups[:2]):
            pair_group(first, count)
            fetch(first, count)
            if g == 0:
                loads[1].wait()
            project_back(first, count)
            point(f"project{g}")
            input_back(first, count)
            swap_q[g].add()
            point(f"input{g}")
        pair_group(*groups[2])
        fetch(*groups[2])
        project_back(*groups[2])

        width = D // S
        ps[...] = jnp.zeros(ps.shape, bf16)
        share = FF // S
        for owner in range(S):
            ps[owner, 0, 0:8, 0:width] = smg[0:8, owner * width : (owner + 1) * width].astype(bf16)
            for r in range(share // width):
                start = owner * share + r * width
                a, b = start // D, start % D
                ps[owner, 1, r : r + 1, 0:width] = smg[IB + a : IB + a + 1, b : b + width].astype(bf16)
        items["s"].start()
        point("project2")
        input_back(*groups[2])
        for r in range(L // PP):
            rows = pl.ds(r * PP, PP)
            grads[rows, :] = gsec[rows, :].astype(bf16)
        swap_q[2].add()
        gin_move = Ungroup(grads, gin_o, rg_send.at[1], rg_recv.at[1], rg_local.at[1], C, G)
        for j in range(G):
            ticks[f"g{j}"] = [functools.partial(gin_move.start, j)]
        point("input2")
        point("end")
        assert ran == {(name, i + 1) for name in ticks for i in range(len(ticks[name]))}
        gin_move.finish()
        gin_move.drain()
        drain_stage()

    pl.run_scoped(
        attention, V((D, 3 * D), bf16), V((L, D), bf16), V((NP, L, 128), bf16),
        V((2, M, L, 128), bf16), V((2, M, L, 128), bf16), V((2, 2, L, L), bf16),
        V((2, L, 128), f32), V((2, L, 128), f32), V((2, max(M - 1, 1), 2, L, 128), bf16),
        V((2, max(M - 1, 1), 2, L, 128), bf16), V((L, 3 * T), bf16), V((128, L), f32),
        V((2, L, 128), bf16),
    )
    out_move.finish()
    out_move.drain()
    for item in items.values():
        item.finish()
        item.drain()
    for swap in swap_u + swap_i + [swap_o] + swap_q:
        swap.drain()


def backward_call(S, C, G, PP, saved):
    (xs, wq, wo, wi, wu, k, v, q, _, p, fac, ctxt, ctx, n1, f1, flow, act, dgel, gsec, gb, outv, smg, sm) = saved
    L, D = xs.shape
    M, NP, FF = C // G, D // 128, wi.shape[1]
    R, RU = D // S, FF // S
    sds = jax.ShapeDtypeStruct
    land = max(M - 1, 1)
    H, SR, SW = D // 2, 32, 256
    outs = [
        ((G, PP, D), bf16), ((G, PP, D), bf16), ((R, 3 * D), bf16), ((R, D), bf16), ((R, FF), bf16), ((RU, D), bf16),
        ((NP, land, 2, L, 128), bf16), ((2, SR // 2, SW), bf16),
    ]
    cut = RU // 3
    scratch = [
        (3, 2, S * cut, H), (2, 2, D, D), (2, D, H), (3, 2, D, H), (S, 2, SR // 2, SW),
        (3, S * cut, H), (2, D, D), (D, H), (3, D, H), (S, SR // 2, SW),
        (3, 2, S - 1, cut // 2, H), (7, 2, S - 1, R // 2, H), (3, 2, S - 1, R // 2, 128), (S - 1, SR // 2, SW),
        (3, cut, H), (7, R, H), (3, R, 128), (3, cut, H), (7, R, H), (3, R, 128),
        (C // 2, SR // 2, SW), (SR // 2, SW),
    ]
    scratch = [(x, bf16) for x in scratch] + [
        ((L, D), f32), ((L, D), bf16), ((NP, L, 128), bf16), ((NP, 128, L), bf16), ((NP, 2, L), f32), ((16, D), f32),
    ]
    dma = pltpu.SemaphoreType.DMA
    sems = [
        dma((10, 8)), dma((10, 8)), dma((1, 1)), dma((1, 1)), dma((1, S - 1)), dma((1, S - 1)), dma((1, C // 2)), dma((1, C // 2)),
        dma((16, 3)), dma((16, 3)), dma((16, 2, S - 1)), dma((16, 2, S - 1)), dma((16, 2)),
        dma((16, 2)),
        dma((2, G)), dma((2, G)), dma((2,)), dma((10,)), dma((NP, 3)), dma((2, 2)), dma((2,)), dma((2, land)), dma((NP, land)), dma((1,)),
        dma((16, 3)),
    ]
    results = pl.pallas_call(
        functools.partial(backward_kernel, (S, C, G, PP)),
        out_shape=[sds(*o) for o in outs],
        in_specs=[ANY] * 19 + [VMEM] * 3,
        out_specs=[ANY] * len(outs),
        scratch_shapes=[pltpu.VMEM(*x) for x in scratch] + sems,
        compiler_params=pltpu.CompilerParams(
            collective_id=1, has_side_effects=True, vmem_limit_bytes=62 << 20
        ),
        name="backward",
    )(outv, gsec, gb, act, dgel, wu, wi, wo, wq, flow, n1, f1, xs, ctx, ctxt, q, k, v, p, fac, smg, sm)
    return results


def solution(mesh):
    S, C = mesh.shape["seq"], mesh.shape["ctx"]

    def on_device(
        hid, cot, seg, wq, qb, vb, wo, ob, fg, fs, wi, ib, wu, ub, sg, ss
    ):
        G, PP, D = hid.shape
        saved = forward_call(S, C, hid, cot, seg.reshape(G, 1, PP), wq, wo, wi, wu, [qb, vb, ob, fg, fs, ub, sg, ss, ib])
        out, gin, gq, go, gi, gu, _, gs = backward_call(S, C, G, PP, saved)
        gu, gi, gq, go, gin, out = widen([gu, gi, gq, go, gin.reshape(G * PP, D)], out.reshape(G * PP, D))
        gs = gs.reshape(-1, gs.shape[-1]).astype(f32)
        width = D // S
        row = lambda r: gs[r, :width]
        grad_ib = gs[16 : 16 + ib.shape[0] // width, :width].reshape(-1)
        return (
            out.reshape(G, PP, D), gin.reshape(G, PP, D), gq, row(QB), row(VB), go, row(OB), row(FG), row(FS), gi,
            grad_ib, gu, row(UB), row(SG), row(SS),
        )

    rows, matrix, vector = P("seq", "ctx", None), P("seq", None), P("seq")
    return jax.shard_map(
        on_device,
        mesh=mesh,
        in_specs=(
            rows, rows, P("seq", "ctx"), matrix, vector, vector, matrix, vector, vector, vector, matrix, vector,
            matrix, vector, vector, vector,
        ),
        out_specs=(
            rows, rows, matrix, vector, vector, matrix, vector, vector, vector, matrix, vector, matrix, vector,
            vector, vector,
        ),
        check_vma=False,
    )
```
